32 devices in a mesh: groups: 2 (over y), ctx: 4 (over z), fsdp: 2 (over x), head: 2 (over core).
Axes of the slice: x: 2, y: 2, z: 4, core: 2. Of those that a mesh axis runs over, the one named last changes fastest.
Arguments:
- hidden_in: bfloat16 [4, 512, 8192], P(('groups', 'fsdp'), 'ctx', 'head'), parts along dimension 0, may hold values from -8 to 8
- w_bc: bfloat16 [8192, 256], P('fsdp'), may hold values from -0.0625 to 0.0625
- x_in: bfloat16 [4, 512, 4096], P(('groups', 'fsdp'), 'ctx', 'head'), parts along dimension 0, may hold values from -6 to 6
- dt_raw: float32 [4, 512, 64], P(('groups', 'fsdp'), 'ctx', 'head'), parts along dimension 0, may hold values from -2 to 5
- decay_rate: float32 [64], P('head'), may hold values from 0.001171875 to 0.033
- conv_x: float32 [4, 4096], P(None, 'head'), may hold values from -3 to 3
- conv_bc: float32 [4, 256], replicated, may hold values from -3 to 3
- skip_gain: float32 [64], P('head'), may hold values from -10 to 10
- span_len: int32 [4, 4], P(('groups', 'fsdp')), parts along dimension 0, may hold values from 1 to 256, 512 in all within a row
- grad_y: bfloat16 [4, 512, 4096], P(('groups', 'fsdp'), 'ctx', 'head'), parts along dimension 0, may hold values from -6 to 6
Outputs:
- grad_x: bfloat16 [4, 512, 4096], P(('groups', 'fsdp'), 'ctx', 'head'), parts along dimension 0
- grad_u: bfloat16 [4, 512, 8192], P(('groups', 'fsdp'), 'ctx', 'head'), parts along dimension 0
- grad_dt: float32 [4, 512, 64], P(('groups', 'fsdp'), 'ctx', 'head'), parts along dimension 0
- grad_w: float32 [4, 4096, 256], P(('groups', 'head'), ('ctx', 'fsdp')), parts along dimension 0
The draws below stay inside these ranges and needn't reach their ends.
There are 2 independent parts, one for each index of `groups`. The reference program is written for one: setup_inputs(seed, part) draws one part's arguments, and reference() takes and returns one part's arrays. A program takes and returns all parts, laid end to end along the dimension named above; an argument that names none is the same for every part. Nothing has to cross between parts.
Inputs may be any that keep to these rules, and one draw needn't show every extreme that they name: `span_len`: each list's spans lie end to end over its 512 tokens; each has 1 to 256 tokens and some span has exactly 256.
All inputs are finite; a program needn't handle non-finite values.
Results may differ from the reference program's by a relative error of at most 0.0057.
Values may be sent and summed in bfloat16 or wider, within the bound.
A program may use at most 128 MiB of HBM per device.

```python
import math
import jax
import jax.numpy as jnp
import numpy as np
from jax import lax

D = 8192
HEADS = 64
HEAD_DIM = 64
STATE = 128
TOK_DEV = 128
INNER = 4096
TOKENS_PER_GROUP = 512
GROUP_COUNT = 2
SPANS = 4
MOST = 256
N_HEAD = 2


def draw_dt_raw(key, part):
    seed_generator, surge_seed_generator = jax.random.split(key)
    ambient_entries = jnp.clip(0.6 * jax.random.normal(seed_generator, (GROUP_COUNT, TOKENS_PER_GROUP, HEADS), jnp.float32) - 0.3, -2.0, 1.0)
    surge_indices = jax.random.randint(surge_seed_generator, (GROUP_COUNT, 8), 0, TOKENS_PER_GROUP)
    surge_amplitudes = jnp.any(jnp.arange(TOKENS_PER_GROUP)[None, :, None] == surge_indices[:, None, :], axis=-1)
    return jnp.where(surge_amplitudes[:, :, None], ambient_entries + 4.0, ambient_entries)


def draw_skip_gain(key, part):
    sign_key, size_key = jax.random.split(jax.random.fold_in(key, 17))
    sign_values = jnp.where(jax.random.bernoulli(sign_key, 0.5, (HEADS,)), 1.0, -1.0).astype(jnp.float32)
    magnitude = jnp.exp(jax.random.uniform(size_key, (HEADS,), jnp.float32, math.log(0.25), math.log(10.0)))
    return sign_values * magnitude


def strengthened(entries, own_key, source, target, parts, factor):
    def block_of(dim):
        return (jnp.arange(entries.shape[dim]) // (entries.shape[dim] // parts)).reshape((-1,) + (1,) * (entries.ndim - 1 - dim))

    near = jax.random.permutation(own_key, parts)[block_of(target)]
    second = (block_of(target) + parts // 2) % parts
    return jnp.where((block_of(source) == near) | (block_of(source) == second), factor * entries, entries)


def steps_of(own_key, extent, cuts, low, high):
    level, own = 1.0, jax.random.fold_in(own_key, 6)
    for dim, parts in cuts:
        steps = jnp.exp(jax.random.uniform(jax.random.fold_in(own, dim), (parts,), jnp.float32, low / len(cuts), high / len(cuts)))
        level = level * jnp.repeat(steps, extent[dim] // parts).reshape([-1 if axis == dim else 1 for axis in range(len(extent))])
    return level


def profile(count, total, limit, slope):
    loads = [(1 << 20) // math.isqrt(rank ** slope) + 1 for rank in range(2, count + 1)]
    rest, given = total - limit - (count - 1), [1] * (count - 1)
    while rest > 0:
        free = [i for i in range(count - 1) if given[i] < limit]
        pool, remaining = sum([loads[i] for i in free]), rest
        for i in free:
            more = min(limit - given[i], max(1, remaining * loads[i] // pool), rest)
            given[i] = given[i] + more
            rest = rest - more
    return np.array([limit] + given)


def ragged(own_key, amount, total, most, lean):
    if amount == 2:
        one = jax.random.randint(own_key, (), max(1, total - most), min(most, total - 1) + 1)
        return jnp.stack([one, total - one])
    sizes = jnp.asarray(profile(amount, total, most, lean), jnp.int32)
    couples = (amount - 1) // 2
    source_of, sink = sizes[1:1 + 2 * couples:2], sizes[2:2 + 2 * couples:2]
    margin = jnp.minimum(source_of - 1, most - sink)
    passed = jax.random.randint(jax.random.fold_in(own_key, 1), (couples,), 0, 1 << 20) % (margin + 1)
    sizes = sizes.at[1:1 + 2 * couples:2].set(source_of - passed).at[2:2 + 2 * couples:2].set(sink + passed)
    return sizes[jax.random.permutation(jax.random.fold_in(own_key, 2), amount)]


def noise(stream_key, extent, spread, reach, shards=(), dtype=jnp.bfloat16):
    values = spread * jax.random.normal(stream_key, extent, jnp.float32)
    if shards:
        values = values * steps_of(stream_key, extent, shards, -0.22, 0.18)
    return jnp.clip(values, -reach, reach).astype(dtype)


def heavy_noise(key, shape, scale, limit, cuts, heavy, kind=jnp.bfloat16):
    entries = scale * jax.random.normal(key, shape, jnp.float32)
    if cuts:
        entries = entries * steps_of(key, shape, cuts, -0.22, 0.18)
    return jnp.clip(strengthened(entries, jax.random.fold_in(key, 3), *heavy), -limit, limit).astype(kind)


def setup_inputs(seed: int = 0, part: int = 0) -> dict:
    keys = jax.random.split(jax.random.key(seed), 11)
    own_keys = jax.random.split(jax.random.fold_in(keys[10], part), 11)
    return {
        "hidden_in": heavy_noise(own_keys[0], (GROUP_COUNT, TOKENS_PER_GROUP, D), 1.0, 8.0, ((0, 2), (1, 4), (2, 2)), (1, 2, 4, 2.0)),
        "w_bc": noise(keys[1], (D, 2 * STATE), D ** -0.5, 0.0625, ((0, 2),)),
        "x_in": noise(own_keys[2], (GROUP_COUNT, TOKENS_PER_GROUP, INNER), 1.0, 6.0, ((0, 2), (1, 4), (2, 2))),
        "dt_raw": draw_dt_raw(jax.random.fold_in(jax.random.fold_in(keys[10], part), 71), part),
        "decay_rate": jnp.clip(jnp.exp(math.log(0.033) - 3.3379025 * jax.random.uniform(keys[4], (HEADS,), jnp.float32) ** steps_of(keys[4], (HEADS,), ((0, 2),), -0.2, 0.2)), 0.001171875, 0.033),
        "conv_x": noise(keys[5], (4, INNER), 0.5, 3.0, ((1, 2),), jnp.float32),
        "conv_bc": noise(keys[6], (4, 2 * STATE), 0.5, 3.0, (), jnp.float32),
        "skip_gain": draw_skip_gain(jax.random.fold_in(keys[10], 71), part),
        "span_len": jax.vmap(lambda own: ragged(own, SPANS, TOKENS_PER_GROUP, MOST, 1))(jax.random.split(own_keys[8], GROUP_COUNT)).reshape((GROUP_COUNT, SPANS)).astype(jnp.int32),
        "grad_y": noise(own_keys[9], (GROUP_COUNT, TOKENS_PER_GROUP, INNER), 1.0, 6.0, ((0, 2), (1, 4), (2, 2))),
    }


exact_mode = lax.Precision.HIGHEST

def causal_conv(values, conv_taps, segment):
    tok_rows = values.shape[0] - 3
    summed = jnp.zeros((tok_rows, values.shape[1]), jnp.float32)
    for offset in range(4):
        same_span = (segment[offset:offset + tok_rows] == segment[3:]).astype(jnp.float32)
        summed = summed + conv_taps[offset][None, :] * values[offset:offset + tok_rows] * same_span[:, None]
    return summed

def prepare(x_halo, bc_halo, raw_steps, segment, conv_x, conv_bc, decay_rate):
    x_conv = jax.nn.silu(causal_conv(x_halo, conv_x, segment))
    bc_conv = jax.nn.silu(causal_conv(bc_halo, conv_bc, segment))
    dt_soft = jax.nn.softplus(raw_steps)
    log_step = -dt_soft * decay_rate[None, :]
    return (x_conv, bc_conv[:, :STATE], bc_conv[:, STATE:], dt_soft, log_step)

def block_outputs(x_conv, b_state, c_state, dt_soft, log_step, start_state, segment, seg_before, skip_gain):
    tok_rows = x_conv.shape[0]
    head_count = dt_soft.shape[1]
    x_heads = x_conv.reshape(tok_rows, head_count, -1)
    cumulative = jnp.cumsum(log_step, axis=0).T
    token_index = jnp.arange(tok_rows)
    within = (segment[:, None] == segment[None, :]) & (token_index[:, None] >= token_index[None, :])
    log_gap = cumulative[:, :, None] - cumulative[:, None, :]
    decay_table = jnp.where(within[None], jnp.exp(jnp.where(within[None], log_gap, 0.0)), 0.0)
    scores = jnp.dot(c_state, b_state.T, precision=exact_mode, preferred_element_type=jnp.float32)
    weighted = x_heads * dt_soft[:, :, None]
    intra_out = jnp.einsum('hts,shp->thp', decay_table * scores[None], weighted, precision=exact_mode)
    alive_mask = (segment == seg_before).astype(jnp.float32)
    carried = jnp.exp(cumulative.T) * alive_mask[:, None]
    state_out = jnp.einsum('tn,hpn->thp', c_state, start_state, precision=exact_mode) * carried[:, :, None]
    result = intra_out + state_out + skip_gain[None, :, None] * x_heads
    return result.reshape(tok_rows, -1)

def block_ends(x_conv, b_state, dt_soft, log_step, segment, seg_before):
    tok_rows = x_conv.shape[0]
    head_count = dt_soft.shape[1]
    x_heads = x_conv.reshape(tok_rows, head_count, -1)
    cumulative = jnp.cumsum(log_step, axis=0)
    last_same = (segment == segment[-1]).astype(jnp.float32)
    toward = jnp.exp(cumulative[-1][None, :] - cumulative) * last_same[:, None]
    weighted = x_heads * (dt_soft * toward)[:, :, None]
    ends_state = jnp.einsum('shp,sn->hpn', weighted, b_state, precision=exact_mode)
    through = jnp.exp(cumulative[-1]) * (segment[-1] == seg_before).astype(jnp.float32)
    return (through, ends_state)

def reference(hidden_in, w_bc, x_in, dt_raw, decay_rate, conv_x, conv_bc, skip_gain, span_len, grad_y):
    blocks = TOKENS_PER_GROUP // TOK_DEV

    def one_list(grad_w, list_items):
        hidden, x_list, raw_list, lengths, cotangent = list_items
        span_ends = jnp.cumsum(lengths)
        position = jnp.arange(TOKENS_PER_GROUP)
        segment = lax.optimization_barrier(jnp.sum((span_ends[None, :] <= position[:, None]).astype(jnp.int32), axis=1)).astype(jnp.int32)
        padded_seg = jnp.concatenate([jnp.full((3,), -1, jnp.int32), segment])
        bc_pre = jnp.dot(hidden, w_bc, preferred_element_type=jnp.float32).astype(jnp.bfloat16)
        befores = padded_seg[2:2 + TOKENS_PER_GROUP:TOK_DEV]

        def forward(x_vals, bc_vals, raw_vals):
            x_halo = jnp.concatenate([jnp.zeros((3, INNER), jnp.float32), x_vals])
            bc_halo = jnp.concatenate([jnp.zeros((3, 2 * STATE), jnp.float32), bc_vals])
            x_conv, b_state, c_state, dt_soft, log_step = prepare(x_halo, bc_halo, raw_vals, padded_seg, conv_x, conv_bc, decay_rate)

            def block_step(carry_state, block_items):
                x_block, b_block, c_block, dt_block, log_block, seg_block, before = block_items
                result = block_outputs(x_block, b_block, c_block, dt_block, log_block, carry_state, seg_block, before, skip_gain)
                through, ends_state = block_ends(x_block, b_block, dt_block, log_block, seg_block, before)
                return (through[:, None, None] * carry_state + ends_state, result)
            block_items = (x_conv.reshape(blocks, TOK_DEV, INNER), b_state.reshape(blocks, TOK_DEV, STATE), c_state.reshape(blocks, TOK_DEV, STATE), dt_soft.reshape(blocks, TOK_DEV, HEADS), log_step.reshape(blocks, TOK_DEV, HEADS), segment.reshape(blocks, TOK_DEV), befores)
            start = jnp.zeros((HEADS, HEAD_DIM, STATE), jnp.float32)
            unused, outputs = lax.scan(block_step, start, block_items)
            return outputs.reshape(TOKENS_PER_GROUP, INNER)
        unused, pullback = jax.vjp(forward, x_list.astype(jnp.float32), bc_pre.astype(jnp.float32), raw_list)
        grad_xin, d_bcpre, grad_raw = pullback(cotangent.astype(jnp.float32))
        d_bc = d_bcpre.astype(jnp.bfloat16)
        grad_hidden = jnp.dot(d_bc, w_bc.T, preferred_element_type=jnp.float32).astype(jnp.bfloat16)
        grad_w = grad_w + lax.dot_general(hidden, d_bc, (((0,), (0,)), ((), ())), preferred_element_type=jnp.float32)
        return (grad_w, (grad_xin.astype(jnp.bfloat16), grad_hidden, grad_raw))
    start_w = jnp.zeros((D, 2 * STATE), jnp.float32)
    grad_w, stacked = lax.scan(one_list, start_w, (hidden_in, x_in, dt_raw, span_len, grad_y))
    grad_x, grad_u, grad_dt = stacked
    return (grad_x, grad_u, grad_dt, grad_w.reshape(N_HEAD, D // N_HEAD, 2 * STATE))
```

```python
import jax
import jax.numpy as jnp
from jax import lax
from jax.experimental import pallas as pl
from jax.experimental.pallas import tpu as pltpu
from jax.sharding import PartitionSpec as P

STATE = 128
HEAD = 64
MOST = 256
BF = jnp.bfloat16
F32 = jnp.float32
EXACT = lax.Precision.HIGHEST


def shifted(block, axis, distance):
    devices = range(lax.axis_size(axis))
    route = [(i - distance, i) for i in devices if i - distance in devices]
    return lax.ppermute(block, axis, route)


def dot(a, b, ca, cb, precision=None):
    return lax.dot_general(
        a, b, (((ca,), (cb,)), ((), ())), precision=precision, preferred_element_type=F32
    )


def ssm_kernel(
    x2, x1, x0, g0, g1, g2, b2, b1, b0, b3, b4, raw_ref, info_ref, segrow_ref,
    decay_ref, skip_ref, tapx_ref, tapb_ref,
    dx_ref, tail_ref, rim_ref, dbc_ref, rimbc_ref, ddt_ref,
    masks, bias_ref, s_ref, cols_a, cols_b, cum_rows, bprev, cnext, bown, cown,
    silu_bc, d_s, d_b, d_c, acc,
):
    T = x0.shape[0]
    pairs = x0.shape[1] // 128
    lane = lax.broadcasted_iota(jnp.int32, (T, 128), 1)
    row = lax.broadcasted_iota(jnp.int32, (T, 128), 0)
    low = lane < HEAD
    group = lane // 32
    info = info_ref[...]
    for k in range(3):
        masks[k] = jnp.broadcast_to(info[: 3 * T, k : k + 1], (3 * T, 128))

    def col(block, k):
        return info[block * T : (block + 1) * T, k : k + 1]

    tri = (row >= lane).astype(F32)
    decay = decay_ref[...]
    dts, cums, carried, toward = [], [], [], []
    for j in range(5):
        raw = raw_ref[j * T : (j + 1) * T, :]
        dt = jnp.maximum(raw, 0.0) + jnp.log1p(jnp.exp(-jnp.abs(raw)))
        cum = dot(tri, -dt * decay, 1, 0, EXACT)
        dts.append(dt)
        cums.append(cum)
        carried.append(jnp.exp(cum) * col(j, 3))
        toward.append(jnp.exp(cum[T - 1 :, :] - cum) * col(j, 4))
    a1 = dts[1] * toward[1]
    a2 = dts[0] * toward[0] * carried[1][T - 1 :, :]
    c1 = carried[3]
    c2 = carried[4] * carried[3][T - 1 :, :]

    def packed(p, q, r, s):
        return jnp.where(group == 0, p, jnp.where(group == 1, q, jnp.where(group == 2, r, s)))

    cols_a[...] = packed(dts[2], cums[2], carried[2], toward[2])
    cols_b[...] = packed(a2, a1, c1, c2)
    cum_rows[...] = cums[2].T
    same = col(2, 5) == segrow_ref[...]
    bias_ref[...] = jnp.where(same & (row >= lane), 0.0, -1e30)

    taps_b = tapb_ref[...]
    bc = jnp.concatenate([b2[...], b1[...], b0[...], b3[...], b4[...]]).astype(F32)
    pre_bc = taps_b[3:4, :] * bc
    for k in range(3):
        pre_bc += taps_b[k : k + 1, :] * pltpu.roll(bc, 3 - k, 0) * info[:, k : k + 1]
    sig_bc = jax.nn.sigmoid(pre_bc)
    conv_bc = pre_bc * sig_bc
    own_sig = sig_bc[2 * T : 3 * T]
    silu_bc[...] = own_sig * (1.0 + pre_bc[2 * T : 3 * T] * (1.0 - own_sig))
    bprev[...] = conv_bc[: 2 * T, :STATE].astype(BF)
    cnext[...] = conv_bc[3 * T :, STATE:].astype(BF)
    bown[...] = conv_bc[2 * T : 3 * T, :STATE]
    cown[...] = conv_bc[2 * T : 3 * T, STATE:]
    s_ref[...] = dot(cown[...], bown[...], 1, 1, EXACT)
    d_s[...] = jnp.zeros_like(d_s)
    d_b[...] = jnp.zeros_like(d_b)
    d_c[...] = jnp.zeros_like(d_c)
    acc[...] = jnp.zeros_like(acc)

    def pair(i, carry):
        at = pl.ds(pl.multiple_of(i * 128, 128), 128)
        ca = pltpu.roll(cols_a[...], (128 - 2 * i) % 128, 1)
        cb = pltpu.roll(cols_b[...], (128 - 2 * i) % 128, 1)

        def wide(c, q):
            return jnp.where(low, c[:, 32 * q : 32 * q + 1], c[:, 32 * q + 1 : 32 * q + 2])

        def tall(c, q):
            return c[:, 32 * q : 32 * q + 1], c[:, 32 * q + 1 : 32 * q + 2]

        taps = tapx_ref[:, at]
        xe = jnp.concatenate([x2[:, at], x1[:, at], x0[:, at]]).astype(F32)
        pre = taps[3:4, :] * xe
        for k in range(3):
            pre += taps[k : k + 1, :] * pltpu.roll(xe, 3 - k, 0) * masks[k]
        sig = jax.nn.sigmoid(pre)
        xc = pre * sig
        xown = xc[2 * T :]
        sown = sig[2 * T :]
        dsilu = sown * (1.0 + pre[2 * T :] * (1.0 - sown))
        dt_w = wide(ca, 0)
        toward_w = wide(ca, 3)
        xw = jnp.concatenate([xc[:T] * wide(cb, 0), xc[T : 2 * T] * wide(cb, 1)]).astype(BF)
        start = dot(xw, bprev[...], 0, 0)
        gw = jnp.concatenate(
            [g1[:, at].astype(F32) * wide(cb, 2), g2[:, at].astype(F32) * wide(cb, 3)]
        ).astype(BF)
        end_grad = dot(gw, cnext[...], 0, 0)
        start_b = start.astype(BF)
        end_b = end_grad.astype(BF)
        gy = g0[:, at].astype(F32)
        gg = jnp.concatenate([jnp.where(low, gy, 0.0), jnp.where(low, 0.0, gy)]).astype(BF)
        xt = xown * dt_w
        xt_b = xt.astype(BF)
        xx = jnp.concatenate([jnp.where(low, xt, 0.0), jnp.where(low, 0.0, xt)]).astype(BF)
        d_m = dot(gg, xt_b, 1, 1)
        cum_a, cum_b = tall(ca, 1)
        bias = bias_ref[...]
        decay_t = jnp.concatenate(
            [
                jnp.exp(cum_a - cum_rows[pl.ds(2 * i, 1), :] + bias),
                jnp.exp(cum_b - cum_rows[pl.ds(2 * i + 1, 1), :] + bias),
            ]
        )
        s_all = s_ref[...]
        s_two = jnp.concatenate([s_all, s_all])
        ls = decay_t * s_two
        ldm = decay_t * d_m
        d_s[...] += ldm[:T] + ldm[T:]
        d_x = dot(ls.astype(BF), gg, 0, 0)
        car = jnp.concatenate(tall(ca, 2))
        tow = jnp.concatenate(tall(ca, 3))
        c_u = car * dot(gg, start_b, 1, 0)
        d_c[...] += c_u[:T] + c_u[T:]
        c_own = cown[...]
        c_two = jnp.concatenate([c_own, c_own])
        r = jnp.sum(ldm * s_two + c_u * c_two, axis=1, keepdims=True)
        t_v = tow * dot(xx, end_b, 1, 0)
        d_b[...] += t_v[:T] + t_v[T:]
        d_xe = dot(bown[...].astype(BF), end_b, 1, 1) * toward_w
        d_xt = d_x + d_xe
        prod = xown * d_xt
        q_a = jnp.sum(jnp.where(low, prod, 0.0), axis=1, keepdims=True)
        q_b = jnp.sum(jnp.where(low, 0.0, prod), axis=1, keepdims=True)
        ends = jnp.sum(xt * d_xe, axis=0, keepdims=True)
        inner = end_grad * start
        low_row = low[:1]
        through_a, through_b = (v[T - 1 :, :] for v in tall(ca, 2))
        last_a = jnp.sum(jnp.where(low_row, ends, 0.0), axis=1, keepdims=True) + through_a * jnp.sum(
            jnp.sum(inner[:HEAD], axis=0, keepdims=True), axis=1, keepdims=True
        )
        last_b = jnp.sum(jnp.where(low_row, 0.0, ends), axis=1, keepdims=True) + through_b * jnp.sum(
            jnp.sum(inner[HEAD:], axis=0, keepdims=True), axis=1, keepdims=True
        )
        dt_a, dt_b = tall(ca, 0)
        final = row[:, :1] == T - 1
        cum_ga = r[:T] - dt_a * q_a + jnp.where(final, last_a, 0.0)
        cum_gb = r[T:] - dt_b * q_b + jnp.where(final, last_b, 0.0)
        placed = jnp.where(
            lane == 0,
            q_a,
            jnp.where(
                lane == 1, q_b, jnp.where(lane == 32, cum_ga, jnp.where(lane == 33, cum_gb, 0.0))
            ),
        )
        acc[...] += pltpu.roll(placed, 2 * i, 1)
        d_pre = (dt_w * d_xt + skip_ref[:, at] * gy) * dsilu
        own = taps[3:4, :] * d_pre
        rim = jnp.zeros((8, 128), F32)
        for k in range(3):
            d = 3 - k
            z = pltpu.roll(taps[k : k + 1, :] * masks[k, 2 * T :] * d_pre, T - d, 0)
            own += jnp.where(row < T - d, z, 0.0)
            rim += jnp.where(row[T - 8 :] < T - d, 0.0, z[T - 8 :])
        dx_ref[:, at] = own.astype(BF)
        tail_ref[:, at] = own[T - 8 :]
        rim_ref[:, at] = rim
        return carry

    lax.fori_loop(0, pairs, pair, 0)

    ds = d_s[...]
    full_c = d_c[...] + dot(ds, bown[...], 1, 0, EXACT)
    full_b = d_b[...] + dot(ds, cown[...], 0, 0, EXACT)
    d_pre = jnp.concatenate([full_b, full_c], axis=1) * silu_bc[...]
    own = taps_b[3:4, :] * d_pre
    rim = jnp.zeros((8, 2 * STATE), F32)
    row2 = lax.broadcasted_iota(jnp.int32, (T, 2 * STATE), 0)
    for k in range(3):
        d = 3 - k
        z = pltpu.roll(taps_b[k : k + 1, :] * info[2 * T : 3 * T, k : k + 1] * d_pre, T - d, 0)
        own += jnp.where(row2 < T - d, z, 0.0)
        rim += jnp.where(row2[T - 8 :] < T - d, 0.0, z[T - 8 :])
    dbc_ref[...] = own
    rimbc_ref[...] = rim
    total = acc[...]
    d_log = pltpu.roll(dot(tri, total, 0, 0, EXACT), 96, 1)
    raw = raw_ref[2 * T : 3 * T, :]
    ddt_ref[...] = ((total - decay * d_log) * jax.nn.sigmoid(raw))[:, :32]


def ssm(xs, gs, bcs, raw, info, segrow, decay, skip, tapx, tapb):
    T, W = xs[0].shape
    vm = pltpu.VMEM
    return pl.pallas_call(
        ssm_kernel,
        out_shape=(
            jax.ShapeDtypeStruct((T, W), BF),
            jax.ShapeDtypeStruct((8, W), F32),
            jax.ShapeDtypeStruct((8, W), F32),
            jax.ShapeDtypeStruct((T, 2 * STATE), F32),
            jax.ShapeDtypeStruct((8, 2 * STATE), F32),
            jax.ShapeDtypeStruct((T, 32), F32),
        ),
        scratch_shapes=[
            vm((3, 3 * T, 128), F32), vm((T, T), F32), vm((T, T), F32), vm((T, 128), F32),
            vm((T, 128), F32), vm((128, T), F32), vm((2 * T, STATE), BF), vm((2 * T, STATE), BF),
            vm((T, STATE), F32), vm((T, STATE), F32), vm((T, 2 * STATE), F32),
            vm((T, T), F32), vm((T, STATE), F32), vm((T, STATE), F32), vm((T, 128), F32),
        ],
        compiler_params=pltpu.CompilerParams(vmem_limit_bytes=40 << 20),
        cost_estimate=pl.CostEstimate(
            flops=2 * 9 * T * 256 * W, bytes_accessed=8 * T * W * 2, transcendentals=6 * T * W
        ),
    )(*xs, *gs, *bcs, raw, info, segrow, decay, skip, tapx, tapb)


def on_device(
    hidden_in, w_bc, x_in, dt_raw, decay_rate, conv_x, conv_bc, skip_gain, span_len, grad_y
):
    T = x_in.shape[1]
    hidden = hidden_in[0]
    half_width = hidden.shape[1]
    n_ctx, n_fsdp, n_head = (lax.axis_size(a) for a in ("ctx", "fsdp", "head"))
    assert T * 2 == MOST and dt_raw.shape[2] == 32
    x0, g0, raw0 = x_in[0], grad_y[0], dt_raw[0]
    if n_fsdp == n_head:
        route = [(f * n_head + h, h * n_head + f) for f in range(n_fsdp) for h in range(n_head)]
        w_half = lax.ppermute(w_bc, ("fsdp", "head"), route)
    else:
        w_full = lax.all_gather(w_bc, "fsdp", axis=0, tiled=True)
        w_half = lax.dynamic_slice_in_dim(
            w_full, lax.axis_index("head") * half_width, half_width, 0
        )
    raws = [shifted(raw0, "ctx", d) for d in (2, 1)] + [raw0] + [shifted(raw0, "ctx", -d) for d in (1, 2)]
    x1, g1 = shifted(x0, "ctx", 1), shifted(g0, "ctx", -1)
    x2, g2 = shifted(x0, "ctx", 2), shifted(g0, "ctx", -2)

    swap = [(i, (i + 1) % n_head) for i in range(n_head)]
    partial_bc = jnp.dot(hidden, w_half, preferred_element_type=F32)
    bc_pre = (partial_bc + lax.ppermute(partial_bc, "head", swap)).astype(BF)
    bcs = [shifted(bc_pre, "ctx", d) for d in (2, 1)] + [bc_pre] + [shifted(bc_pre, "ctx", -d) for d in (1, 2)]

    n_blocks = n_ctx * n_fsdp
    blocks = hidden.reshape(T, n_blocks, half_width // n_blocks).transpose(1, 0, 2)
    hidden_all = lax.all_to_all(blocks, ("ctx", "fsdp"), 0, 0, tiled=True)

    position = (lax.axis_index("ctx") - 2) * T + jnp.arange(-3, 5 * T, dtype=jnp.int32)
    spans = span_len.shape[1]
    earlier = jnp.arange(spans)[:, None] <= jnp.arange(spans)[None, :]
    span_ends = jnp.sum(jnp.where(earlier, span_len[0][:, None], 0), axis=0)
    counted = jnp.sum((span_ends[None, :] <= position[:, None]).astype(jnp.int32), axis=1)
    segment = jnp.where(position >= 0, counted, -1).astype(F32)
    own_seg = segment[3:]
    by_block = own_seg.reshape(5, T)
    before = jnp.broadcast_to(segment[2 : 2 + 5 * T : T][:, None], (5, T)).reshape(-1)
    last = jnp.broadcast_to(by_block[:, T - 1 :], (5, T)).reshape(-1)
    info = jnp.stack(
        [(segment[k : k + 5 * T] == own_seg).astype(F32) for k in range(3)]
        + [(own_seg == before).astype(F32), (own_seg == last).astype(F32), own_seg],
        axis=1,
    )
    segrow = by_block[2:3]
    raw = jnp.tile(jnp.concatenate(raws), (1, 4))
    decay = jnp.tile(decay_rate, 4)[None, :]
    skip = jnp.repeat(skip_gain, HEAD)[None, :]

    dx, tail, rim, dbc, rimbc, ddt = ssm(
        (x2, x1, x0), (g0, g1, g2), bcs, raw, info, segrow, decay, skip, conv_x, conv_bc
    )
    back = shifted(rim, "ctx", -1)
    grad_x = lax.dynamic_update_slice(dx, (tail + back).astype(BF), (T - 8, 0))

    other = lax.ppermute(dbc, "head", swap)
    rim_same = shifted(rimbc, "ctx", -1)
    cross = [
        (c * n_head + h, (c - 1) * n_head + (h + 1) % n_head)
        for c in range(1, n_ctx)
        for h in range(n_head)
    ]
    rim_cross = lax.ppermute(rimbc, ("ctx", "head"), cross)
    d_bc = ((dbc + other) + jnp.pad(rim_same + rim_cross, ((T - 8, 0), (0, 0)))).astype(BF)
    grad_u = lax.dot_general(
        d_bc, w_half, (((1,), (1,)), ((), ())), preferred_element_type=F32
    ).astype(BF)
    d_all = lax.all_gather(d_bc, ("ctx", "fsdp"), axis=0)
    grad_w = lax.dot_general(
        hidden_all.reshape(n_blocks * T, -1),
        d_all.reshape(n_blocks * T, -1),
        (((0,), (0,)), ((), ())),
        preferred_element_type=F32,
    )
    return (grad_x[None], grad_u[None], ddt[None], grad_w[None])


def solution(mesh):
    return jax.shard_map(
        on_device,
        mesh=mesh,
        in_specs=(
            P(("groups", "fsdp"), "ctx", "head"),
            P("fsdp", None),
            P(("groups", "fsdp"), "ctx", "head"),
            P(("groups", "fsdp"), "ctx", "head"),
            P("head"),
            P(None, "head"),
            P(),
            P("head"),
            P(("groups", "fsdp"), None),
            P(("groups", "fsdp"), "ctx", "head"),
        ),
        out_specs=(
            P(("groups", "fsdp"), "ctx", "head"),
            P(("groups", "fsdp"), "ctx", "head"),
            P(("groups", "fsdp"), "ctx", "head"),
            P(("groups", "head"), ("ctx", "fsdp"), None),
        ),
        check_vma=False,
    )
```

```python
import jax
import jax.numpy as jnp
from jax import lax
from jax.experimental import pallas as pl
from jax.experimental.pallas import tpu as pltpu
from jax.sharding import PartitionSpec as P

STATE = 128
HEAD = 64
MOST = 256
BF = jnp.bfloat16
F32 = jnp.float32
EXACT = lax.Precision.HIGHEST


def shifted(block, axis, distance):
    devices = range(lax.axis_size(axis))
    route = [(i - distance, i) for i in devices if i - distance in devices]
    return lax.ppermute(block, axis, route)


def dot(a, b, ca, cb, precision=None):
    return lax.dot_general(
        a, b, (((ca,), (cb,)), ((), ())), precision=precision, preferred_element_type=F32
    )


def ssm_kernel(
    x2, x1, x0, g0, g1, g2, b2, b1, b0, b3, b4, raw_ref, info_ref, segrow_ref,
    decay_ref, skip_ref, tapx_ref, tapb_ref,
    dx_ref, tail_ref, rim_ref, dbc_ref, rimbc_ref, ddt_ref,
    masks, bias_ref, s_ref, cols_a, cols_b, cum_rows, bprev, cnext, bown, cown,
    silu_bc, d_s, d_b, d_c, acc,
):
    T = x0.shape[0]
    pairs = x0.shape[1] // 128
    lane = lax.broadcasted_iota(jnp.int32, (T, 128), 1)
    row = lax.broadcasted_iota(jnp.int32, (T, 128), 0)
    low = lane < HEAD
    group = lane // 32
    info = info_ref[...]
    for k in range(3):
        masks[k] = jnp.broadcast_to(info[: 3 * T, k : k + 1], (3 * T, 128))

    def col(block, k):
        return info[block * T : (block + 1) * T, k : k + 1]

    tri = (row >= lane).astype(F32)
    decay = decay_ref[...]
    dts, cums, carried, toward = [], [], [], []
    for j in range(5):
        raw = raw_ref[j * T : (j + 1) * T, :]
        dt = jnp.maximum(raw, 0.0) + jnp.log1p(jnp.exp(-jnp.abs(raw)))
        cum = dot(tri, -dt * decay, 1, 0, EXACT)
        dts.append(dt)
        cums.append(cum)
        carried.append(jnp.exp(cum) * col(j, 3))
        toward.append(jnp.exp(cum[T - 1 :, :] - cum) * col(j, 4))
    a1 = dts[1] * toward[1]
    a2 = dts[0] * toward[0] * carried[1][T - 1 :, :]
    c1 = carried[3]
    c2 = carried[4] * carried[3][T - 1 :, :]

    def packed(p, q, r, s):
        return jnp.where(group == 0, p, jnp.where(group == 1, q, jnp.where(group == 2, r, s)))

    cols_a[...] = packed(dts[2], cums[2], carried[2], toward[2])
    cols_b[...] = packed(a2, a1, c1, c2)
    cum_rows[...] = cums[2].T
    same = col(2, 5) == segrow_ref[...]
    bias_ref[...] = jnp.where(same & (row >= lane), 0.0, -1e30)

    taps_b = tapb_ref[...]
    bc = jnp.concatenate([b2[...], b1[...], b0[...], b3[...], b4[...]]).astype(F32)
    pre_bc = taps_b[3:4, :] * bc
    for k in range(3):
        pre_bc += taps_b[k : k + 1, :] * pltpu.roll(bc, 3 - k, 0) * info[:, k : k + 1]
    sig_bc = jax.nn.sigmoid(pre_bc)
    conv_bc = pre_bc * sig_bc
    own_sig = sig_bc[2 * T : 3 * T]
    silu_bc[...] = own_sig * (1.0 + pre_bc[2 * T : 3 * T] * (1.0 - own_sig))
    bprev[...] = conv_bc[: 2 * T, :STATE].astype(BF)
    cnext[...] = conv_bc[3 * T :, STATE:].astype(BF)
    bown[...] = conv_bc[2 * T : 3 * T, :STATE]
    cown[...] = conv_bc[2 * T : 3 * T, STATE:]
    s_ref[...] = dot(cown[...], bown[...], 1, 1, EXACT)
    d_s[...] = jnp.zeros_like(d_s)
    d_b[...] = jnp.zeros_like(d_b)
    d_c[...] = jnp.zeros_like(d_c)
    acc[...] = jnp.zeros_like(acc)

    def pair(i, carry):
        at = pl.ds(pl.multiple_of(i * 128, 128), 128)
        ca = pltpu.roll(cols_a[...], (128 - 2 * i) % 128, 1)
        cb = pltpu.roll(cols_b[...], (128 - 2 * i) % 128, 1)

        def wide(c, q):
            return jnp.where(low, c[:, 32 * q : 32 * q + 1], c[:, 32 * q + 1 : 32 * q + 2])

        def tall(c, q):
            return c[:, 32 * q : 32 * q + 1], c[:, 32 * q + 1 : 32 * q + 2]

        taps = tapx_ref[:, at]
        xe = jnp.concatenate([x2[:, at], x1[:, at], x0[:, at]]).astype(F32)
        pre = taps[3:4, :] * xe
        for k in range(3):
            pre += taps[k : k + 1, :] * pltpu.roll(xe, 3 - k, 0) * masks[k]
        sig = jax.nn.sigmoid(pre)
        xc = pre * sig
        xown = xc[2 * T :]
        sown = sig[2 * T :]
        dsilu = sown * (1.0 + pre[2 * T :] * (1.0 - sown))
        dt_w = wide(ca, 0)
        toward_w = wide(ca, 3)
        xw = jnp.concatenate([xc[:T] * wide(cb, 0), xc[T : 2 * T] * wide(cb, 1)]).astype(BF)
        start = dot(xw, bprev[...], 0, 0)
        gw = jnp.concatenate(
            [g1[:, at].astype(F32) * wide(cb, 2), g2[:, at].astype(F32) * wide(cb, 3)]
        ).astype(BF)
        end_grad = dot(gw, cnext[...], 0, 0)
        start_b = start.astype(BF)
        end_b = end_grad.astype(BF)
        gy = g0[:, at].astype(F32)
        gg = jnp.concatenate([jnp.where(low, gy, 0.0), jnp.where(low, 0.0, gy)]).astype(BF)
        xt = xown * dt_w
        xt_b = xt.astype(BF)
        xx = jnp.concatenate([jnp.where(low, xt, 0.0), jnp.where(low, 0.0, xt)]).astype(BF)
        d_m = dot(gg, xt_b, 1, 1)
        cum_a, cum_b = tall(ca, 1)
        bias = bias_ref[...]
        decay_t = jnp.concatenate(
            [
                jnp.exp(cum_a - cum_rows[pl.ds(2 * i, 1), :] + bias),
                jnp.exp(cum_b - cum_rows[pl.ds(2 * i + 1, 1), :] + bias),
            ]
        )
        s_all = s_ref[...]
        s_two = jnp.concatenate([s_all, s_all])
        ls = decay_t * s_two
        ldm = decay_t * d_m
        d_s[...] += ldm[:T] + ldm[T:]
        d_x = dot(ls.astype(BF), gg, 0, 0)
        car = jnp.concatenate(tall(ca, 2))
        tow = jnp.concatenate(tall(ca, 3))
        c_u = car * dot(gg, start_b, 1, 0)
        d_c[...] += c_u[:T] + c_u[T:]
        c_own = cown[...]
        c_two = jnp.concatenate([c_own, c_own])
        r = jnp.sum(ldm * s_two + c_u * c_two, axis=1, keepdims=True)
        t_v = tow * dot(xx, end_b, 1, 0)
        d_b[...] += t_v[:T] + t_v[T:]
        d_xe = dot(bown[...].astype(BF), end_b, 1, 1) * toward_w
        d_xt = d_x + d_xe
        prod = xown * d_xt
        q_a = jnp.sum(jnp.where(low, prod, 0.0), axis=1, keepdims=True)
        q_b = jnp.sum(jnp.where(low, 0.0, prod), axis=1, keepdims=True)
        ends = jnp.sum(xt * d_xe, axis=0, keepdims=True)
        inner = end_grad * start
        low_row = low[:1]
        through_a, through_b = (v[T - 1 :, :] for v in tall(ca, 2))
        last_a = jnp.sum(jnp.where(low_row, ends, 0.0), axis=1, keepdims=True) + through_a * jnp.sum(
            jnp.sum(inner[:HEAD], axis=0, keepdims=True), axis=1, keepdims=True
        )
        last_b = jnp.sum(jnp.where(low_row, 0.0, ends), axis=1, keepdims=True) + through_b * jnp.sum(
            jnp.sum(inner[HEAD:], axis=0, keepdims=True), axis=1, keepdims=True
        )
        dt_a, dt_b = tall(ca, 0)
        final = row[:, :1] == T - 1
        cum_ga = r[:T] - dt_a * q_a + jnp.where(final, last_a, 0.0)
        cum_gb = r[T:] - dt_b * q_b + jnp.where(final, last_b, 0.0)
        placed = jnp.where(
            lane == 0,
            q_a,
            jnp.where(
                lane == 1, q_b, jnp.where(lane == 32, cum_ga, jnp.where(lane == 33, cum_gb, 0.0))
            ),
        )
        acc[...] += pltpu.roll(placed, 2 * i, 1)
        d_pre = (dt_w * d_xt + skip_ref[:, at] * gy) * dsilu
        own = taps[3:4, :] * d_pre
        rim = jnp.zeros((8, 128), F32)
        for k in range(3):
            d = 3 - k
            z = pltpu.roll(taps[k : k + 1, :] * masks[k, 2 * T :] * d_pre, T - d, 0)
            own += jnp.where(row < T - d, z, 0.0)
            rim += jnp.where(row[T - 8 :] < T - d, 0.0, z[T - 8 :])
        dx_ref[:, at] = own.astype(BF)
        tail_ref[:, at] = own[T - 8 :]
        rim_ref[:, at] = rim
        return carry

    lax.fori_loop(0, pairs, pair, 0)

    ds = d_s[...]
    full_c = d_c[...] + dot(ds, bown[...], 1, 0, EXACT)
    full_b = d_b[...] + dot(ds, cown[...], 0, 0, EXACT)
    d_pre = jnp.concatenate([full_b, full_c], axis=1) * silu_bc[...]
    own = taps_b[3:4, :] * d_pre
    rim = jnp.zeros((8, 2 * STATE), F32)
    row2 = lax.broadcasted_iota(jnp.int32, (T, 2 * STATE), 0)
    for k in range(3):
        d = 3 - k
        z = pltpu.roll(taps_b[k : k + 1, :] * info[2 * T : 3 * T, k : k + 1] * d_pre, T - d, 0)
        own += jnp.where(row2 < T - d, z, 0.0)
        rim += jnp.where(row2[T - 8 :] < T - d, 0.0, z[T - 8 :])
    dbc_ref[...] = own
    rimbc_ref[...] = rim
    total = acc[...]
    d_log = pltpu.roll(dot(tri, total, 0, 0, EXACT), 96, 1)
    raw = raw_ref[2 * T : 3 * T, :]
    ddt_ref[...] = ((total - decay * d_log) * jax.nn.sigmoid(raw))[:, :32]


def ssm(xs, gs, bcs, raw, info, segrow, decay, skip, tapx, tapb):
    T, W = xs[0].shape
    vm = pltpu.VMEM
    return pl.pallas_call(
        ssm_kernel,
        out_shape=(
            jax.ShapeDtypeStruct((T, W), BF),
            jax.ShapeDtypeStruct((8, W), F32),
            jax.ShapeDtypeStruct((8, W), F32),
            jax.ShapeDtypeStruct((T, 2 * STATE), F32),
            jax.ShapeDtypeStruct((8, 2 * STATE), F32),
            jax.ShapeDtypeStruct((T, 32), F32),
        ),
        scratch_shapes=[
            vm((3, 3 * T, 128), F32), vm((T, T), F32), vm((T, T), F32), vm((T, 128), F32),
            vm((T, 128), F32), vm((128, T), F32), vm((2 * T, STATE), BF), vm((2 * T, STATE), BF),
            vm((T, STATE), F32), vm((T, STATE), F32), vm((T, 2 * STATE), F32),
            vm((T, T), F32), vm((T, STATE), F32), vm((T, STATE), F32), vm((T, 128), F32),
        ],
        compiler_params=pltpu.CompilerParams(vmem_limit_bytes=40 << 20),
        cost_estimate=pl.CostEstimate(
            flops=2 * 9 * T * 256 * W, bytes_accessed=8 * T * W * 2, transcendentals=6 * T * W
        ),
    )(*xs, *gs, *bcs, raw, info, segrow, decay, skip, tapx, tapb)


MESH = pl.DeviceIdType.MESH
NC = 256
HI = 16


def pieces(v):
    hi = v.astype(BF)
    rest = v - hi.astype(F32)
    mid = rest.astype(BF)
    lo = (rest - mid.astype(F32)).astype(BF)
    return hi, mid, lo


def fused_kernel(
    hidden, w, x, g, raw_ref, decay_ref, skip_ref, tapx_ref, tapb_ref, span_ref,
    gx_out, gu_out, ddt_ref, gw_out,
    xv, gv, hv, wh, xhalo, xf, dsf, aw, bw, dtw, bx, tx, ag, thrc, start, endg, sn, sp,
    masks, same_ref, alive_ref, last_ref, small, ds_acc, part, partr, tails, silu_bc,
    sm_ref, lastb, alivec, db_acc, dc_acc, dps, dpsr, rims, rimx_s, rimx_r, gxtail, r_acc, q_acc, l_acc,
    hall, dall, gxs, gus, gws,
    s_loc, s_ws, s_wr, s_ys, s_yr, s_hs, s_hr, s_halo, s_fs, s_fr, s_bs, s_br,
    s_ps, s_pr, s_tr, s_ds, s_dr, s_rr, s_rim, s_zs, s_zr, s_xs, s_xr, s_cs, s_cr, s_out,
):
    T, W = gxs.shape
    gi, c, f, h = (lax.axis_index(a) for a in ("groups", "ctx", "fsdp", "head"))
    n_ctx = lax.axis_size("ctx")
    DH = hv.shape[1]
    chunks = W // NC
    wrows = wh.shape[0] // 2 // chunks
    heads = raw_ref.shape[1]
    wb = hall.shape[2]
    first, last_c = c == 0, c == n_ctx - 1
    needing = h != f
    me = c * 2 + f

    def remote(src, dst, ss, rs, device):
        return pltpu.make_async_remote_copy(
            src_ref=src, dst_ref=dst, send_sem=ss, recv_sem=rs, device_id=device, device_id_type=MESH
        )

    barrier = pltpu.get_barrier_semaphore()
    for o in range(1, 4 * n_ctx):
        oc, of, oh = o // 4, (o // 2) % 2, o % 2
        pl.semaphore_signal(
            barrier, 1, device_id=(gi, lax.rem(c + oc, n_ctx), lax.rem(f + of, 2), lax.rem(h + oh, 2)),
            device_id_type=MESH,
        )
    pl.semaphore_signal(barrier, 1, device_id=(1 - gi, c, f, h), device_id_type=MESH)
    pl.semaphore_wait(barrier, 4 * n_ctx)

    def w_rows(k):
        return pl.ds(pl.multiple_of(k * wrows, wrows), wrows)

    def w_send(k):
        at = w_rows(gi * chunks + k)
        return remote(w.at[at], wh.at[at], s_ws.at[k], s_wr.at[k], (gi, c, 1 - f, h))

    def w_forward(k):
        at = w_rows(gi * chunks + k)
        return remote(wh.at[at], wh.at[at], s_ys.at[k], s_yr.at[k], (1 - gi, c, f, h))

    def h_send(d, ff):
        cc = lax.rem(c + d, n_ctx)
        at = pl.ds(pl.multiple_of((cc * 2 + ff) * wb, wb), wb)
        return remote(
            hidden.at[:, at], hall.at[me], s_hs.at[d + n_ctx * (1 if ff is not f else 0)], s_hr.at[me], (gi, cc, ff, h)
        )

    halo_copy = remote(
        x.at[T - HI :], xhalo, s_halo.at[0], s_halo.at[1], (gi, lax.rem(c + 1, n_ctx), f, h)
    )

    @pl.when(jnp.logical_not(last_c))
    def _():
        halo_copy.start()

    x_load = pltpu.make_async_copy(x, xv, s_loc.at[0])
    g_load = pltpu.make_async_copy(g, gv, s_loc.at[1])
    h_load = pltpu.make_async_copy(hidden, hv, s_loc.at[2])
    w_load = pltpu.make_async_copy(w, wh, s_loc.at[3])
    own_at = pl.ds(pl.multiple_of(me * wb, wb), wb)
    own_load = pltpu.make_async_copy(hidden.at[:, own_at], hall.at[me], s_loc.at[4])
    x_load.start()
    g_load.start()

    @pl.when(jnp.logical_not(needing))
    def _():
        lax.fori_loop(0, chunks, lambda k, z: (w_send(k).start(), z)[1], 0)
        w_load.start()

    for d in range(1, n_ctx):
        h_send(d, f).start()
    h_load.start()
    own_load.start()

    @pl.when(first)
    def _():
        xhalo[...] = jnp.zeros_like(xhalo)
        tails[...] = jnp.zeros_like(tails)
        start[...] = jnp.zeros_like(start)

    @pl.when(last_c)
    def _():
        endg[...] = jnp.zeros_like(endg)
        rims[...] = jnp.zeros_like(rims)
        rimx_r[...] = jnp.zeros_like(rimx_r)

    ends = [span_ref[0, 0]]
    for i in range(1, span_ref.shape[1]):
        ends.append(ends[-1] + span_ref[0, i])

    def segment(pos):
        counted = sum((e <= pos).astype(jnp.int32) for e in ends)
        return jnp.where(pos >= 0, counted, -1)

    pos0 = c * T
    row = lax.broadcasted_iota(jnp.int32, (T, 128), 0)
    lane = lax.broadcasted_iota(jnp.int32, (T, 128), 1)
    seg = segment(pos0 + row)
    for k in range(3):
        m = (segment(pos0 + row - 3 + k) == seg).astype(F32)
        masks[k] = jnp.concatenate([m, m], axis=1)
    same = (seg == segment(pos0 + lane)) & (row >= lane)
    same_ref[...] = same.astype(F32)
    seg_before = segment(jnp.full((T, 128), pos0 - 1, jnp.int32))
    seg_last = segment(jnp.full((T, 128), pos0 + T - 1, jnp.int32))
    alive_ref[...] = (seg == seg_before).astype(F32)
    last_ref[...] = (seg == seg_last).astype(F32)
    through = (seg_last == seg_before).astype(F32)[:heads]

    decay = decay_ref[...]
    raw = raw_ref[...]
    dt = jnp.maximum(raw, 0.0) + jnp.log1p(jnp.exp(-jnp.abs(raw)))
    tri = (row >= lane).astype(F32)
    cum = dot(tri, -dt * decay, 1, 0, EXACT)
    ea = jnp.exp(cum)
    eb = jnp.exp(-cum)
    small[0] = dt
    small[1] = ea
    small[2] = eb
    eye = (
        lax.broadcasted_iota(jnp.int32, (heads, heads), 0)
        == lax.broadcasted_iota(jnp.int32, (heads, heads), 1)
    ).astype(F32)
    ones = jnp.ones((heads, 128), BF)
    thr = through * sum(dot(p, ones, 1, 0) for p in pieces(eye * ea[T - 1 :, :]))
    ds_acc[...] = jnp.zeros_like(ds_acc)
    r_acc[...] = jnp.zeros_like(r_acc)
    q_acc[...] = jnp.zeros_like(q_acc)
    l_acc[...] = jnp.zeros_like(l_acc)
    db_acc[...] = jnp.zeros_like(db_acc)
    dc_acc[...] = jnp.zeros_like(dc_acc)

    per = NC // HEAD

    def spread(k):
        hr = lax.broadcasted_iota(jnp.int32, (heads, NC), 0)
        cl = lax.broadcasted_iota(jnp.int32, (heads, NC), 1)
        return (hr == k * per + cl // HEAD).astype(F32).astype(BF)

    def widen(v, sel):
        return sum(dot(p, sel, 1, 0) for p in pieces(v))

    def narrow(v, sel):
        hi, mid, _ = pieces(v)
        return dot(hi, sel, 1, 1) + dot(mid, sel, 1, 1)

    def chunk(k):
        return pl.ds(pl.multiple_of(k * NC, NC), NC)

    x_load.wait()
    g_load.wait()

    @pl.when(jnp.logical_not(first))
    def _():
        halo_copy.wait_recv()

    def prepare(k, z):
        @pl.when(needing)
        def _():
            w_send(k).wait_recv()
            w_forward(k).start()

        at = chunk(k)
        taps = tapx_ref[:, at]
        xe = jnp.concatenate([xhalo[:, at], xv[:, at]]).astype(F32)
        pre = taps[3:4, :] * xe[HI:]
        for d in range(1, 4):
            pre += taps[3 - d : 4 - d, :] * pltpu.roll(xe, d, 0)[HI:] * masks[3 - d]
        sig = jax.nn.sigmoid(pre)
        xc = pre * sig
        xf[:, at] = xc
        dsf[:, at] = sig * (1.0 + pre * (1.0 - sig))
        sel = spread(k)
        dt_w, a_w, b_w = widen(small[0], sel), widen(small[1], sel), widen(small[2], sel)
        dtw[:, at] = dt_w
        aw[:, at] = a_w
        bw[:, at] = b_w
        scaled = xc * dt_w * b_w
        b_x = scaled.astype(BF)
        bx[:, at] = b_x
        tx[:, at] = (scaled * a_w[T - 1 :, :]).astype(BF)
        a_g = (a_w * gv[:, at].astype(F32)).astype(BF)
        ag[:, at] = a_g
        ds_acc[...] += dot(a_g, b_x, 1, 1)
        thrc[at, :] = sum(dot(sel, p, 0, 0) for p in pieces(thr))
        return z

    lax.fori_loop(0, chunks, prepare, 0)

    h_load.wait()

    @pl.when(jnp.logical_not(needing))
    def _():
        w_load.wait()

    part[...] = jnp.zeros_like(part)

    def project(k, z):
        @pl.when(jnp.logical_and(needing, k >= chunks))
        def _():
            w_forward(k - chunks).wait_recv()

        i = lax.rem(gi * chunks + k, 2 * chunks)
        part[...] += dot(hv[:, w_rows(i)], wh[w_rows(i)], 1, 0)
        return z

    lax.fori_loop(0, 2 * chunks, project, 0)

    p_swap = remote(part, partr, s_ps.at[0], s_pr, (gi, c, f, 1 - h))
    p_swap.start()
    p_tails = [
        remote(
            part.at[T - 8 :], tails.at[h], s_ps.at[1 + o], s_tr.at[h],
            (gi, lax.rem(c + 1, n_ctx), f, lax.rem(h + o, 2)),
        )
        for o in range(2)
    ]

    @pl.when(jnp.logical_not(last_c))
    def _():
        for p in p_tails:
            p.start()

    h_send(0, 1 - f).start()
    p_swap.wait_recv()

    @pl.when(jnp.logical_not(first))
    def _():
        for o in range(2):
            remote(part.at[T - 8 :], tails.at[o], s_ps.at[1], s_tr.at[o], (gi, c, f, 1 - h)).wait_recv()

    taps_b = tapb_ref[...]
    bc = (part[...] + partr[...]).astype(BF).astype(F32)
    tail = (tails[0] + tails[1]).astype(BF).astype(F32)
    be = jnp.concatenate([tail, bc])
    pre_bc = taps_b[3:4, :] * bc
    for d in range(1, 4):
        pre_bc += taps_b[3 - d : 4 - d, :] * pltpu.roll(be, d, 0)[8:] * masks[3 - d]
    sig_bc = jax.nn.sigmoid(pre_bc)
    conv_bc = pre_bc * sig_bc
    silu_bc[...] = sig_bc * (1.0 + pre_bc * (1.0 - sig_bc))
    b_own, c_own = conv_bc[:, :STATE], conv_bc[:, STATE:]
    same_f = same_ref[...] > 0.5
    sm_ref[...] = jnp.where(same_f, dot(c_own, b_own, 1, 1, EXACT), 0.0).astype(BF)
    lastb[...] = (last_ref[...] * b_own).astype(BF)
    alivec[...] = (alive_ref[...] * c_own).astype(BF)
    d_sm = jnp.where(same_f, ds_acc[...], 0.0)
    dps[:, :STATE] = dot(d_sm, c_own, 0, 0, EXACT)
    dps[:, STATE:] = dot(d_sm, b_own, 1, 0, EXACT)

    def f_copy(k):
        return remote(sn.at[chunk(k)], start.at[chunk(k)], s_fs.at[k], s_fr.at[k], (gi, lax.rem(c + 1, n_ctx), f, h))

    def b_copy(k):
        return remote(
            sp.at[chunk(k)], endg.at[chunk(k)], s_bs.at[k], s_br.at[k], (gi, lax.rem(c + n_ctx - 1, n_ctx), f, h)
        )

    def forward(k):
        @pl.when(jnp.logical_not(first))
        def _():
            f_copy(k).wait_recv()

        at = chunk(k)
        e = dot(tx[:, at], lastb[...], 0, 0)
        sn[at, :] = (e + thrc[at, :] * start[at, :].astype(F32)).astype(BF)

        @pl.when(jnp.logical_not(last_c))
        def _():
            f_copy(k).start()

    def backward(k):
        @pl.when(jnp.logical_not(last_c))
        def _():
            b_copy(k).wait_recv()

        at = chunk(k)
        e = dot(ag[:, at], alivec[...], 0, 0)
        sp[at, :] = (e + thrc[at, :] * endg[at, :].astype(F32)).astype(BF)

        @pl.when(jnp.logical_not(first))
        def _():
            b_copy(k).start()

    row_n = lax.broadcasted_iota(jnp.int32, (T, NC), 0)
    row_8 = lax.broadcasted_iota(jnp.int32, (8, NC), 0)

    def transposed_conv(d_pre, taps):
        own = taps[3:4, :] * d_pre
        rim = jnp.zeros((8, NC), F32)
        for d in range(1, 4):
            z = pltpu.roll(taps[3 - d : 4 - d, :] * masks[3 - d] * d_pre, T - d, 0)
            own += jnp.where(row_n < T - d, z, 0.0)
            rim += jnp.where(row_8 < 8 - d, 0.0, z[T - 8 :])
        return own, rim

    def finish(k):
        at = chunk(k)
        taps = tapx_ref[:, at]
        sel = spread(k)
        sm = sm_ref[...]
        a_w, b_w = aw[:, at], bw[:, at]
        gf = gv[:, at].astype(F32)
        b_x, a_g = bx[:, at], ag[:, at]
        st, en = start[at, :], endg[at, :]
        y = dot(sm, b_x, 1, 0) + dot(alivec[...], st, 1, 1)
        r_acc[...] += narrow(a_w * gf * y, sel)
        d_xt = b_w * (dot(sm, a_g, 0, 0) + a_w[T - 1 :, :] * dot(lastb[...], en, 1, 1))
        q_acc[...] += narrow(xf[:, at] * d_xt, sel)
        db_acc[...] += dot(tx[:, at], en, 1, 0)
        dc_acc[...] += dot(a_g, st, 1, 0)
        prod = en.astype(F32) * sn[at, :].astype(F32)
        hi, mid, _ = pieces(prod)
        ones8 = jnp.ones((8, 128), BF)
        l_acc[...] += narrow(dot(ones8, hi, 1, 1) + dot(ones8, mid, 1, 1), sel)
        skip_w = widen(jnp.broadcast_to(skip_ref[...], (8, heads)), sel)[:1]
        d_pre = (dtw[:, at] * d_xt + skip_w * gf) * dsf[:, at]
        own, rim = transposed_conv(d_pre, taps)
        gxs[:, at] = own.astype(BF)
        gxtail[:, at] = own[T - HI :]
        rimx_s[:, at] = rim

    inner = jnp.logical_and(c > 0, c < n_ctx - 1)
    offset = jnp.where(inner, 2, chunks)
    early = c < n_ctx // 2

    def step(k, z):
        @pl.when(k < chunks)
        def _():
            @pl.when(early)
            def _():
                forward(k)

            @pl.when(jnp.logical_not(early))
            def _():
                backward(k)

        @pl.when(jnp.logical_and(k >= offset, k < offset + chunks))
        def _():
            @pl.when(early)
            def _():
                backward(k - offset)

            @pl.when(jnp.logical_not(early))
            def _():
                forward(k - offset)

            finish(k - offset)

        return z

    lax.fori_loop(0, 2 * chunks, step, 0)

    for d in range(1, n_ctx):
        h_send(d, 1 - f).start()

    rimx = remote(rimx_s, rimx_r, s_rim.at[0], s_rim.at[1], (gi, lax.rem(c + n_ctx - 1, n_ctx), f, h))

    alive, last = alive_ref[...], last_ref[...]
    d_bcc = jnp.concatenate([last * db_acc[...], alive * dc_acc[...]], axis=1)
    dps[...] = (dps[...] + d_bcc) * silu_bc[...]
    d_swap = remote(dps, dpsr, s_ds.at[0], s_dr, (gi, c, f, 1 - h))
    d_swap.start()
    d_rims = [
        remote(
            dps.at[:8], rims.at[h], s_ds.at[1 + o], s_rr.at[h],
            (gi, lax.rem(c + n_ctx - 1, n_ctx), f, lax.rem(h + o, 2)),
        )
        for o in range(2)
    ]

    @pl.when(jnp.logical_not(first))
    def _():
        for p in d_rims:
            p.start()
        rimx.start()

    total_q = q_acc[...]
    dts = small[0]
    at_end = row[:, :heads] == T - 1
    d_cum = r_acc[...] - dts * total_q + jnp.where(at_end, l_acc[:1, :], 0.0)
    d_log = dot(tri, d_cum, 0, 0, EXACT)
    ddt_ref[...] = (total_q - decay_ref[...] * d_log) * jax.nn.sigmoid(raw_ref[...])

    d_swap.wait_recv()

    @pl.when(jnp.logical_not(last_c))
    def _():
        for o in range(2):
            remote(dps.at[:8], rims.at[o], s_ds.at[1], s_rr.at[o], (gi, c, f, 1 - h)).wait_recv()

    own, _ = transposed_conv(dps[...] + dpsr[...], taps_b)
    rim_in = rims[0] + rims[1]
    row8 = lax.broadcasted_iota(jnp.int32, (8, 2 * STATE), 0)
    npos = pos0 + T + row8
    nseg = segment(npos)
    rim = jnp.zeros((8, 2 * STATE), F32)
    for d in range(1, 4):
        mask = (segment(npos - d) == nseg).astype(F32)
        z = pltpu.roll(taps_b[3 - d : 4 - d, :] * mask * rim_in, 8 - d, 0)
        rim += jnp.where(row8 < 8 - d, 0.0, z)
    d_bc = jnp.concatenate([own[: T - 8], own[T - 8 :] + rim]).astype(BF)
    dall[me] = d_bc

    half = pl.ds(pl.multiple_of(h * (T // 2), T // 2), T // 2)
    other = pl.ds(pl.multiple_of((1 - h) * (T // 2), T // 2), T // 2)

    def z_copy(d):
        return remote(
            dall.at[me, half], dall.at[me, half], s_zs.at[d], s_zr.at[me], (gi, lax.rem(c + d, n_ctx), f, h)
        )

    def x_copy(cc):
        b = cc * 2 + f
        return remote(dall.at[b, half], dall.at[b, half], s_xs.at[cc], s_xr.at[cc], (gi, c, 1 - f, h))

    def c_copy(b):
        return remote(dall.at[b, half], dall.at[b, half], s_cs.at[b], s_cr.at[b], (gi, c, f, 1 - h))

    def from_z(cc):
        b = cc * 2 + f
        return remote(dall.at[b, half], dall.at[b, half], s_zs.at[0], s_zr.at[b], (gi, c, f, 1 - h))

    def from_x(cc):
        b = cc * 2 + 1 - f
        return remote(dall.at[b, half], dall.at[b, half], s_xs.at[0], s_xr.at[cc], (gi, c, f, 1 - h))

    def from_c(b):
        return remote(dall.at[b, other], dall.at[b, other], s_cs.at[0], s_cr.at[b], (gi, c, f, 1 - h))

    for d in range(1, n_ctx):
        z_copy(d).start()
    x_copy(c).start()

    def grad_u(k, z):
        at = w_rows(k)
        gus[:, at] = dot(dall[me], wh[at], 1, 1).astype(BF)
        return z

    lax.fori_loop(0, 2 * chunks, grad_u, 0)
    u_out = pltpu.make_async_copy(gus, gu_out, s_out.at[0])
    u_out.start()

    for d in range(1, n_ctx):
        cc = lax.rem(c + d, n_ctx)
        from_z(cc).wait_recv()
        x_copy(cc).start()
        c_copy(cc * 2 + f).start()

    @pl.when(jnp.logical_not(last_c))
    def _():
        rimx.wait_recv()

    fixed = gxtail[HI - 8 :, :] + rimx_r[...]
    gxs[T - HI :, :] = jnp.concatenate([gxtail[: HI - 8, :], fixed]).astype(BF)
    x_out = pltpu.make_async_copy(gxs, gx_out, s_out.at[1])
    x_out.start()

    own_load.wait()
    gws[...] = dot(hall[me], dall[me], 0, 0)

    for d in range(n_ctx):
        cc = lax.rem(c + d, n_ctx)
        from_x(cc).wait_recv()
        c_copy(cc * 2 + 1 - f).start()

    def h_wait(b):
        remote(hall.at[b], hall.at[b], s_hs.at[0], s_hr.at[b], (gi, c, f, 1 - h)).wait_recv()

    for d in range(1, n_ctx):
        b = lax.rem(c + d, n_ctx) * 2 + f
        from_c(b).wait_recv()
        h_wait(b)
        gws[...] += dot(hall[b], dall[b], 0, 0)
    for d in range(n_ctx):
        b = lax.rem(c + d, n_ctx) * 2 + 1 - f
        from_c(b).wait_recv()
        h_wait(b)
        gws[...] += dot(hall[b], dall[b], 0, 0)
    w_out = pltpu.make_async_copy(gws, gw_out, s_out.at[2])
    w_out.start()

    @pl.when(jnp.logical_not(needing))
    def _():
        lax.fori_loop(0, chunks, lambda k, z: (w_send(k).wait_send(), z)[1], 0)

    @pl.when(needing)
    def _():
        lax.fori_loop(0, chunks, lambda k, z: (w_forward(k).wait_send(), z)[1], 0)

    @pl.when(jnp.logical_not(last_c))
    def _():
        halo_copy.wait_send()
        for p in p_tails:
            p.wait_send()
        lax.fori_loop(0, chunks, lambda k, z: (f_copy(k).wait_send(), z)[1], 0)

    @pl.when(jnp.logical_not(first))
    def _():
        for p in d_rims:
            p.wait_send()
        rimx.wait_send()
        lax.fori_loop(0, chunks, lambda k, z: (b_copy(k).wait_send(), z)[1], 0)

    p_swap.wait_send()
    d_swap.wait_send()
    for d in range(n_ctx):
        h_send(d, 1 - f).wait_send()
        x_copy(lax.rem(c + d, n_ctx)).wait_send()
        c_copy(lax.rem(c + d, n_ctx) * 2 + 1 - f).wait_send()
        if d:
            h_send(d, f).wait_send()
            z_copy(d).wait_send()
            c_copy(lax.rem(c + d, n_ctx) * 2 + f).wait_send()
    u_out.wait()
    x_out.wait()
    w_out.wait()


def fused(hidden, w, x, g, raw, decay, skip, tapx, tapb, spans):
    T, W = x.shape
    DH = hidden.shape[1]
    n_ctx = lax.axis_size("ctx")
    blocks = 2 * n_ctx
    wb = DH // blocks
    heads = raw.shape[1]
    K = W // NC
    vm, dma = pltpu.VMEM, pltpu.SemaphoreType.DMA
    spec = pl.BlockSpec
    hbm, vmem, smem = spec(memory_space=pl.ANY), spec(memory_space=pltpu.VMEM), spec(memory_space=pltpu.SMEM)
    S2 = 2 * STATE
    return pl.pallas_call(
        fused_kernel,
        out_shape=(
            jax.ShapeDtypeStruct((T, W), BF),
            jax.ShapeDtypeStruct((T, DH), BF),
            jax.ShapeDtypeStruct((T, heads), F32),
            jax.ShapeDtypeStruct((wb, S2), F32),
        ),
        in_specs=[hbm] * 4 + [vmem] * 5 + [smem],
        out_specs=(hbm, hbm, vmem, hbm),
        scratch_shapes=[
            vm((T, W), BF), vm((T, W), BF), vm((T, DH), BF), vm((DH, S2), BF), vm((HI, W), BF),
            vm((T, W), F32), vm((T, W), F32), vm((T, W), F32), vm((T, W), F32), vm((T, W), F32),
            vm((T, W), BF), vm((T, W), BF), vm((T, W), BF), vm((W, STATE), F32),
            vm((W, STATE), BF), vm((W, STATE), BF), vm((W, STATE), BF), vm((W, STATE), BF),
            vm((3, T, S2), F32), vm((T, STATE), F32), vm((T, STATE), F32), vm((T, STATE), F32),
            vm((3, T, heads), F32), vm((T, T), F32), vm((T, S2), F32), vm((T, S2), F32), vm((2, 8, S2), F32),
            vm((T, S2), F32), vm((T, T), BF), vm((T, STATE), BF), vm((T, STATE), BF),
            vm((T, STATE), F32), vm((T, STATE), F32), vm((T, S2), F32), vm((T, S2), F32), vm((2, 8, S2), F32),
            vm((8, W), F32), vm((8, W), F32), vm((HI, W), F32),
            vm((T, heads), F32), vm((T, heads), F32), vm((8, heads), F32),
            vm((blocks, T, wb), BF), vm((blocks, T, S2), BF),
            vm((T, W), BF), vm((T, DH), BF), vm((wb, S2), F32),
            dma((5,)), dma((K,)), dma((K,)), dma((K,)), dma((K,)), dma((blocks,)), dma((blocks,)), dma((2,)),
            dma((K,)), dma((K,)), dma((K,)), dma((K,)),
            dma((3,)), dma, dma((2,)), dma((3,)), dma, dma((2,)), dma((2,)),
            dma((n_ctx,)), dma((blocks,)), dma((n_ctx,)), dma((n_ctx,)), dma((blocks,)), dma((blocks,)), dma((3,)),
        ],
        compiler_params=pltpu.CompilerParams(
            collective_id=0, has_side_effects=True, vmem_limit_bytes=48 << 20
        ),
        cost_estimate=pl.CostEstimate(
            flops=2 * T * 256 * (W * 9 + DH * 4), bytes_accessed=8 << 20, transcendentals=4 * T * W
        ),
    )(hidden, w, x, g, raw, decay, skip, tapx, tapb, spans)


def on_device(
    hidden_in, w_bc, x_in, dt_raw, decay_rate, conv_x, conv_bc, skip_gain, span_len, grad_y
):
    T = x_in.shape[1]
    hidden = hidden_in[0]
    half_width = hidden.shape[1]
    n_ctx, n_fsdp, n_head = (lax.axis_size(a) for a in ("ctx", "fsdp", "head"))
    assert T * 2 == MOST and dt_raw.shape[2] == 32
    x0, g0, raw0 = x_in[0], grad_y[0], dt_raw[0]
    if (lax.axis_size("groups"), n_ctx, n_fsdp, n_head) == (2, 4, 2, 2):
        outs = fused(
            hidden, w_bc, x0, g0, raw0, decay_rate[None, :], skip_gain[None, :], conv_x, conv_bc, span_len
        )
        return tuple(o[None] for o in outs)
    if n_fsdp == n_head:
        route = [(f * n_head + h, h * n_head + f) for f in range(n_fsdp) for h in range(n_head)]
        w_half = lax.ppermute(w_bc, ("fsdp", "head"), route)
    else:
        w_full = lax.all_gather(w_bc, "fsdp", axis=0, tiled=True)
        w_half = lax.dynamic_slice_in_dim(
            w_full, lax.axis_index("head") * half_width, half_width, 0
        )
    raws = [shifted(raw0, "ctx", d) for d in (2, 1)] + [raw0] + [shifted(raw0, "ctx", -d) for d in (1, 2)]
    x1, g1 = shifted(x0, "ctx", 1), shifted(g0, "ctx", -1)
    x2, g2 = shifted(x0, "ctx", 2), shifted(g0, "ctx", -2)

    swap = [(i, (i + 1) % n_head) for i in range(n_head)]
    partial_bc = jnp.dot(hidden, w_half, preferred_element_type=F32)
    bc_pre = (partial_bc + lax.ppermute(partial_bc, "head", swap)).astype(BF)
    bcs = [shifted(bc_pre, "ctx", d) for d in (2, 1)] + [bc_pre] + [shifted(bc_pre, "ctx", -d) for d in (1, 2)]

    n_blocks = n_ctx * n_fsdp
    blocks = hidden.reshape(T, n_blocks, half_width // n_blocks).transpose(1, 0, 2)
    hidden_all = lax.all_to_all(blocks, ("ctx", "fsdp"), 0, 0, tiled=True)

    position = (lax.axis_index("ctx") - 2) * T + jnp.arange(-3, 5 * T, dtype=jnp.int32)
    spans = span_len.shape[1]
    earlier = jnp.arange(spans)[:, None] <= jnp.arange(spans)[None, :]
    span_ends = jnp.sum(jnp.where(earlier, span_len[0][:, None], 0), axis=0)
    counted = jnp.sum((span_ends[None, :] <= position[:, None]).astype(jnp.int32), axis=1)
    segment = jnp.where(position >= 0, counted, -1).astype(F32)
    own_seg = segment[3:]
    by_block = own_seg.reshape(5, T)
    before = jnp.broadcast_to(segment[2 : 2 + 5 * T : T][:, None], (5, T)).reshape(-1)
    last = jnp.broadcast_to(by_block[:, T - 1 :], (5, T)).reshape(-1)
    info = jnp.stack(
        [(segment[k : k + 5 * T] == own_seg).astype(F32) for k in range(3)]
        + [(own_seg == before).astype(F32), (own_seg == last).astype(F32), own_seg],
        axis=1,
    )
    segrow = by_block[2:3]
    raw = jnp.tile(jnp.concatenate(raws), (1, 4))
    decay = jnp.tile(decay_rate, 4)[None, :]
    skip = jnp.repeat(skip_gain, HEAD)[None, :]

    dx, tail, rim, dbc, rimbc, ddt = ssm(
        (x2, x1, x0), (g0, g1, g2), bcs, raw, info, segrow, decay, skip, conv_x, conv_bc
    )
    back = shifted(rim, "ctx", -1)
    grad_x = lax.dynamic_update_slice(dx, (tail + back).astype(BF), (T - 8, 0))

    other = lax.ppermute(dbc, "head", swap)
    rim_same = shifted(rimbc, "ctx", -1)
    cross = [
        (c * n_head + h, (c - 1) * n_head + (h + 1) % n_head)
        for c in range(1, n_ctx)
        for h in range(n_head)
    ]
    rim_cross = lax.ppermute(rimbc, ("ctx", "head"), cross)
    d_bc = ((dbc + other) + jnp.pad(rim_same + rim_cross, ((T - 8, 0), (0, 0)))).astype(BF)
    grad_u = lax.dot_general(
        d_bc, w_half, (((1,), (1,)), ((), ())), preferred_element_type=F32
    ).astype(BF)
    d_all = lax.all_gather(d_bc, ("ctx", "fsdp"), axis=0)
    grad_w = lax.dot_general(
        hidden_all.reshape(n_blocks * T, -1),
        d_all.reshape(n_blocks * T, -1),
        (((0,), (0,)), ((), ())),
        preferred_element_type=F32,
    )
    return (grad_x[None], grad_u[None], ddt[None], grad_w[None])


def solution(mesh):
    return jax.shard_map(
        on_device,
        mesh=mesh,
        in_specs=(
            P(("groups", "fsdp"), "ctx", "head"),
            P("fsdp", None),
            P(("groups", "fsdp"), "ctx", "head"),
            P(("groups", "fsdp"), "ctx", "head"),
            P("head"),
            P(None, "head"),
            P(),
            P("head"),
            P(("groups", "fsdp"), None),
            P(("groups", "fsdp"), "ctx", "head"),
        ),
        out_specs=(
            P(("groups", "fsdp"), "ctx", "head"),
            P(("groups", "fsdp"), "ctx", "head"),
            P(("groups", "fsdp"), "ctx", "head"),
            P(("groups", "head"), ("ctx", "fsdp"), None),
        ),
        check_vma=False,
    )
```

```python
import jax
import jax.numpy as jnp
from jax import lax
from jax.experimental import pallas as pl
from jax.experimental.pallas import tpu as pltpu
from jax.sharding import PartitionSpec as P

STATE = 128
HEAD = 64
MOST = 256
BF = jnp.bfloat16
F32 = jnp.float32
EXACT = lax.Precision.HIGHEST


def shifted(block, axis, distance):
    devices = range(lax.axis_size(axis))
    route = [(i - distance, i) for i in devices if i - distance in devices]
    return lax.ppermute(block, axis, route)


def dot(a, b, ca, cb, precision=None):
    return lax.dot_general(
        a, b, (((ca,), (cb,)), ((), ())), precision=precision, preferred_element_type=F32
    )


def ssm_kernel(
    x2, x1, x0, g0, g1, g2, b2, b1, b0, b3, b4, raw_ref, info_ref, segrow_ref,
    decay_ref, skip_ref, tapx_ref, tapb_ref,
    dx_ref, tail_ref, rim_ref, dbc_ref, rimbc_ref, ddt_ref,
    masks, bias_ref, s_ref, cols_a, cols_b, cum_rows, bprev, cnext, bown, cown,
    silu_bc, d_s, d_b, d_c, acc,
):
    T = x0.shape[0]
    pairs = x0.shape[1] // 128
    lane = lax.broadcasted_iota(jnp.int32, (T, 128), 1)
    row = lax.broadcasted_iota(jnp.int32, (T, 128), 0)
    low = lane < HEAD
    group = lane // 32
    info = info_ref[...]
    for k in range(3):
        masks[k] = jnp.broadcast_to(info[: 3 * T, k : k + 1], (3 * T, 128))

    def col(block, k):
        return info[block * T : (block + 1) * T, k : k + 1]

    tri = (row >= lane).astype(F32)
    decay = decay_ref[...]
    dts, cums, carried, toward = [], [], [], []
    for j in range(5):
        raw = raw_ref[j * T : (j + 1) * T, :]
        dt = jnp.maximum(raw, 0.0) + jnp.log1p(jnp.exp(-jnp.abs(raw)))
        cum = dot(tri, -dt * decay, 1, 0, EXACT)
        dts.append(dt)
        cums.append(cum)
        carried.append(jnp.exp(cum) * col(j, 3))
        toward.append(jnp.exp(cum[T - 1 :, :] - cum) * col(j, 4))
    a1 = dts[1] * toward[1]
    a2 = dts[0] * toward[0] * carried[1][T - 1 :, :]
    c1 = carried[3]
    c2 = carried[4] * carried[3][T - 1 :, :]

    def packed(p, q, r, s):
        return jnp.where(group == 0, p, jnp.where(group == 1, q, jnp.where(group == 2, r, s)))

    cols_a[...] = packed(dts[2], cums[2], carried[2], toward[2])
    cols_b[...] = packed(a2, a1, c1, c2)
    cum_rows[...] = cums[2].T
    same = col(2, 5) == segrow_ref[...]
    bias_ref[...] = jnp.where(same & (row >= lane), 0.0, -1e30)

    taps_b = tapb_ref[...]
    bc = jnp.concatenate([b2[...], b1[...], b0[...], b3[...], b4[...]]).astype(F32)
    pre_bc = taps_b[3:4, :] * bc
    for k in range(3):
        pre_bc += taps_b[k : k + 1, :] * pltpu.roll(bc, 3 - k, 0) * info[:, k : k + 1]
    sig_bc = jax.nn.sigmoid(pre_bc)
    conv_bc = pre_bc * sig_bc
    own_sig = sig_bc[2 * T : 3 * T]
    silu_bc[...] = own_sig * (1.0 + pre_bc[2 * T : 3 * T] * (1.0 - own_sig))
    bprev[...] = conv_bc[: 2 * T, :STATE].astype(BF)
    cnext[...] = conv_bc[3 * T :, STATE:].astype(BF)
    bown[...] = conv_bc[2 * T : 3 * T, :STATE]
    cown[...] = conv_bc[2 * T : 3 * T, STATE:]
    s_ref[...] = dot(cown[...], bown[...], 1, 1, EXACT)
    d_s[...] = jnp.zeros_like(d_s)
    d_b[...] = jnp.zeros_like(d_b)
    d_c[...] = jnp.zeros_like(d_c)
    acc[...] = jnp.zeros_like(acc)

    def pair(i, carry):
        at = pl.ds(pl.multiple_of(i * 128, 128), 128)
        ca = pltpu.roll(cols_a[...], (128 - 2 * i) % 128, 1)
        cb = pltpu.roll(cols_b[...], (128 - 2 * i) % 128, 1)

        def wide(c, q):
            return jnp.where(low, c[:, 32 * q : 32 * q + 1], c[:, 32 * q + 1 : 32 * q + 2])

        def tall(c, q):
            return c[:, 32 * q : 32 * q + 1], c[:, 32 * q + 1 : 32 * q + 2]

        taps = tapx_ref[:, at]
        xe = jnp.concatenate([x2[:, at], x1[:, at], x0[:, at]]).astype(F32)
        pre = taps[3:4, :] * xe
        for k in range(3):
            pre += taps[k : k + 1, :] * pltpu.roll(xe, 3 - k, 0) * masks[k]
        sig = jax.nn.sigmoid(pre)
        xc = pre * sig
        xown = xc[2 * T :]
        sown = sig[2 * T :]
        dsilu = sown * (1.0 + pre[2 * T :] * (1.0 - sown))
        dt_w = wide(ca, 0)
        toward_w = wide(ca, 3)
        xw = jnp.concatenate([xc[:T] * wide(cb, 0), xc[T : 2 * T] * wide(cb, 1)]).astype(BF)
        start = dot(xw, bprev[...], 0, 0)
        gw = jnp.concatenate(
            [g1[:, at].astype(F32) * wide(cb, 2), g2[:, at].astype(F32) * wide(cb, 3)]
        ).astype(BF)
        end_grad = dot(gw, cnext[...], 0, 0)
        start_b = start.astype(BF)
        end_b = end_grad.astype(BF)
        gy = g0[:, at].astype(F32)
        gg = jnp.concatenate([jnp.where(low, gy, 0.0), jnp.where(low, 0.0, gy)]).astype(BF)
        xt = xown * dt_w
        xt_b = xt.astype(BF)
        xx = jnp.concatenate([jnp.where(low, xt, 0.0), jnp.where(low, 0.0, xt)]).astype(BF)
        d_m = dot(gg, xt_b, 1, 1)
        cum_a, cum_b = tall(ca, 1)
        bias = bias_ref[...]
        decay_t = jnp.concatenate(
            [
                jnp.exp(cum_a - cum_rows[pl.ds(2 * i, 1), :] + bias),
                jnp.exp(cum_b - cum_rows[pl.ds(2 * i + 1, 1), :] + bias),
            ]
        )
        s_all = s_ref[...]
        s_two = jnp.concatenate([s_all, s_all])
        ls = decay_t * s_two
        ldm = decay_t * d_m
        d_s[...] += ldm[:T] + ldm[T:]
        d_x = dot(ls.astype(BF), gg, 0, 0)
        car = jnp.concatenate(tall(ca, 2))
        tow = jnp.concatenate(tall(ca, 3))
        c_u = car * dot(gg, start_b, 1, 0)
        d_c[...] += c_u[:T] + c_u[T:]
        c_own = cown[...]
        c_two = jnp.concatenate([c_own, c_own])
        r = jnp.sum(ldm * s_two + c_u * c_two, axis=1, keepdims=True)
        t_v = tow * dot(xx, end_b, 1, 0)
        d_b[...] += t_v[:T] + t_v[T:]
        d_xe = dot(bown[...].astype(BF), end_b, 1, 1) * toward_w
        d_xt = d_x + d_xe
        prod = xown * d_xt
        q_a = jnp.sum(jnp.where(low, prod, 0.0), axis=1, keepdims=True)
        q_b = jnp.sum(jnp.where(low, 0.0, prod), axis=1, keepdims=True)
        ends = jnp.sum(xt * d_xe, axis=0, keepdims=True)
        inner = end_grad * start
        low_row = low[:1]
        through_a, through_b = (v[T - 1 :, :] for v in tall(ca, 2))
        last_a = jnp.sum(jnp.where(low_row, ends, 0.0), axis=1, keepdims=True) + through_a * jnp.sum(
            jnp.sum(inner[:HEAD], axis=0, keepdims=True), axis=1, keepdims=True
        )
        last_b = jnp.sum(jnp.where(low_row, 0.0, ends), axis=1, keepdims=True) + through_b * jnp.sum(
            jnp.sum(inner[HEAD:], axis=0, keepdims=True), axis=1, keepdims=True
        )
        dt_a, dt_b = tall(ca, 0)
        final = row[:, :1] == T - 1
        cum_ga = r[:T] - dt_a * q_a + jnp.where(final, last_a, 0.0)
        cum_gb = r[T:] - dt_b * q_b + jnp.where(final, last_b, 0.0)
        placed = jnp.where(
            lane == 0,
            q_a,
            jnp.where(
                lane == 1, q_b, jnp.where(lane == 32, cum_ga, jnp.where(lane == 33, cum_gb, 0.0))
            ),
        )
        acc[...] += pltpu.roll(placed, 2 * i, 1)
        d_pre = (dt_w * d_xt + skip_ref[:, at] * gy) * dsilu
        own = taps[3:4, :] * d_pre
        rim = jnp.zeros((8, 128), F32)
        for k in range(3):
            d = 3 - k
            z = pltpu.roll(taps[k : k + 1, :] * masks[k, 2 * T :] * d_pre, T - d, 0)
            own += jnp.where(row < T - d, z, 0.0)
            rim += jnp.where(row[T - 8 :] < T - d, 0.0, z[T - 8 :])
        dx_ref[:, at] = own.astype(BF)
        tail_ref[:, at] = own[T - 8 :]
        rim_ref[:, at] = rim
        return carry

    lax.fori_loop(0, pairs, pair, 0)

    ds = d_s[...]
    full_c = d_c[...] + dot(ds, bown[...], 1, 0, EXACT)
    full_b = d_b[...] + dot(ds, cown[...], 0, 0, EXACT)
    d_pre = jnp.concatenate([full_b, full_c], axis=1) * silu_bc[...]
    own = taps_b[3:4, :] * d_pre
    rim = jnp.zeros((8, 2 * STATE), F32)
    row2 = lax.broadcasted_iota(jnp.int32, (T, 2 * STATE), 0)
    for k in range(3):
        d = 3 - k
        z = pltpu.roll(taps_b[k : k + 1, :] * info[2 * T : 3 * T, k : k + 1] * d_pre, T - d, 0)
        own += jnp.where(row2 < T - d, z, 0.0)
        rim += jnp.where(row2[T - 8 :] < T - d, 0.0, z[T - 8 :])
    dbc_ref[...] = own
    rimbc_ref[...] = rim
    total = acc[...]
    d_log = pltpu.roll(dot(tri, total, 0, 0, EXACT), 96, 1)
    raw = raw_ref[2 * T : 3 * T, :]
    ddt_ref[...] = ((total - decay * d_log) * jax.nn.sigmoid(raw))[:, :32]


def ssm(xs, gs, bcs, raw, info, segrow, decay, skip, tapx, tapb):
    T, W = xs[0].shape
    vm = pltpu.VMEM
    return pl.pallas_call(
        ssm_kernel,
        out_shape=(
            jax.ShapeDtypeStruct((T, W), BF),
            jax.ShapeDtypeStruct((8, W), F32),
            jax.ShapeDtypeStruct((8, W), F32),
            jax.ShapeDtypeStruct((T, 2 * STATE), F32),
            jax.ShapeDtypeStruct((8, 2 * STATE), F32),
            jax.ShapeDtypeStruct((T, 32), F32),
        ),
        scratch_shapes=[
            vm((3, 3 * T, 128), F32), vm((T, T), F32), vm((T, T), F32), vm((T, 128), F32),
            vm((T, 128), F32), vm((128, T), F32), vm((2 * T, STATE), BF), vm((2 * T, STATE), BF),
            vm((T, STATE), F32), vm((T, STATE), F32), vm((T, 2 * STATE), F32),
            vm((T, T), F32), vm((T, STATE), F32), vm((T, STATE), F32), vm((T, 128), F32),
        ],
        compiler_params=pltpu.CompilerParams(vmem_limit_bytes=40 << 20),
        cost_estimate=pl.CostEstimate(
            flops=2 * 9 * T * 256 * W, bytes_accessed=8 * T * W * 2, transcendentals=6 * T * W
        ),
    )(*xs, *gs, *bcs, raw, info, segrow, decay, skip, tapx, tapb)


MESH = pl.DeviceIdType.MESH
NC = 256
HI = 16


def pieces(v):
    hi = v.astype(BF)
    rest = v - hi.astype(F32)
    mid = rest.astype(BF)
    lo = (rest - mid.astype(F32)).astype(BF)
    return hi, mid, lo


def fused_kernel(
    hidden, w, x, g, raw_in, decay_in, skip_in, tapx_in, tapb_in, span_in,
    gx_out, gu_out, ddt_out, gw_out,
    raw_ref, decay_ref, skip_ref, tapx_ref, tapb_ref, span_ref, ddt_ref,
    xv, gv, hv, wh, xhalo, xf, dsf, aw, bw, dtw, bx, tx, ag, thrc, start, endg, sn, sp,
    masks, same_ref, alive_ref, last_ref, small, ds_acc, part, partr, tails, silu_bc,
    sm_ref, lastb, alivec, db_acc, dc_acc, dps, dpsr, rims, rimx_s, rimx_r, gxtail, r_acc, q_acc, l_acc,
    hall, dall, gxs, gus, gws,
    s_loc, s_ws, s_wr, s_ys, s_yr, s_hs, s_hr, s_halo, s_fs, s_fr, s_bs, s_br,
    s_ps, s_pr, s_tr, s_ds, s_dr, s_rr, s_rim, s_zs, s_zr, s_xs, s_xr, s_cs, s_cr, s_small, s_out,
):
    T, W = gxs.shape
    gi, c, f, h = (lax.axis_index(a) for a in ("groups", "ctx", "fsdp", "head"))
    n_ctx = lax.axis_size("ctx")
    DH = hv.shape[1]
    chunks = W // NC
    wrows = wh.shape[0] // 2 // chunks
    heads = raw_ref.shape[0]
    wb = hall.shape[2]
    first, last_c = c == 0, c == n_ctx - 1
    needing = h != f
    me = c * 2 + f

    def remote(src, dst, ss, rs, device):
        return pltpu.make_async_remote_copy(
            src_ref=src, dst_ref=dst, send_sem=ss, recv_sem=rs, device_id=device, device_id_type=MESH
        )

    smalls = [
        pltpu.make_async_copy(src, dst, s_small.at[i])
        for i, (src, dst) in enumerate(
            (
                (span_in, span_ref), (raw_in, raw_ref), (decay_in, decay_ref), (skip_in, skip_ref),
                (tapx_in, tapx_ref), (tapb_in, tapb_ref),
            )
        )
    ]
    for copy in smalls:
        copy.start()
    barrier = pltpu.get_barrier_semaphore()
    for o in range(1, 4 * n_ctx):
        oc, of, oh = o // 4, (o // 2) % 2, o % 2
        pl.semaphore_signal(
            barrier, 1, device_id=(gi, lax.rem(c + oc, n_ctx), lax.rem(f + of, 2), lax.rem(h + oh, 2)),
            device_id_type=MESH,
        )
    pl.semaphore_signal(barrier, 1, device_id=(1 - gi, c, f, h), device_id_type=MESH)
    pl.semaphore_wait(barrier, 4 * n_ctx)

    def w_rows(k):
        return pl.ds(pl.multiple_of(k * wrows, wrows), wrows)

    def w_send(k):
        at = w_rows(gi * chunks + k)
        return remote(w.at[at], wh.at[at], s_ws.at[k], s_wr.at[k], (gi, c, 1 - f, h))

    def w_forward(k):
        at = w_rows(gi * chunks + k)
        return remote(wh.at[at], wh.at[at], s_ys.at[k], s_yr.at[k], (1 - gi, c, f, h))

    def h_send(d, ff):
        cc = lax.rem(c + d, n_ctx)
        at = pl.ds(pl.multiple_of((cc * 2 + ff) * wb, wb), wb)
        return remote(
            hidden.at[:, at], hall.at[me], s_hs.at[d + n_ctx * (1 if ff is not f else 0)], s_hr.at[me], (gi, cc, ff, h)
        )

    halo_copy = remote(
        x.at[T - HI :], xhalo, s_halo.at[0], s_halo.at[1], (gi, lax.rem(c + 1, n_ctx), f, h)
    )

    @pl.when(jnp.logical_not(last_c))
    def _():
        halo_copy.start()

    x_load = pltpu.make_async_copy(x, xv, s_loc.at[0])
    g_load = pltpu.make_async_copy(g, gv, s_loc.at[1])
    h_load = pltpu.make_async_copy(hidden, hv, s_loc.at[2])
    w_load = pltpu.make_async_copy(w, wh, s_loc.at[3])
    own_at = pl.ds(pl.multiple_of(me * wb, wb), wb)
    own_load = pltpu.make_async_copy(hidden.at[:, own_at], hall.at[me], s_loc.at[4])
    x_load.start()
    g_load.start()

    @pl.when(jnp.logical_not(needing))
    def _():
        lax.fori_loop(0, chunks, lambda k, z: (w_send(k).start(), z)[1], 0)
        w_load.start()

    for d in range(1, n_ctx):
        h_send(d, f).start()
    h_load.start()
    own_load.start()

    @pl.when(first)
    def _():
        xhalo[...] = jnp.zeros_like(xhalo)
        tails[...] = jnp.zeros_like(tails)
        start[...] = jnp.zeros_like(start)

    @pl.when(last_c)
    def _():
        endg[...] = jnp.zeros_like(endg)
        rims[...] = jnp.zeros_like(rims)
        rimx_r[...] = jnp.zeros_like(rimx_r)

    for copy in smalls:
        copy.wait()
    ends = [span_ref[0, 0]]
    for i in range(1, span_ref.shape[1]):
        ends.append(ends[-1] + span_ref[0, i])

    def segment(pos):
        counted = sum((e <= pos).astype(jnp.int32) for e in ends)
        return jnp.where(pos >= 0, counted, -1)

    pos0 = c * T
    row = lax.broadcasted_iota(jnp.int32, (T, 128), 0)
    lane = lax.broadcasted_iota(jnp.int32, (T, 128), 1)
    seg = segment(pos0 + row)
    for k in range(3):
        m = (segment(pos0 + row - 3 + k) == seg).astype(F32)
        masks[k] = jnp.concatenate([m, m], axis=1)
    same = (seg == segment(pos0 + lane)) & (row >= lane)
    same_ref[...] = same.astype(F32)
    seg_before = segment(jnp.full((T, 128), pos0 - 1, jnp.int32))
    seg_last = segment(jnp.full((T, 128), pos0 + T - 1, jnp.int32))
    alive_ref[...] = (seg == seg_before).astype(F32)
    last_ref[...] = (seg == seg_last).astype(F32)
    through = (seg_last == seg_before).astype(F32)[:heads]

    decay = decay_ref[...]
    raw = raw_ref[...].T
    dt = jnp.maximum(raw, 0.0) + jnp.log1p(jnp.exp(-jnp.abs(raw)))
    tri = (row >= lane).astype(F32)
    cum = dot(tri, -dt * decay, 1, 0, EXACT)
    ea = jnp.exp(cum)
    eb = jnp.exp(-cum)
    small[0] = dt
    small[1] = ea
    small[2] = eb
    small[3] = raw
    eye = (
        lax.broadcasted_iota(jnp.int32, (heads, heads), 0)
        == lax.broadcasted_iota(jnp.int32, (heads, heads), 1)
    ).astype(F32)
    ones = jnp.ones((heads, 128), BF)
    thr = through * sum(dot(p, ones, 1, 0) for p in pieces(eye * ea[T - 1 :, :]))
    ds_acc[...] = jnp.zeros_like(ds_acc)
    r_acc[...] = jnp.zeros_like(r_acc)
    q_acc[...] = jnp.zeros_like(q_acc)
    l_acc[...] = jnp.zeros_like(l_acc)
    db_acc[...] = jnp.zeros_like(db_acc)
    dc_acc[...] = jnp.zeros_like(dc_acc)

    per = NC // HEAD

    def spread(k):
        hr = lax.broadcasted_iota(jnp.int32, (heads, NC), 0)
        cl = lax.broadcasted_iota(jnp.int32, (heads, NC), 1)
        return (hr == k * per + cl // HEAD).astype(F32).astype(BF)

    def widen(v, sel):
        return sum(dot(p, sel, 1, 0) for p in pieces(v))

    def narrow(v, sel):
        hi, mid, _ = pieces(v)
        return dot(hi, sel, 1, 1) + dot(mid, sel, 1, 1)

    def chunk(k):
        return pl.ds(pl.multiple_of(k * NC, NC), NC)

    x_load.wait()
    g_load.wait()

    @pl.when(jnp.logical_not(first))
    def _():
        halo_copy.wait_recv()

    def prepare(k, z):
        @pl.when(needing)
        def _():
            w_send(k).wait_recv()
            w_forward(k).start()

        at = chunk(k)
        taps = tapx_ref[:, at]
        xe = jnp.concatenate([xhalo[:, at], xv[:, at]]).astype(F32)
        pre = taps[3:4, :] * xe[HI:]
        for d in range(1, 4):
            pre += taps[3 - d : 4 - d, :] * pltpu.roll(xe, d, 0)[HI:] * masks[3 - d]
        sig = jax.nn.sigmoid(pre)
        xc = pre * sig
        xf[:, at] = xc
        dsf[:, at] = sig * (1.0 + pre * (1.0 - sig))
        sel = spread(k)
        dt_w, a_w, b_w = widen(small[0], sel), widen(small[1], sel), widen(small[2], sel)
        dtw[:, at] = dt_w
        aw[:, at] = a_w
        bw[:, at] = b_w
        scaled = xc * dt_w * b_w
        b_x = scaled.astype(BF)
        bx[:, at] = b_x
        tx[:, at] = (scaled * a_w[T - 1 :, :]).astype(BF)
        a_g = (a_w * gv[:, at].astype(F32)).astype(BF)
        ag[:, at] = a_g
        ds_acc[...] += dot(a_g, b_x, 1, 1)
        thrc[at, :] = sum(dot(sel, p, 0, 0) for p in pieces(thr))
        return z

    lax.fori_loop(0, chunks, prepare, 0)

    @pl.when(jnp.logical_not(needing))
    def _():
        lax.fori_loop(0, chunks, lambda k, z: (w_send(k).wait_send(), z)[1], 0)

    for d in (*range(1, n_ctx), 0):
        h_send(d, 1 - f).start()

    h_load.wait()

    @pl.when(jnp.logical_not(needing))
    def _():
        w_load.wait()

    part[...] = jnp.zeros_like(part)

    def project(k, z):
        @pl.when(jnp.logical_and(needing, k >= chunks))
        def _():
            w_forward(k - chunks).wait_recv()

        i = lax.rem(gi * chunks + k, 2 * chunks)
        part[...] += dot(hv[:, w_rows(i)], wh[w_rows(i)], 1, 0)
        return z

    lax.fori_loop(0, 2 * chunks, project, 0)

    p_swap = remote(part, partr, s_ps.at[0], s_pr, (gi, c, f, 1 - h))
    p_swap.start()
    p_tails = [
        remote(
            part.at[T - 8 :], tails.at[h], s_ps.at[1 + o], s_tr.at[h],
            (gi, lax.rem(c + 1, n_ctx), f, lax.rem(h + o, 2)),
        )
        for o in range(2)
    ]

    @pl.when(jnp.logical_not(last_c))
    def _():
        for p in p_tails:
            p.start()

    p_swap.wait_recv()

    @pl.when(jnp.logical_not(first))
    def _():
        for o in range(2):
            remote(part.at[T - 8 :], tails.at[o], s_ps.at[1], s_tr.at[o], (gi, c, f, 1 - h)).wait_recv()

    taps_b = tapb_ref[...]
    bc = (part[...] + partr[...]).astype(BF).astype(F32)
    tail = (tails[0] + tails[1]).astype(BF).astype(F32)
    be = jnp.concatenate([tail, bc])
    pre_bc = taps_b[3:4, :] * bc
    for d in range(1, 4):
        pre_bc += taps_b[3 - d : 4 - d, :] * pltpu.roll(be, d, 0)[8:] * masks[3 - d]
    sig_bc = jax.nn.sigmoid(pre_bc)
    conv_bc = pre_bc * sig_bc
    silu_bc[...] = sig_bc * (1.0 + pre_bc * (1.0 - sig_bc))
    b_own, c_own = conv_bc[:, :STATE], conv_bc[:, STATE:]
    same_f = same_ref[...] > 0.5
    sm_ref[...] = jnp.where(same_f, dot(c_own, b_own, 1, 1, EXACT), 0.0).astype(BF)
    lastb[...] = (last_ref[...] * b_own).astype(BF)
    alivec[...] = (alive_ref[...] * c_own).astype(BF)
    d_sm = jnp.where(same_f, ds_acc[...], 0.0)
    dps[:, :STATE] = dot(d_sm, c_own, 0, 0, EXACT)
    dps[:, STATE:] = dot(d_sm, b_own, 1, 0, EXACT)

    def f_copy(k):
        return remote(sn.at[chunk(k)], start.at[chunk(k)], s_fs.at[k], s_fr.at[k], (gi, lax.rem(c + 1, n_ctx), f, h))

    def b_copy(k):
        return remote(
            sp.at[chunk(k)], endg.at[chunk(k)], s_bs.at[k], s_br.at[k], (gi, lax.rem(c + n_ctx - 1, n_ctx), f, h)
        )

    def forward(k):
        @pl.when(jnp.logical_not(first))
        def _():
            f_copy(k).wait_recv()

        at = chunk(k)
        e = dot(tx[:, at], lastb[...], 0, 0)
        sn[at, :] = (e + thrc[at, :] * start[at, :].astype(F32)).astype(BF)

        @pl.when(jnp.logical_not(last_c))
        def _():
            f_copy(k).start()

    def backward(k):
        @pl.when(jnp.logical_not(last_c))
        def _():
            b_copy(k).wait_recv()

        at = chunk(k)
        e = dot(ag[:, at], alivec[...], 0, 0)
        sp[at, :] = (e + thrc[at, :] * endg[at, :].astype(F32)).astype(BF)

        @pl.when(jnp.logical_not(first))
        def _():
            b_copy(k).start()

    row_n = lax.broadcasted_iota(jnp.int32, (T, NC), 0)
    row_8 = lax.broadcasted_iota(jnp.int32, (8, NC), 0)

    def transposed_conv(d_pre, taps):
        own = taps[3:4, :] * d_pre
        rim = jnp.zeros((8, NC), F32)
        for d in range(1, 4):
            z = pltpu.roll(taps[3 - d : 4 - d, :] * masks[3 - d] * d_pre, T - d, 0)
            own += jnp.where(row_n < T - d, z, 0.0)
            rim += jnp.where(row_8 < 8 - d, 0.0, z[T - 8 :])
        return own, rim

    def collect(k):
        at = chunk(k)
        db_acc[...] += dot(tx[:, at], endg[at, :], 1, 0)
        dc_acc[...] += dot(ag[:, at], start[at, :], 1, 0)

    def finish(k):
        at = chunk(k)
        taps = tapx_ref[:, at]
        sel = spread(k)
        sm = sm_ref[...]
        a_w, b_w = aw[:, at], bw[:, at]
        gf = gv[:, at].astype(F32)
        b_x, a_g = bx[:, at], ag[:, at]
        st, en = start[at, :], endg[at, :]
        y = dot(sm, b_x, 1, 0) + dot(alivec[...], st, 1, 1)
        r_acc[...] += narrow(a_w * gf * y, sel)
        d_xt = b_w * (dot(sm, a_g, 0, 0) + a_w[T - 1 :, :] * dot(lastb[...], en, 1, 1))
        q_acc[...] += narrow(xf[:, at] * d_xt, sel)
        prod = en.astype(F32) * sn[at, :].astype(F32)
        hi, mid, _ = pieces(prod)
        ones8 = jnp.ones((8, 128), BF)
        l_acc[...] += narrow(dot(ones8, hi, 1, 1) + dot(ones8, mid, 1, 1), sel)
        skip_w = widen(jnp.broadcast_to(skip_ref[...], (8, heads)), sel)[:1]
        d_pre = (dtw[:, at] * d_xt + skip_w * gf) * dsf[:, at]
        own, rim = transposed_conv(d_pre, taps)
        gxs[:, at] = own.astype(BF)
        gxtail[:, at] = own[T - HI :]
        rimx_s[:, at] = rim

    inner = jnp.logical_and(c > 0, c < n_ctx - 1)
    offset = jnp.where(inner, 2, chunks)
    early = c < n_ctx // 2

    def step(k, z):
        @pl.when(k < chunks)
        def _():
            @pl.when(early)
            def _():
                forward(k)

            @pl.when(jnp.logical_not(early))
            def _():
                backward(k)

        @pl.when(jnp.logical_and(k >= offset, k < offset + chunks))
        def _():
            @pl.when(early)
            def _():
                backward(k - offset)

            @pl.when(jnp.logical_not(early))
            def _():
                forward(k - offset)

            collect(k - offset)

            @pl.when(k > offset)
            def _():
                finish(k - offset - 1)

        return z

    lax.fori_loop(0, 2 * chunks, step, 0)

    rimx = remote(rimx_s, rimx_r, s_rim.at[0], s_rim.at[1], (gi, lax.rem(c + n_ctx - 1, n_ctx), f, h))

    alive, last = alive_ref[...], last_ref[...]
    d_bcc = jnp.concatenate([last * db_acc[...], alive * dc_acc[...]], axis=1)
    dps[...] = (dps[...] + d_bcc) * silu_bc[...]
    d_swap = remote(dps, dpsr, s_ds.at[0], s_dr, (gi, c, f, 1 - h))
    d_swap.start()
    d_rims = [
        remote(
            dps.at[:8], rims.at[h], s_ds.at[1 + o], s_rr.at[h],
            (gi, lax.rem(c + n_ctx - 1, n_ctx), f, lax.rem(h + o, 2)),
        )
        for o in range(2)
    ]

    @pl.when(jnp.logical_not(first))
    def _():
        for p in d_rims:
            p.start()

    finish(chunks - 1)

    @pl.when(jnp.logical_not(first))
    def _():
        rimx.start()

    d_swap.wait_recv()

    @pl.when(jnp.logical_not(last_c))
    def _():
        for o in range(2):
            remote(dps.at[:8], rims.at[o], s_ds.at[1], s_rr.at[o], (gi, c, f, 1 - h)).wait_recv()

    own, _ = transposed_conv(dps[...] + dpsr[...], taps_b)
    rim_in = rims[0] + rims[1]
    row8 = lax.broadcasted_iota(jnp.int32, (8, 2 * STATE), 0)
    npos = pos0 + T + row8
    nseg = segment(npos)
    rim = jnp.zeros((8, 2 * STATE), F32)
    for d in range(1, 4):
        mask = (segment(npos - d) == nseg).astype(F32)
        z = pltpu.roll(taps_b[3 - d : 4 - d, :] * mask * rim_in, 8 - d, 0)
        rim += jnp.where(row8 < 8 - d, 0.0, z)
    d_bc = jnp.concatenate([own[: T - 8], own[T - 8 :] + rim]).astype(BF)
    dall[me] = d_bc

    half = pl.ds(pl.multiple_of(h * (T // 2), T // 2), T // 2)
    other = pl.ds(pl.multiple_of((1 - h) * (T // 2), T // 2), T // 2)

    def z_copy(d):
        return remote(
            dall.at[me, half], dall.at[me, half], s_zs.at[d], s_zr.at[me], (gi, lax.rem(c + d, n_ctx), f, h)
        )

    def x_copy(cc):
        b = cc * 2 + f
        return remote(dall.at[b, half], dall.at[b, half], s_xs.at[cc], s_xr.at[cc], (gi, c, 1 - f, h))

    def c_copy(b):
        return remote(dall.at[b, half], dall.at[b, half], s_cs.at[b], s_cr.at[b], (gi, c, f, 1 - h))

    def from_z(cc):
        b = cc * 2 + f
        return remote(dall.at[b, half], dall.at[b, half], s_zs.at[0], s_zr.at[b], (gi, c, f, 1 - h))

    def from_x(cc):
        b = cc * 2 + 1 - f
        return remote(dall.at[b, half], dall.at[b, half], s_xs.at[0], s_xr.at[cc], (gi, c, f, 1 - h))

    def from_c(b):
        return remote(dall.at[b, other], dall.at[b, other], s_cs.at[0], s_cr.at[b], (gi, c, f, 1 - h))

    for d in range(1, n_ctx):
        z_copy(d).start()
    x_copy(c).start()

    total_q = q_acc[...]
    dts = small[0]
    at_end = row[:, :heads] == T - 1
    d_cum = r_acc[...] - dts * total_q + jnp.where(at_end, l_acc[:1, :], 0.0)
    d_log = dot(tri, d_cum, 0, 0, EXACT)
    ddt_ref[...] = ((total_q - decay_ref[...] * d_log) * jax.nn.sigmoid(small[3])).T
    t_out = pltpu.make_async_copy(ddt_ref, ddt_out, s_out.at[3])
    t_out.start()

    def grad_u(k, z):
        at = w_rows(k)
        gus[:, at] = dot(dall[me], wh[at], 1, 1).astype(BF)
        return z

    lax.fori_loop(0, 2 * chunks, grad_u, 0)
    u_out = pltpu.make_async_copy(gus, gu_out, s_out.at[0])
    u_out.start()

    for d in range(1, n_ctx):
        cc = lax.rem(c + d, n_ctx)
        from_z(cc).wait_recv()
        x_copy(cc).start()
        c_copy(cc * 2 + f).start()

    @pl.when(jnp.logical_not(last_c))
    def _():
        rimx.wait_recv()

    fixed = gxtail[HI - 8 :, :] + rimx_r[...]
    gxs[T - HI :, :] = jnp.concatenate([gxtail[: HI - 8, :], fixed]).astype(BF)
    x_out = pltpu.make_async_copy(gxs, gx_out, s_out.at[1])
    x_out.start()

    for d in range(n_ctx):
        cc = lax.rem(c + d, n_ctx)
        from_x(cc).wait_recv()
        c_copy(cc * 2 + 1 - f).start()

    def h_wait(b):
        remote(hall.at[b], hall.at[b], s_hs.at[0], s_hr.at[b], (gi, c, f, 1 - h)).wait_recv()

    own_load.wait()
    for d in range(1, n_ctx):
        b = lax.rem(c + d, n_ctx) * 2 + f
        from_c(b).wait_recv()
        h_wait(b)
    for d in range(n_ctx):
        b = lax.rem(c + d, n_ctx) * 2 + 1 - f
        from_c(b).wait_recv()
        h_wait(b)
    gws[...] = dot(
        hall[...].reshape(2 * n_ctx * T, wb), dall[...].reshape(2 * n_ctx * T, 2 * STATE), 0, 0
    )
    w_out = pltpu.make_async_copy(gws, gw_out, s_out.at[2])
    w_out.start()

    @pl.when(needing)
    def _():
        lax.fori_loop(0, chunks, lambda k, z: (w_forward(k).wait_send(), z)[1], 0)

    @pl.when(jnp.logical_not(last_c))
    def _():
        halo_copy.wait_send()
        for p in p_tails:
            p.wait_send()
        lax.fori_loop(0, chunks, lambda k, z: (f_copy(k).wait_send(), z)[1], 0)

    @pl.when(jnp.logical_not(first))
    def _():
        for p in d_rims:
            p.wait_send()
        rimx.wait_send()
        lax.fori_loop(0, chunks, lambda k, z: (b_copy(k).wait_send(), z)[1], 0)

    p_swap.wait_send()
    d_swap.wait_send()
    for d in range(n_ctx):
        h_send(d, 1 - f).wait_send()
        x_copy(lax.rem(c + d, n_ctx)).wait_send()
        c_copy(lax.rem(c + d, n_ctx) * 2 + 1 - f).wait_send()
        if d:
            h_send(d, f).wait_send()
            z_copy(d).wait_send()
            c_copy(lax.rem(c + d, n_ctx) * 2 + f).wait_send()
    u_out.wait()
    x_out.wait()
    w_out.wait()
    t_out.wait()


def fused(hidden, w, x, g, raw, decay, skip, tapx, tapb, spans):
    T, W = x.shape
    DH = hidden.shape[1]
    n_ctx = lax.axis_size("ctx")
    blocks = 2 * n_ctx
    wb = DH // blocks
    heads = raw.shape[0]
    K = W // NC
    vm, dma = pltpu.VMEM, pltpu.SemaphoreType.DMA
    spec = pl.BlockSpec
    hbm = spec(memory_space=pltpu.HBM)
    out = spec(memory_space=pl.ANY)
    S2 = 2 * STATE
    return pl.pallas_call(
        fused_kernel,
        out_shape=(
            jax.ShapeDtypeStruct((T, W), BF),
            jax.ShapeDtypeStruct((T, DH), BF),
            jax.ShapeDtypeStruct((heads, T), F32),
            jax.ShapeDtypeStruct((wb, S2), F32),
        ),
        in_specs=[hbm] * 10,
        out_specs=(out,) * 4,
        scratch_shapes=[
            vm((heads, T), F32), vm((1, heads), F32), vm((1, heads), F32), vm((4, W), F32), vm((4, S2), F32),
            pltpu.SMEM(spans.shape, jnp.int32), vm((heads, T), F32),
            vm((T, W), BF), vm((T, W), BF), vm((T, DH), BF), vm((DH, S2), BF), vm((HI, W), BF),
            vm((T, W), F32), vm((T, W), F32), vm((T, W), F32), vm((T, W), F32), vm((T, W), F32),
            vm((T, W), BF), vm((T, W), BF), vm((T, W), BF), vm((W, STATE), F32),
            vm((W, STATE), BF), vm((W, STATE), BF), vm((W, STATE), BF), vm((W, STATE), BF),
            vm((3, T, S2), F32), vm((T, STATE), F32), vm((T, STATE), F32), vm((T, STATE), F32),
            vm((4, T, heads), F32), vm((T, T), F32), vm((T, S2), F32), vm((T, S2), F32), vm((2, 8, S2), F32),
            vm((T, S2), F32), vm((T, T), BF), vm((T, STATE), BF), vm((T, STATE), BF),
            vm((T, STATE), F32), vm((T, STATE), F32), vm((T, S2), F32), vm((T, S2), F32), vm((2, 8, S2), F32),
            vm((8, W), F32), vm((8, W), F32), vm((HI, W), F32),
            vm((T, heads), F32), vm((T, heads), F32), vm((8, heads), F32),
            vm((blocks, T, wb), BF), vm((blocks, T, S2), BF),
            vm((T, W), BF), vm((T, DH), BF), vm((wb, S2), F32),
            dma((5,)), dma((K,)), dma((K,)), dma((K,)), dma((K,)), dma((blocks,)), dma((blocks,)), dma((2,)),
            dma((K,)), dma((K,)), dma((K,)), dma((K,)),
            dma((3,)), dma, dma((2,)), dma((3,)), dma, dma((2,)), dma((2,)),
            dma((n_ctx,)), dma((blocks,)), dma((n_ctx,)), dma((n_ctx,)), dma((blocks,)), dma((blocks,)), dma((6,)), dma((4,)),
        ],
        compiler_params=pltpu.CompilerParams(
            collective_id=0, has_side_effects=True, vmem_limit_bytes=60 << 20
        ),
        cost_estimate=pl.CostEstimate(
            flops=2 * T * 256 * (W * 9 + DH * 4), bytes_accessed=8 << 20, transcendentals=4 * T * W
        ),
    )(hidden, w, x, g, raw, decay, skip, tapx, tapb, spans)


def publish_kernel(*refs):
    n = (len(refs) - 2) // 3
    ins, outs, held, in_sem, out_sem = refs[:n], refs[n : 2 * n], refs[2 * n : 3 * n], refs[-2], refs[-1]
    loads = [pltpu.make_async_copy(ins[i], held[i], in_sem.at[i]) for i in range(n)]
    stores = [pltpu.make_async_copy(held[i], outs[i], out_sem.at[i]) for i in range(n)]
    for copy in loads:
        copy.start()
    for load, store in zip(loads, stores):
        load.wait()
        store.start()
    for copy in stores:
        copy.wait()


def publish(arrays):
    n = len(arrays)
    hbm = pl.BlockSpec(memory_space=pl.ANY)
    return pl.pallas_call(
        publish_kernel,
        out_shape=tuple(jax.ShapeDtypeStruct(a.shape, a.dtype) for a in arrays),
        in_specs=[hbm] * n,
        out_specs=(hbm,) * n,
        scratch_shapes=[pltpu.VMEM(a.shape, a.dtype) for a in arrays]
        + [pltpu.SemaphoreType.DMA((n,)), pltpu.SemaphoreType.DMA((n,))],
        compiler_params=pltpu.CompilerParams(vmem_limit_bytes=60 << 20),
    )(*arrays)


def on_device(
    hidden_in, w_bc, x_in, dt_raw, decay_rate, conv_x, conv_bc, skip_gain, span_len, grad_y
):
    T = x_in.shape[1]
    hidden = hidden_in[0]
    half_width = hidden.shape[1]
    n_ctx, n_fsdp, n_head = (lax.axis_size(a) for a in ("ctx", "fsdp", "head"))
    assert T * 2 == MOST and dt_raw.shape[2] == 32
    x0, g0, raw0 = x_in[0], grad_y[0], dt_raw[0]
    if (lax.axis_size("groups"), n_ctx, n_fsdp, n_head) == (2, 4, 2, 2):
        outs = fused(
            hidden, w_bc, x0, g0, raw0.T, decay_rate[None, :], skip_gain[None, :], conv_x, conv_bc, span_len
        )
        outs = publish(outs)
        return (outs[0][None], outs[1][None], outs[2].T[None], outs[3][None])
    if n_fsdp == n_head:
        route = [(f * n_head + h, h * n_head + f) for f in range(n_fsdp) for h in range(n_head)]
        w_half = lax.ppermute(w_bc, ("fsdp", "head"), route)
    else:
        w_full = lax.all_gather(w_bc, "fsdp", axis=0, tiled=True)
        w_half = lax.dynamic_slice_in_dim(
            w_full, lax.axis_index("head") * half_width, half_width, 0
        )
    raws = [shifted(raw0, "ctx", d) for d in (2, 1)] + [raw0] + [shifted(raw0, "ctx", -d) for d in (1, 2)]
    x1, g1 = shifted(x0, "ctx", 1), shifted(g0, "ctx", -1)
    x2, g2 = shifted(x0, "ctx", 2), shifted(g0, "ctx", -2)

    swap = [(i, (i + 1) % n_head) for i in range(n_head)]
    partial_bc = jnp.dot(hidden, w_half, preferred_element_type=F32)
    bc_pre = (partial_bc + lax.ppermute(partial_bc, "head", swap)).astype(BF)
    bcs = [shifted(bc_pre, "ctx", d) for d in (2, 1)] + [bc_pre] + [shifted(bc_pre, "ctx", -d) for d in (1, 2)]

    n_blocks = n_ctx * n_fsdp
    blocks = hidden.reshape(T, n_blocks, half_width // n_blocks).transpose(1, 0, 2)
    hidden_all = lax.all_to_all(blocks, ("ctx", "fsdp"), 0, 0, tiled=True)

    position = (lax.axis_index("ctx") - 2) * T + jnp.arange(-3, 5 * T, dtype=jnp.int32)
    spans = span_len.shape[1]
    earlier = jnp.arange(spans)[:, None] <= jnp.arange(spans)[None, :]
    span_ends = jnp.sum(jnp.where(earlier, span_len[0][:, None], 0), axis=0)
    counted = jnp.sum((span_ends[None, :] <= position[:, None]).astype(jnp.int32), axis=1)
    segment = jnp.where(position >= 0, counted, -1).astype(F32)
    own_seg = segment[3:]
    by_block = own_seg.reshape(5, T)
    before = jnp.broadcast_to(segment[2 : 2 + 5 * T : T][:, None], (5, T)).reshape(-1)
    last = jnp.broadcast_to(by_block[:, T - 1 :], (5, T)).reshape(-1)
    info = jnp.stack(
        [(segment[k : k + 5 * T] == own_seg).astype(F32) for k in range(3)]
        + [(own_seg == before).astype(F32), (own_seg == last).astype(F32), own_seg],
        axis=1,
    )
    segrow = by_block[2:3]
    raw = jnp.tile(jnp.concatenate(raws), (1, 4))
    decay = jnp.tile(decay_rate, 4)[None, :]
    skip = jnp.repeat(skip_gain, HEAD)[None, :]

    dx, tail, rim, dbc, rimbc, ddt = ssm(
        (x2, x1, x0), (g0, g1, g2), bcs, raw, info, segrow, decay, skip, conv_x, conv_bc
    )
    back = shifted(rim, "ctx", -1)
    grad_x = lax.dynamic_update_slice(dx, (tail + back).astype(BF), (T - 8, 0))

    other = lax.ppermute(dbc, "head", swap)
    rim_same = shifted(rimbc, "ctx", -1)
    cross = [
        (c * n_head + h, (c - 1) * n_head + (h + 1) % n_head)
        for c in range(1, n_ctx)
        for h in range(n_head)
    ]
    rim_cross = lax.ppermute(rimbc, ("ctx", "head"), cross)
    d_bc = ((dbc + other) + jnp.pad(rim_same + rim_cross, ((T - 8, 0), (0, 0)))).astype(BF)
    grad_u = lax.dot_general(
        d_bc, w_half, (((1,), (1,)), ((), ())), preferred_element_type=F32
    ).astype(BF)
    d_all = lax.all_gather(d_bc, ("ctx", "fsdp"), axis=0)
    grad_w = lax.dot_general(
        hidden_all.reshape(n_blocks * T, -1),
        d_all.reshape(n_blocks * T, -1),
        (((0,), (0,)), ((), ())),
        preferred_element_type=F32,
    )
    return (grad_x[None], grad_u[None], ddt[None], grad_w[None])


def solution(mesh):
    return jax.shard_map(
        on_device,
        mesh=mesh,
        in_specs=(
            P(("groups", "fsdp"), "ctx", "head"),
            P("fsdp", None),
            P(("groups", "fsdp"), "ctx", "head"),
            P(("groups", "fsdp"), "ctx", "head"),
            P("head"),
            P(None, "head"),
            P(),
            P("head"),
            P(("groups", "fsdp"), None),
            P(("groups", "fsdp"), "ctx", "head"),
        ),
        out_specs=(
            P(("groups", "fsdp"), "ctx", "head"),
            P(("groups", "fsdp"), "ctx", "head"),
            P(("groups", "fsdp"), "ctx", "head"),
            P(("groups", "head"), ("ctx", "fsdp"), None),
        ),
        check_vma=False,
    )
```

```python
import jax
import jax.numpy as jnp
from jax import lax
from jax.experimental import pallas as pl
from jax.experimental.pallas import tpu as pltpu
from jax.sharding import PartitionSpec as P

STATE = 128
HEAD = 64
MOST = 256
BF = jnp.bfloat16
F32 = jnp.float32
EXACT = lax.Precision.HIGHEST


def shifted(block, axis, distance):
    devices = range(lax.axis_size(axis))
    route = [(i - distance, i) for i in devices if i - distance in devices]
    return lax.ppermute(block, axis, route)


def dot(a, b, ca, cb, precision=None):
    return lax.dot_general(
        a, b, (((ca,), (cb,)), ((), ())), precision=precision, preferred_element_type=F32
    )


def ssm_kernel(
    x2, x1, x0, g0, g1, g2, b2, b1, b0, b3, b4, raw_ref, info_ref, segrow_ref,
    decay_ref, skip_ref, tapx_ref, tapb_ref,
    dx_ref, tail_ref, rim_ref, dbc_ref, rimbc_ref, ddt_ref,
    masks, bias_ref, s_ref, cols_a, cols_b, cum_rows, bprev, cnext, bown, cown,
    silu_bc, d_s, d_b, d_c, acc,
):
    T = x0.shape[0]
    pairs = x0.shape[1] // 128
    lane = lax.broadcasted_iota(jnp.int32, (T, 128), 1)
    row = lax.broadcasted_iota(jnp.int32, (T, 128), 0)
    low = lane < HEAD
    group = lane // 32
    info = info_ref[...]
    for k in range(3):
        masks[k] = jnp.broadcast_to(info[: 3 * T, k : k + 1], (3 * T, 128))

    def col(block, k):
        return info[block * T : (block + 1) * T, k : k + 1]

    tri = (row >= lane).astype(F32)
    decay = decay_ref[...]
    dts, cums, carried, toward = [], [], [], []
    for j in range(5):
        raw = raw_ref[j * T : (j + 1) * T, :]
        dt = jnp.maximum(raw, 0.0) + jnp.log1p(jnp.exp(-jnp.abs(raw)))
        cum = dot(tri, -dt * decay, 1, 0, EXACT)
        dts.append(dt)
        cums.append(cum)
        carried.append(jnp.exp(cum) * col(j, 3))
        toward.append(jnp.exp(cum[T - 1 :, :] - cum) * col(j, 4))
    a1 = dts[1] * toward[1]
    a2 = dts[0] * toward[0] * carried[1][T - 1 :, :]
    c1 = carried[3]
    c2 = carried[4] * carried[3][T - 1 :, :]

    def packed(p, q, r, s):
        return jnp.where(group == 0, p, jnp.where(group == 1, q, jnp.where(group == 2, r, s)))

    cols_a[...] = packed(dts[2], cums[2], carried[2], toward[2])
    cols_b[...] = packed(a2, a1, c1, c2)
    cum_rows[...] = cums[2].T
    same = col(2, 5) == segrow_ref[...]
    bias_ref[...] = jnp.where(same & (row >= lane), 0.0, -1e30)

    taps_b = tapb_ref[...]
    bc = jnp.concatenate([b2[...], b1[...], b0[...], b3[...], b4[...]]).astype(F32)
    pre_bc = taps_b[3:4, :] * bc
    for k in range(3):
        pre_bc += taps_b[k : k + 1, :] * pltpu.roll(bc, 3 - k, 0) * info[:, k : k + 1]
    sig_bc = jax.nn.sigmoid(pre_bc)
    conv_bc = pre_bc * sig_bc
    own_sig = sig_bc[2 * T : 3 * T]
    silu_bc[...] = own_sig * (1.0 + pre_bc[2 * T : 3 * T] * (1.0 - own_sig))
    bprev[...] = conv_bc[: 2 * T, :STATE].astype(BF)
    cnext[...] = conv_bc[3 * T :, STATE:].astype(BF)
    bown[...] = conv_bc[2 * T : 3 * T, :STATE]
    cown[...] = conv_bc[2 * T : 3 * T, STATE:]
    s_ref[...] = dot(cown[...], bown[...], 1, 1, EXACT)
    d_s[...] = jnp.zeros_like(d_s)
    d_b[...] = jnp.zeros_like(d_b)
    d_c[...] = jnp.zeros_like(d_c)
    acc[...] = jnp.zeros_like(acc)

    def pair(i, carry):
        at = pl.ds(pl.multiple_of(i * 128, 128), 128)
        ca = pltpu.roll(cols_a[...], (128 - 2 * i) % 128, 1)
        cb = pltpu.roll(cols_b[...], (128 - 2 * i) % 128, 1)

        def wide(c, q):
            return jnp.where(low, c[:, 32 * q : 32 * q + 1], c[:, 32 * q + 1 : 32 * q + 2])

        def tall(c, q):
            return c[:, 32 * q : 32 * q + 1], c[:, 32 * q + 1 : 32 * q + 2]

        taps = tapx_ref[:, at]
        xe = jnp.concatenate([x2[:, at], x1[:, at], x0[:, at]]).astype(F32)
        pre = taps[3:4, :] * xe
        for k in range(3):
            pre += taps[k : k + 1, :] * pltpu.roll(xe, 3 - k, 0) * masks[k]
        sig = jax.nn.sigmoid(pre)
        xc = pre * sig
        xown = xc[2 * T :]
        sown = sig[2 * T :]
        dsilu = sown * (1.0 + pre[2 * T :] * (1.0 - sown))
        dt_w = wide(ca, 0)
        toward_w = wide(ca, 3)
        xw = jnp.concatenate([xc[:T] * wide(cb, 0), xc[T : 2 * T] * wide(cb, 1)]).astype(BF)
        start = dot(xw, bprev[...], 0, 0)
        gw = jnp.concatenate(
            [g1[:, at].astype(F32) * wide(cb, 2), g2[:, at].astype(F32) * wide(cb, 3)]
        ).astype(BF)
        end_grad = dot(gw, cnext[...], 0, 0)
        start_b = start.astype(BF)
        end_b = end_grad.astype(BF)
        gy = g0[:, at].astype(F32)
        gg = jnp.concatenate([jnp.where(low, gy, 0.0), jnp.where(low, 0.0, gy)]).astype(BF)
        xt = xown * dt_w
        xt_b = xt.astype(BF)
        xx = jnp.concatenate([jnp.where(low, xt, 0.0), jnp.where(low, 0.0, xt)]).astype(BF)
        d_m = dot(gg, xt_b, 1, 1)
        cum_a, cum_b = tall(ca, 1)
        bias = bias_ref[...]
        decay_t = jnp.concatenate(
            [
                jnp.exp(cum_a - cum_rows[pl.ds(2 * i, 1), :] + bias),
                jnp.exp(cum_b - cum_rows[pl.ds(2 * i + 1, 1), :] + bias),
            ]
        )
        s_all = s_ref[...]
        s_two = jnp.concatenate([s_all, s_all])
        ls = decay_t * s_two
        ldm = decay_t * d_m
        d_s[...] += ldm[:T] + ldm[T:]
        d_x = dot(ls.astype(BF), gg, 0, 0)
        car = jnp.concatenate(tall(ca, 2))
        tow = jnp.concatenate(tall(ca, 3))
        c_u = car * dot(gg, start_b, 1, 0)
        d_c[...] += c_u[:T] + c_u[T:]
        c_own = cown[...]
        c_two = jnp.concatenate([c_own, c_own])
        r = jnp.sum(ldm * s_two + c_u * c_two, axis=1, keepdims=True)
        t_v = tow * dot(xx, end_b, 1, 0)
        d_b[...] += t_v[:T] + t_v[T:]
        d_xe = dot(bown[...].astype(BF), end_b, 1, 1) * toward_w
        d_xt = d_x + d_xe
        prod = xown * d_xt
        q_a = jnp.sum(jnp.where(low, prod, 0.0), axis=1, keepdims=True)
        q_b = jnp.sum(jnp.where(low, 0.0, prod), axis=1, keepdims=True)
        ends = jnp.sum(xt * d_xe, axis=0, keepdims=True)
        inner = end_grad * start
        low_row = low[:1]
        through_a, through_b = (v[T - 1 :, :] for v in tall(ca, 2))
        last_a = jnp.sum(jnp.where(low_row, ends, 0.0), axis=1, keepdims=True) + through_a * jnp.sum(
            jnp.sum(inner[:HEAD], axis=0, keepdims=True), axis=1, keepdims=True
        )
        last_b = jnp.sum(jnp.where(low_row, 0.0, ends), axis=1, keepdims=True) + through_b * jnp.sum(
            jnp.sum(inner[HEAD:], axis=0, keepdims=True), axis=1, keepdims=True
        )
        dt_a, dt_b = tall(ca, 0)
        final = row[:, :1] == T - 1
        cum_ga = r[:T] - dt_a * q_a + jnp.where(final, last_a, 0.0)
        cum_gb = r[T:] - dt_b * q_b + jnp.where(final, last_b, 0.0)
        placed = jnp.where(
            lane == 0,
            q_a,
            jnp.where(
                lane == 1, q_b, jnp.where(lane == 32, cum_ga, jnp.where(lane == 33, cum_gb, 0.0))
            ),
        )
        acc[...] += pltpu.roll(placed, 2 * i, 1)
        d_pre = (dt_w * d_xt + skip_ref[:, at] * gy) * dsilu
        own = taps[3:4, :] * d_pre
        rim = jnp.zeros((8, 128), F32)
        for k in range(3):
            d = 3 - k
            z = pltpu.roll(taps[k : k + 1, :] * masks[k, 2 * T :] * d_pre, T - d, 0)
            own += jnp.where(row < T - d, z, 0.0)
            rim += jnp.where(row[T - 8 :] < T - d, 0.0, z[T - 8 :])
        dx_ref[:, at] = own.astype(BF)
        tail_ref[:, at] = own[T - 8 :]
        rim_ref[:, at] = rim
        return carry

    lax.fori_loop(0, pairs, pair, 0)

    ds = d_s[...]
    full_c = d_c[...] + dot(ds, bown[...], 1, 0, EXACT)
    full_b = d_b[...] + dot(ds, cown[...], 0, 0, EXACT)
    d_pre = jnp.concatenate([full_b, full_c], axis=1) * silu_bc[...]
    own = taps_b[3:4, :] * d_pre
    rim = jnp.zeros((8, 2 * STATE), F32)
    row2 = lax.broadcasted_iota(jnp.int32, (T, 2 * STATE), 0)
    for k in range(3):
        d = 3 - k
        z = pltpu.roll(taps_b[k : k + 1, :] * info[2 * T : 3 * T, k : k + 1] * d_pre, T - d, 0)
        own += jnp.where(row2 < T - d, z, 0.0)
        rim += jnp.where(row2[T - 8 :] < T - d, 0.0, z[T - 8 :])
    dbc_ref[...] = own
    rimbc_ref[...] = rim
    total = acc[...]
    d_log = pltpu.roll(dot(tri, total, 0, 0, EXACT), 96, 1)
    raw = raw_ref[2 * T : 3 * T, :]
    ddt_ref[...] = ((total - decay * d_log) * jax.nn.sigmoid(raw))[:, :32]


def ssm(xs, gs, bcs, raw, info, segrow, decay, skip, tapx, tapb):
    T, W = xs[0].shape
    vm = pltpu.VMEM
    return pl.pallas_call(
        ssm_kernel,
        out_shape=(
            jax.ShapeDtypeStruct((T, W), BF),
            jax.ShapeDtypeStruct((8, W), F32),
            jax.ShapeDtypeStruct((8, W), F32),
            jax.ShapeDtypeStruct((T, 2 * STATE), F32),
            jax.ShapeDtypeStruct((8, 2 * STATE), F32),
            jax.ShapeDtypeStruct((T, 32), F32),
        ),
        scratch_shapes=[
            vm((3, 3 * T, 128), F32), vm((T, T), F32), vm((T, T), F32), vm((T, 128), F32),
            vm((T, 128), F32), vm((128, T), F32), vm((2 * T, STATE), BF), vm((2 * T, STATE), BF),
            vm((T, STATE), F32), vm((T, STATE), F32), vm((T, 2 * STATE), F32),
            vm((T, T), F32), vm((T, STATE), F32), vm((T, STATE), F32), vm((T, 128), F32),
        ],
        compiler_params=pltpu.CompilerParams(vmem_limit_bytes=40 << 20),
        cost_estimate=pl.CostEstimate(
            flops=2 * 9 * T * 256 * W, bytes_accessed=8 * T * W * 2, transcendentals=6 * T * W
        ),
    )(*xs, *gs, *bcs, raw, info, segrow, decay, skip, tapx, tapb)


MESH = pl.DeviceIdType.MESH
NC = 256
HI = 16
CH = 256
LAG = 3
YLAG = 3
PUB = 4


def pieces(v):
    hi = v.astype(BF)
    rest = v - hi.astype(F32)
    mid = rest.astype(BF)
    lo = (rest - mid.astype(F32)).astype(BF)
    return hi, mid, lo


def fused_kernel(
    hidden, w, x, g, raw_in, decay_in, skip_in, tapx_in, tapb_in, span_in,
    gx_out, gu_out, ddt_out, gw_out,
    raw_ref, decay_ref, skip_ref, tapx_ref, tapb_ref, span_ref, ddt_ref,
    xv, gv, hv, wh, xhalo, xf, dsf, aw, bw, dtw, bx, tx, ag, thrc, start, endg, sn, sp,
    masks, same_ref, alive_ref, last_ref, small, ds_acc, part, partr, tails, silu_bc,
    sm_ref, lastb, alivec, db_acc, dc_acc, dps, dpsr, rims, rimx_s, rimx_r, gxtail, r_acc, q_acc, l_acc,
    hall, dall, gxs, gus, gws,
    s_loc, s_ws, s_wr, s_ys, s_yr, s_hs, s_hr, s_halo, s_fs, s_fr, s_bs, s_br,
    s_ps, s_pr, s_tr, s_ds, s_dr, s_rr, s_rim, s_zs, s_zr, s_xs, s_xr, s_cs, s_cr, s_small, s_out,
):
    T, W = gxs.shape
    gi, c, f, h = (lax.axis_index(a) for a in ("groups", "ctx", "fsdp", "head"))
    n_ctx = lax.axis_size("ctx")
    DH = hv.shape[1]
    chunks = W // NC
    wrows = wh.shape[0] // 2 // chunks
    heads = raw_ref.shape[0]
    wb = hall.shape[2]
    first, last_c = c == 0, c == n_ctx - 1
    needing = h != f
    me = c * 2 + f

    def remote(src, dst, ss, rs, device):
        return pltpu.make_async_remote_copy(
            src_ref=src, dst_ref=dst, send_sem=ss, recv_sem=rs, device_id=device, device_id_type=MESH
        )

    smalls = [
        pltpu.make_async_copy(src, dst, s_small.at[i])
        for i, (src, dst) in enumerate(
            (
                (span_in, span_ref), (raw_in, raw_ref), (decay_in, decay_ref), (skip_in, skip_ref),
                (tapx_in, tapx_ref), (tapb_in, tapb_ref),
            )
        )
    ]
    for copy in smalls:
        copy.start()
    barrier = pltpu.get_barrier_semaphore()
    for o in range(1, 4 * n_ctx):
        oc, of, oh = o // 4, (o // 2) % 2, o % 2
        pl.semaphore_signal(
            barrier, 1, device_id=(gi, lax.rem(c + oc, n_ctx), lax.rem(f + of, 2), lax.rem(h + oh, 2)),
            device_id_type=MESH,
        )
    pl.semaphore_signal(barrier, 1, device_id=(1 - gi, c, f, h), device_id_type=MESH)
    pl.semaphore_wait(barrier, 4 * n_ctx)

    def w_rows(k):
        return pl.ds(pl.multiple_of(k * wrows, wrows), wrows)

    def w_rows(k):
        return pl.ds(pl.multiple_of(k * wrows, wrows), wrows)

    def w_send(k):
        at = w_rows(gi * chunks + k)
        return remote(w.at[at], wh.at[at], s_ws.at[k], s_wr.at[k], (gi, c, 1 - f, h))

    def w_forward(k):
        at = w_rows(gi * chunks + k)
        return remote(wh.at[at], wh.at[at], s_ys.at[k], s_yr.at[k], (1 - gi, c, f, h))

    def w_all(copy, act):
        lax.fori_loop(0, chunks, lambda k, z: (getattr(copy(k), act)(), z)[1], 0)

    def h_send(d, ff):
        cc = lax.rem(c + d, n_ctx)
        at = pl.ds(pl.multiple_of((cc * 2 + ff) * wb, wb), wb)
        return remote(
            hidden.at[:, at], hall.at[me], s_hs.at[d + n_ctx * (1 if ff is not f else 0)], s_hr.at[me], (gi, cc, ff, h)
        )

    halo_copy = remote(
        x.at[T - HI :], xhalo, s_halo.at[0], s_halo.at[1], (gi, lax.rem(c + 1, n_ctx), f, h)
    )

    @pl.when(jnp.logical_not(last_c))
    def _():
        halo_copy.start()

    x_load = pltpu.make_async_copy(x, xv, s_loc.at[0])
    g_load = pltpu.make_async_copy(g, gv, s_loc.at[1])
    h_load = pltpu.make_async_copy(hidden, hv, s_loc.at[2])
    w_load = pltpu.make_async_copy(w, wh, s_loc.at[3])
    own_at = pl.ds(pl.multiple_of(me * wb, wb), wb)
    own_load = pltpu.make_async_copy(hidden.at[:, own_at], hall.at[me], s_loc.at[4])
    x_load.start()
    g_load.start()

    @pl.when(jnp.logical_not(needing))
    def _():
        w_all(w_send, "start")
        w_load.start()

    for d in range(1, n_ctx):
        h_send(d, f).start()
    h_load.start()
    own_load.start()

    @pl.when(first)
    def _():
        xhalo[...] = jnp.zeros_like(xhalo)
        tails[...] = jnp.zeros_like(tails)
        start[...] = jnp.zeros_like(start)

    @pl.when(last_c)
    def _():
        endg[...] = jnp.zeros_like(endg)
        rims[...] = jnp.zeros_like(rims)
        rimx_r[...] = jnp.zeros_like(rimx_r)

    for copy in smalls:
        copy.wait()
    ends = [span_ref[0, 0]]
    for i in range(1, span_ref.shape[1]):
        ends.append(ends[-1] + span_ref[0, i])

    def segment(pos):
        counted = sum((e <= pos).astype(jnp.int32) for e in ends)
        return jnp.where(pos >= 0, counted, -1)

    pos0 = c * T
    row = lax.broadcasted_iota(jnp.int32, (T, 128), 0)
    lane = lax.broadcasted_iota(jnp.int32, (T, 128), 1)
    seg = segment(pos0 + row)
    for k in range(3):
        m = (segment(pos0 + row - 3 + k) == seg).astype(F32)
        masks[k] = jnp.concatenate([m, m], axis=1)
    same = (seg == segment(pos0 + lane)) & (row >= lane)
    same_ref[...] = same.astype(F32)
    seg_before = segment(jnp.full((T, 128), pos0 - 1, jnp.int32))
    seg_last = segment(jnp.full((T, 128), pos0 + T - 1, jnp.int32))
    alive_ref[...] = (seg == seg_before).astype(F32)
    last_ref[...] = (seg == seg_last).astype(F32)
    through = (seg_last == seg_before).astype(F32)[:heads]

    decay = decay_ref[...]
    raw = raw_ref[...].T
    dt = jnp.maximum(raw, 0.0) + jnp.log1p(jnp.exp(-jnp.abs(raw)))
    tri = (row >= lane).astype(F32)
    cum = dot(tri, -dt * decay, 1, 0, EXACT)
    ea = jnp.exp(cum)
    eb = jnp.exp(-cum)
    small[0] = dt
    small[1] = ea
    small[2] = eb
    small[3] = raw
    eye = (
        lax.broadcasted_iota(jnp.int32, (heads, heads), 0)
        == lax.broadcasted_iota(jnp.int32, (heads, heads), 1)
    ).astype(F32)
    ones = jnp.ones((heads, 128), BF)
    thr = through * sum(dot(p, ones, 1, 0) for p in pieces(eye * ea[T - 1 :, :]))
    ds_acc[...] = jnp.zeros_like(ds_acc)
    r_acc[...] = jnp.zeros_like(r_acc)
    q_acc[...] = jnp.zeros_like(q_acc)
    l_acc[...] = jnp.zeros_like(l_acc)
    db_acc[...] = jnp.zeros_like(db_acc)
    dc_acc[...] = jnp.zeros_like(dc_acc)

    per = NC // HEAD

    def spread(k):
        hr = lax.broadcasted_iota(jnp.int32, (heads, NC), 0)
        cl = lax.broadcasted_iota(jnp.int32, (heads, NC), 1)
        return (hr == k * per + cl // HEAD).astype(F32).astype(BF)

    def widen(v, sel):
        return sum(dot(p, sel, 1, 0) for p in pieces(v))

    def narrow(v, sel):
        hi, mid, _ = pieces(v)
        return dot(hi, sel, 1, 1) + dot(mid, sel, 1, 1)

    def chunk(k):
        return pl.ds(pl.multiple_of(k * NC, NC), NC)

    x_load.wait()
    g_load.wait()

    @pl.when(jnp.logical_not(first))
    def _():
        halo_copy.wait_recv()

    part[...] = jnp.zeros_like(part)
    h_load.wait()

    @pl.when(jnp.logical_not(needing))
    def _():
        w_load.wait()

    def product(i):
        part[...] += dot(hv[:, w_rows(i)], wh[w_rows(i)], 1, 0)

    def second(k, z):
        @pl.when(needing)
        def _():
            w_forward(k).wait_recv()

        product((1 - gi) * chunks + k)
        return z

    def prepare(k, z):
        @pl.when(needing)
        def _():
            w_send(k).wait_recv()
            w_forward(k).start()

        product(gi * chunks + k)

        @pl.when(k >= YLAG)
        def _():
            second(k - YLAG, 0)

        at = chunk(k)
        taps = tapx_ref[:, at]
        xe = jnp.concatenate([xhalo[:, at], xv[:, at]]).astype(F32)
        pre = taps[3:4, :] * xe[HI:]
        for d in range(1, 4):
            pre += taps[3 - d : 4 - d, :] * pltpu.roll(xe, d, 0)[HI:] * masks[3 - d]
        sig = jax.nn.sigmoid(pre)
        xc = pre * sig
        xf[:, at] = xc
        dsf[:, at] = sig * (1.0 + pre * (1.0 - sig))
        sel = spread(k)
        dt_w, a_w, b_w = widen(small[0], sel), widen(small[1], sel), widen(small[2], sel)
        dtw[:, at] = dt_w
        aw[:, at] = a_w
        bw[:, at] = b_w
        scaled = xc * dt_w * b_w
        b_x = scaled.astype(BF)
        bx[:, at] = b_x
        tx[:, at] = (scaled * a_w[T - 1 :, :]).astype(BF)
        a_g = (a_w * gv[:, at].astype(F32)).astype(BF)
        ag[:, at] = a_g
        ds_acc[...] += dot(a_g, b_x, 1, 1)
        thrc[at, :] = sum(dot(sel, p, 0, 0) for p in pieces(thr))
        return z

    lax.fori_loop(0, chunks, prepare, 0)

    @pl.when(jnp.logical_not(needing))
    def _():
        w_all(w_send, "wait_send")

    for d in (*range(1, n_ctx), 0):
        h_send(d, 1 - f).start()

    lax.fori_loop(chunks - YLAG, chunks, second, 0)

    p_swap = remote(part, partr, s_ps.at[0], s_pr, (gi, c, f, 1 - h))
    p_swap.start()
    p_tails = [
        remote(
            part.at[T - 8 :], tails.at[h], s_ps.at[1 + o], s_tr.at[h],
            (gi, lax.rem(c + 1, n_ctx), f, lax.rem(h + o, 2)),
        )
        for o in range(2)
    ]

    @pl.when(jnp.logical_not(last_c))
    def _():
        for p in p_tails:
            p.start()

    p_swap.wait_recv()

    @pl.when(jnp.logical_not(first))
    def _():
        for o in range(2):
            remote(part.at[T - 8 :], tails.at[o], s_ps.at[1], s_tr.at[o], (gi, c, f, 1 - h)).wait_recv()

    taps_b = tapb_ref[...]
    bc = (part[...] + partr[...]).astype(BF).astype(F32)
    tail = (tails[0] + tails[1]).astype(BF).astype(F32)
    be = jnp.concatenate([tail, bc])
    pre_bc = taps_b[3:4, :] * bc
    for d in range(1, 4):
        pre_bc += taps_b[3 - d : 4 - d, :] * pltpu.roll(be, d, 0)[8:] * masks[3 - d]
    sig_bc = jax.nn.sigmoid(pre_bc)
    conv_bc = pre_bc * sig_bc
    silu_bc[...] = sig_bc * (1.0 + pre_bc * (1.0 - sig_bc))
    b_own, c_own = conv_bc[:, :STATE], conv_bc[:, STATE:]
    lastb[...] = (last_ref[...] * b_own).astype(BF)
    alivec[...] = (alive_ref[...] * c_own).astype(BF)
    def piece(k):
        return pl.ds(pl.multiple_of(k * CH, CH), CH)

    def f_copy(k):
        return remote(sn.at[piece(k)], start.at[piece(k)], s_fs.at[k], s_fr.at[k], (gi, lax.rem(c + 1, n_ctx), f, h))

    def b_copy(k):
        return remote(
            sp.at[piece(k)], endg.at[piece(k)], s_bs.at[k], s_br.at[k], (gi, lax.rem(c + n_ctx - 1, n_ctx), f, h)
        )

    def forward(k):
        @pl.when(jnp.logical_not(first))
        def _():
            f_copy(k).wait_recv()

        at = piece(k)
        e = dot(tx[:, at], lastb[...], 0, 0)
        sn[at, :] = (e + thrc[at, :] * start[at, :].astype(F32)).astype(BF)

        @pl.when(jnp.logical_not(last_c))
        def _():
            f_copy(k).start()

    def backward(k):
        @pl.when(jnp.logical_not(last_c))
        def _():
            b_copy(k).wait_recv()

        at = piece(k)
        e = dot(ag[:, at], alivec[...], 0, 0)
        sp[at, :] = (e + thrc[at, :] * endg[at, :].astype(F32)).astype(BF)

        @pl.when(jnp.logical_not(first))
        def _():
            b_copy(k).start()

    row_n = lax.broadcasted_iota(jnp.int32, (T, NC), 0)
    row_8 = lax.broadcasted_iota(jnp.int32, (8, NC), 0)

    def transposed_conv(d_pre, taps):
        own = taps[3:4, :] * d_pre
        rim = jnp.zeros((8, NC), F32)
        for d in range(1, 4):
            z = pltpu.roll(taps[3 - d : 4 - d, :] * masks[3 - d] * d_pre, T - d, 0)
            own += jnp.where(row_n < T - d, z, 0.0)
            rim += jnp.where(row_8 < 8 - d, 0.0, z[T - 8 :])
        return own, rim

    def collect(k):
        at = chunk(k)
        db_acc[...] += dot(tx[:, at], endg[at, :], 1, 0)
        dc_acc[...] += dot(ag[:, at], start[at, :], 1, 0)

    def finish(k):
        at = chunk(k)
        taps = tapx_ref[:, at]
        sel = spread(k)
        sm = sm_ref[...]
        a_w, b_w = aw[:, at], bw[:, at]
        gf = gv[:, at].astype(F32)
        b_x, a_g = bx[:, at], ag[:, at]
        st, en = start[at, :], endg[at, :]
        y = dot(sm, b_x, 1, 0) + dot(alivec[...], st, 1, 1)
        r_acc[...] += narrow(a_w * gf * y, sel)
        d_xt = b_w * (dot(sm, a_g, 0, 0) + a_w[T - 1 :, :] * dot(lastb[...], en, 1, 1))
        q_acc[...] += narrow(xf[:, at] * d_xt, sel)
        prod = en.astype(F32) * sn[at, :].astype(F32)
        hi, mid, _ = pieces(prod)
        ones8 = jnp.ones((8, 128), BF)
        l_acc[...] += narrow(dot(ones8, hi, 1, 1) + dot(ones8, mid, 1, 1), sel)
        skip_w = widen(jnp.broadcast_to(skip_ref[...], (8, heads)), sel)[:1]
        d_pre = (dtw[:, at] * d_xt + skip_w * gf) * dsf[:, at]
        own, rim = transposed_conv(d_pre, taps)
        gxs[:, at] = own.astype(BF)
        gxtail[:, at] = own[T - HI :]
        rimx_s[:, at] = rim

    inner = jnp.logical_and(c > 0, c < n_ctx - 1)
    pieces_n = W // CH
    group = NC // CH
    offset = jnp.where(inner, LAG, pieces_n)
    early = c < n_ctx // 2

    def lead(k, z):
        @pl.when(early)
        def _():
            forward(k)

        @pl.when(jnp.logical_not(early))
        def _():
            backward(k)

        return z

    def scores():
        same_f = same_ref[...] > 0.5
        sm_ref[...] = jnp.where(same_f, dot(c_own, b_own, 1, 1, EXACT), 0.0).astype(BF)
        d_sm = jnp.where(same_f, ds_acc[...], 0.0)
        dps[:, :STATE] = dot(d_sm, c_own, 0, 0, EXACT)
        dps[:, STATE:] = dot(d_sm, b_own, 1, 0, EXACT)

    def step(k, z):
        @pl.when(k + offset < pieces_n)
        def _():
            lead(k + offset, 0)

        @pl.when(early)
        def _():
            backward(k)

        @pl.when(jnp.logical_not(early))
        def _():
            forward(k)

        @pl.when(lax.rem(k, group) == group - 1)
        def _():
            collect(k // group)

            @pl.when(k >= group)
            def _():
                finish(k // group - 1)

        return z

    lax.fori_loop(0, jnp.where(inner, 0, offset), lead, 0)
    scores()
    lax.fori_loop(0, jnp.where(inner, offset, 0), lead, 0)
    lax.fori_loop(0, pieces_n, step, 0)

    rimx = remote(rimx_s, rimx_r, s_rim.at[0], s_rim.at[1], (gi, lax.rem(c + n_ctx - 1, n_ctx), f, h))

    alive, last = alive_ref[...], last_ref[...]
    d_bcc = jnp.concatenate([last * db_acc[...], alive * dc_acc[...]], axis=1)
    dps[...] = (dps[...] + d_bcc) * silu_bc[...]
    d_swap = remote(dps, dpsr, s_ds.at[0], s_dr, (gi, c, f, 1 - h))
    d_swap.start()
    d_rims = [
        remote(
            dps.at[:8], rims.at[h], s_ds.at[1 + o], s_rr.at[h],
            (gi, lax.rem(c + n_ctx - 1, n_ctx), f, lax.rem(h + o, 2)),
        )
        for o in range(2)
    ]

    @pl.when(jnp.logical_not(first))
    def _():
        for p in d_rims:
            p.start()

    finish(chunks - 1)

    @pl.when(jnp.logical_not(first))
    def _():
        rimx.start()

    d_swap.wait_recv()

    @pl.when(jnp.logical_not(last_c))
    def _():
        for o in range(2):
            remote(dps.at[:8], rims.at[o], s_ds.at[1], s_rr.at[o], (gi, c, f, 1 - h)).wait_recv()

    own, _ = transposed_conv(dps[...] + dpsr[...], taps_b)
    rim_in = rims[0] + rims[1]
    row8 = lax.broadcasted_iota(jnp.int32, (8, 2 * STATE), 0)
    npos = pos0 + T + row8
    nseg = segment(npos)
    rim = jnp.zeros((8, 2 * STATE), F32)
    for d in range(1, 4):
        mask = (segment(npos - d) == nseg).astype(F32)
        z = pltpu.roll(taps_b[3 - d : 4 - d, :] * mask * rim_in, 8 - d, 0)
        rim += jnp.where(row8 < 8 - d, 0.0, z)
    d_bc = jnp.concatenate([own[: T - 8], own[T - 8 :] + rim]).astype(BF)
    dall[me] = d_bc

    half = pl.ds(pl.multiple_of(h * (T // 2), T // 2), T // 2)
    other = pl.ds(pl.multiple_of((1 - h) * (T // 2), T // 2), T // 2)

    def z_copy(d):
        return remote(
            dall.at[me, half], dall.at[me, half], s_zs.at[d], s_zr.at[me], (gi, lax.rem(c + d, n_ctx), f, h)
        )

    def x_copy(cc):
        b = cc * 2 + f
        return remote(dall.at[b, half], dall.at[b, half], s_xs.at[cc], s_xr.at[cc], (gi, c, 1 - f, h))

    def c_copy(b):
        return remote(dall.at[b, half], dall.at[b, half], s_cs.at[b], s_cr.at[b], (gi, c, f, 1 - h))

    def from_z(cc):
        b = cc * 2 + f
        return remote(dall.at[b, half], dall.at[b, half], s_zs.at[0], s_zr.at[b], (gi, c, f, 1 - h))

    def from_x(cc):
        b = cc * 2 + 1 - f
        return remote(dall.at[b, half], dall.at[b, half], s_xs.at[0], s_xr.at[cc], (gi, c, f, 1 - h))

    def from_c(b):
        return remote(dall.at[b, other], dall.at[b, other], s_cs.at[0], s_cr.at[b], (gi, c, f, 1 - h))

    left = c < n_ctx // 2
    nearest = [c + 1 - 2 * lax.rem(c, 2), jnp.where(left, 2, 1), jnp.where(left, 3, 0)]
    x_copy(c).start()
    for cc in nearest[::-1]:
        z_copy(lax.rem(cc - c + n_ctx, n_ctx)).start()

    total_q = q_acc[...]
    dts = small[0]
    at_end = row[:, :heads] == T - 1
    d_cum = r_acc[...] - dts * total_q + jnp.where(at_end, l_acc[:1, :], 0.0)
    d_log = dot(tri, d_cum, 0, 0, EXACT)
    ddt_ref[...] = ((total_q - decay_ref[...] * d_log) * jax.nn.sigmoid(small[3])).T
    t_out = pltpu.make_async_copy(ddt_ref, ddt_out, s_out.at[3])
    t_out.start()

    def grad_u(k, z):
        at = w_rows(k)
        gus[:, at] = dot(dall[me], wh[at], 1, 1).astype(BF)
        return z

    lax.fori_loop(0, 2 * chunks, grad_u, 0)
    u_out = pltpu.make_async_copy(gus, gu_out, s_out.at[0])
    u_out.start()

    for cc in nearest:
        from_z(cc).wait_recv()
        x_copy(cc).start()
        c_copy(cc * 2 + f).start()

    @pl.when(jnp.logical_not(last_c))
    def _():
        rimx.wait_recv()

    fixed = gxtail[HI - 8 :, :] + rimx_r[...]
    gxs[T - HI :, :] = jnp.concatenate([gxtail[: HI - 8, :], fixed]).astype(BF)
    x_out = pltpu.make_async_copy(gxs, gx_out, s_out.at[1])
    x_out.start()

    for cc in [c, *nearest]:
        from_x(cc).wait_recv()
        c_copy(cc * 2 + 1 - f).start()

    def h_wait(b):
        remote(hall.at[b], hall.at[b], s_hs.at[0], s_hr.at[b], (gi, c, f, 1 - h)).wait_recv()

    own_load.wait()
    for d in range(1, n_ctx):
        b = lax.rem(c + d, n_ctx) * 2 + f
        from_c(b).wait_recv()
        h_wait(b)
    for d in range(n_ctx):
        b = lax.rem(c + d, n_ctx) * 2 + 1 - f
        from_c(b).wait_recv()
        h_wait(b)
    gws[...] = dot(
        hall[...].reshape(2 * n_ctx * T, wb), dall[...].reshape(2 * n_ctx * T, 2 * STATE), 0, 0
    )
    w_out = pltpu.make_async_copy(gws, gw_out, s_out.at[2])
    w_out.start()

    @pl.when(needing)
    def _():
        w_all(w_forward, "wait_send")

    @pl.when(jnp.logical_not(last_c))
    def _():
        halo_copy.wait_send()
        for p in p_tails:
            p.wait_send()
        lax.fori_loop(0, W // CH, lambda k, z: (f_copy(k).wait_send(), z)[1], 0)

    @pl.when(jnp.logical_not(first))
    def _():
        for p in d_rims:
            p.wait_send()
        rimx.wait_send()
        lax.fori_loop(0, W // CH, lambda k, z: (b_copy(k).wait_send(), z)[1], 0)

    p_swap.wait_send()
    d_swap.wait_send()
    for d in range(n_ctx):
        h_send(d, 1 - f).wait_send()
        x_copy(lax.rem(c + d, n_ctx)).wait_send()
        c_copy(lax.rem(c + d, n_ctx) * 2 + 1 - f).wait_send()
        if d:
            h_send(d, f).wait_send()
            z_copy(d).wait_send()
            c_copy(lax.rem(c + d, n_ctx) * 2 + f).wait_send()
    u_out.wait()
    x_out.wait()
    w_out.wait()
    t_out.wait()


def fused(hidden, w, x, g, raw, decay, skip, tapx, tapb, spans):
    T, W = x.shape
    DH = hidden.shape[1]
    n_ctx = lax.axis_size("ctx")
    blocks = 2 * n_ctx
    wb = DH // blocks
    heads = raw.shape[0]
    K = W // CH
    U = W // NC
    vm, dma = pltpu.VMEM, pltpu.SemaphoreType.DMA
    spec = pl.BlockSpec
    hbm = spec(memory_space=pltpu.HBM)
    out = spec(memory_space=pl.ANY)
    S2 = 2 * STATE
    return pl.pallas_call(
        fused_kernel,
        out_shape=(
            jax.ShapeDtypeStruct((T, W), BF),
            jax.ShapeDtypeStruct((T, DH), BF),
            jax.ShapeDtypeStruct((heads, T), F32),
            jax.ShapeDtypeStruct((wb, S2), F32),
        ),
        in_specs=[hbm] * 10,
        out_specs=(out,) * 4,
        scratch_shapes=[
            vm((heads, T), F32), vm((1, heads), F32), vm((1, heads), F32), vm((4, W), F32), vm((4, S2), F32),
            pltpu.SMEM(spans.shape, jnp.int32), vm((heads, T), F32),
            vm((T, W), BF), vm((T, W), BF), vm((T, DH), BF), vm((DH, S2), BF), vm((HI, W), BF),
            vm((T, W), F32), vm((T, W), F32), vm((T, W), F32), vm((T, W), F32), vm((T, W), F32),
            vm((T, W), BF), vm((T, W), BF), vm((T, W), BF), vm((W, STATE), F32),
            vm((W, STATE), BF), vm((W, STATE), BF), vm((W, STATE), BF), vm((W, STATE), BF),
            vm((3, T, S2), F32), vm((T, STATE), F32), vm((T, STATE), F32), vm((T, STATE), F32),
            vm((4, T, heads), F32), vm((T, T), F32), vm((T, S2), F32), vm((T, S2), F32), vm((2, 8, S2), F32),
            vm((T, S2), F32), vm((T, T), BF), vm((T, STATE), BF), vm((T, STATE), BF),
            vm((T, STATE), F32), vm((T, STATE), F32), vm((T, S2), F32), vm((T, S2), F32), vm((2, 8, S2), F32),
            vm((8, W), F32), vm((8, W), F32), vm((HI, W), F32),
            vm((T, heads), F32), vm((T, heads), F32), vm((8, heads), F32),
            vm((blocks, T, wb), BF), vm((blocks, T, S2), BF),
            vm((T, W), BF), vm((T, DH), BF), vm((wb, S2), F32),
            dma((5,)), dma((U,)), dma((U,)), dma((U,)), dma((U,)), dma((blocks,)), dma((blocks,)), dma((2,)),
            dma((K,)), dma((K,)), dma((K,)), dma((K,)),
            dma((3,)), dma, dma((2,)), dma((3,)), dma, dma((2,)), dma((2,)),
            dma((n_ctx,)), dma((blocks,)), dma((n_ctx,)), dma((n_ctx,)), dma((blocks,)), dma((blocks,)), dma((6,)), dma((4,)),
        ],
        compiler_params=pltpu.CompilerParams(
            collective_id=0, has_side_effects=True, vmem_limit_bytes=60 << 20
        ),
        cost_estimate=pl.CostEstimate(
            flops=2 * T * 256 * (W * 9 + DH * 4), bytes_accessed=8 << 20, transcendentals=4 * T * W
        ),
    )(hidden, w, x, g, raw, decay, skip, tapx, tapb, spans)


def publish_kernel(*refs):
    n = (len(refs) - 2) // 3
    ins, outs, held, in_sem, out_sem = refs[:n], refs[n : 2 * n], refs[2 * n : 3 * n], refs[-2], refs[-1]
    loads, stores = [], []
    for i in range(n):
        rows = ins[i].shape[0] // PUB
        for j in range(PUB):
            at = pl.ds(j * rows, rows)
            loads.append(pltpu.make_async_copy(ins[i].at[at], held[i].at[at], in_sem.at[i, j]))
            stores.append(pltpu.make_async_copy(held[i].at[at], outs[i].at[at], out_sem.at[i, j]))
    for copy in loads:
        copy.start()
    for load, store in zip(loads, stores):
        load.wait()
        store.start()
    for copy in stores:
        copy.wait()


def publish(arrays):
    n = len(arrays)
    hbm = pl.BlockSpec(memory_space=pl.ANY)
    return pl.pallas_call(
        publish_kernel,
        out_shape=tuple(jax.ShapeDtypeStruct(a.shape, a.dtype) for a in arrays),
        in_specs=[hbm] * n,
        out_specs=(hbm,) * n,
        scratch_shapes=[pltpu.VMEM(a.shape, a.dtype) for a in arrays]
        + [pltpu.SemaphoreType.DMA((n, PUB)), pltpu.SemaphoreType.DMA((n, PUB))],
        compiler_params=pltpu.CompilerParams(vmem_limit_bytes=60 << 20),
    )(*arrays)


def on_device(
    hidden_in, w_bc, x_in, dt_raw, decay_rate, conv_x, conv_bc, skip_gain, span_len, grad_y
):
    T = x_in.shape[1]
    hidden = hidden_in[0]
    half_width = hidden.shape[1]
    n_ctx, n_fsdp, n_head = (lax.axis_size(a) for a in ("ctx", "fsdp", "head"))
    assert T * 2 == MOST and dt_raw.shape[2] == 32
    x0, g0, raw0 = x_in[0], grad_y[0], dt_raw[0]
    if (lax.axis_size("groups"), n_ctx, n_fsdp, n_head) == (2, 4, 2, 2):
        outs = fused(
            hidden, w_bc, x0, g0, raw0.T, decay_rate[None, :], skip_gain[None, :], conv_x, conv_bc, span_len
        )
        outs = publish(outs)
        return (outs[0][None], outs[1][None], outs[2].T[None], outs[3][None])
    if n_fsdp == n_head:
        route = [(f * n_head + h, h * n_head + f) for f in range(n_fsdp) for h in range(n_head)]
        w_half = lax.ppermute(w_bc, ("fsdp", "head"), route)
    else:
        w_full = lax.all_gather(w_bc, "fsdp", axis=0, tiled=True)
        w_half = lax.dynamic_slice_in_dim(
            w_full, lax.axis_index("head") * half_width, half_width, 0
        )
    raws = [shifted(raw0, "ctx", d) for d in (2, 1)] + [raw0] + [shifted(raw0, "ctx", -d) for d in (1, 2)]
    x1, g1 = shifted(x0, "ctx", 1), shifted(g0, "ctx", -1)
    x2, g2 = shifted(x0, "ctx", 2), shifted(g0, "ctx", -2)

    swap = [(i, (i + 1) % n_head) for i in range(n_head)]
    partial_bc = jnp.dot(hidden, w_half, preferred_element_type=F32)
    bc_pre = (partial_bc + lax.ppermute(partial_bc, "head", swap)).astype(BF)
    bcs = [shifted(bc_pre, "ctx", d) for d in (2, 1)] + [bc_pre] + [shifted(bc_pre, "ctx", -d) for d in (1, 2)]

    n_blocks = n_ctx * n_fsdp
    blocks = hidden.reshape(T, n_blocks, half_width // n_blocks).transpose(1, 0, 2)
    hidden_all = lax.all_to_all(blocks, ("ctx", "fsdp"), 0, 0, tiled=True)

    position = (lax.axis_index("ctx") - 2) * T + jnp.arange(-3, 5 * T, dtype=jnp.int32)
    spans = span_len.shape[1]
    earlier = jnp.arange(spans)[:, None] <= jnp.arange(spans)[None, :]
    span_ends = jnp.sum(jnp.where(earlier, span_len[0][:, None], 0), axis=0)
    counted = jnp.sum((span_ends[None, :] <= position[:, None]).astype(jnp.int32), axis=1)
    segment = jnp.where(position >= 0, counted, -1).astype(F32)
    own_seg = segment[3:]
    by_block = own_seg.reshape(5, T)
    before = jnp.broadcast_to(segment[2 : 2 + 5 * T : T][:, None], (5, T)).reshape(-1)
    last = jnp.broadcast_to(by_block[:, T - 1 :], (5, T)).reshape(-1)
    info = jnp.stack(
        [(segment[k : k + 5 * T] == own_seg).astype(F32) for k in range(3)]
        + [(own_seg == before).astype(F32), (own_seg == last).astype(F32), own_seg],
        axis=1,
    )
    segrow = by_block[2:3]
    raw = jnp.tile(jnp.concatenate(raws), (1, 4))
    decay = jnp.tile(decay_rate, 4)[None, :]
    skip = jnp.repeat(skip_gain, HEAD)[None, :]

    dx, tail, rim, dbc, rimbc, ddt = ssm(
        (x2, x1, x0), (g0, g1, g2), bcs, raw, info, segrow, decay, skip, conv_x, conv_bc
    )
    back = shifted(rim, "ctx", -1)
    grad_x = lax.dynamic_update_slice(dx, (tail + back).astype(BF), (T - 8, 0))

    other = lax.ppermute(dbc, "head", swap)
    rim_same = shifted(rimbc, "ctx", -1)
    cross = [
        (c * n_head + h, (c - 1) * n_head + (h + 1) % n_head)
        for c in range(1, n_ctx)
        for h in range(n_head)
    ]
    rim_cross = lax.ppermute(rimbc, ("ctx", "head"), cross)
    d_bc = ((dbc + other) + jnp.pad(rim_same + rim_cross, ((T - 8, 0), (0, 0)))).astype(BF)
    grad_u = lax.dot_general(
        d_bc, w_half, (((1,), (1,)), ((), ())), preferred_element_type=F32
    ).astype(BF)
    d_all = lax.all_gather(d_bc, ("ctx", "fsdp"), axis=0)
    grad_w = lax.dot_general(
        hidden_all.reshape(n_blocks * T, -1),
        d_all.reshape(n_blocks * T, -1),
        (((0,), (0,)), ((), ())),
        preferred_element_type=F32,
    )
    return (grad_x[None], grad_u[None], ddt[None], grad_w[None])


def solution(mesh):
    return jax.shard_map(
        on_device,
        mesh=mesh,
        in_specs=(
            P(("groups", "fsdp"), "ctx", "head"),
            P("fsdp", None),
            P(("groups", "fsdp"), "ctx", "head"),
            P(("groups", "fsdp"), "ctx", "head"),
            P("head"),
            P(None, "head"),
            P(),
            P("head"),
            P(("groups", "fsdp"), None),
            P(("groups", "fsdp"), "ctx", "head"),
        ),
        out_specs=(
            P(("groups", "fsdp"), "ctx", "head"),
            P(("groups", "fsdp"), "ctx", "head"),
            P(("groups", "fsdp"), "ctx", "head"),
            P(("groups", "head"), ("ctx", "fsdp"), None),
        ),
        check_vma=False,
    )
```

```python
import jax
import jax.numpy as jnp
from jax import lax
from jax.experimental import pallas as pl
from jax.experimental.pallas import tpu as pltpu
from jax.sharding import PartitionSpec as P

STATE = 128
HEAD = 64
MOST = 256
BF = jnp.bfloat16
F32 = jnp.float32
EXACT = lax.Precision.HIGHEST


def shifted(block, axis, distance):
    devices = range(lax.axis_size(axis))
    route = [(i - distance, i) for i in devices if i - distance in devices]
    return lax.ppermute(block, axis, route)


def dot(a, b, ca, cb, precision=None):
    return lax.dot_general(
        a, b, (((ca,), (cb,)), ((), ())), precision=precision, preferred_element_type=F32
    )


def ssm_kernel(
    x2, x1, x0, g0, g1, g2, b2, b1, b0, b3, b4, raw_ref, info_ref, segrow_ref,
    decay_ref, skip_ref, tapx_ref, tapb_ref,
    dx_ref, tail_ref, rim_ref, dbc_ref, rimbc_ref, ddt_ref,
    masks, bias_ref, s_ref, cols_a, cols_b, cum_rows, bprev, cnext, bown, cown,
    silu_bc, d_s, d_b, d_c, acc,
):
    T = x0.shape[0]
    pairs = x0.shape[1] // 128
    lane = lax.broadcasted_iota(jnp.int32, (T, 128), 1)
    row = lax.broadcasted_iota(jnp.int32, (T, 128), 0)
    low = lane < HEAD
    group = lane // 32
    info = info_ref[...]
    for k in range(3):
        masks[k] = jnp.broadcast_to(info[: 3 * T, k : k + 1], (3 * T, 128))

    def col(block, k):
        return info[block * T : (block + 1) * T, k : k + 1]

    tri = (row >= lane).astype(F32)
    decay = decay_ref[...]
    dts, cums, carried, toward = [], [], [], []
    for j in range(5):
        raw = raw_ref[j * T : (j + 1) * T, :]
        dt = jnp.maximum(raw, 0.0) + jnp.log1p(jnp.exp(-jnp.abs(raw)))
        cum = dot(tri, -dt * decay, 1, 0, EXACT)
        dts.append(dt)
        cums.append(cum)
        carried.append(jnp.exp(cum) * col(j, 3))
        toward.append(jnp.exp(cum[T - 1 :, :] - cum) * col(j, 4))
    a1 = dts[1] * toward[1]
    a2 = dts[0] * toward[0] * carried[1][T - 1 :, :]
    c1 = carried[3]
    c2 = carried[4] * carried[3][T - 1 :, :]

    def packed(p, q, r, s):
        return jnp.where(group == 0, p, jnp.where(group == 1, q, jnp.where(group == 2, r, s)))

    cols_a[...] = packed(dts[2], cums[2], carried[2], toward[2])
    cols_b[...] = packed(a2, a1, c1, c2)
    cum_rows[...] = cums[2].T
    same = col(2, 5) == segrow_ref[...]
    bias_ref[...] = jnp.where(same & (row >= lane), 0.0, -1e30)

    taps_b = tapb_ref[...]
    bc = jnp.concatenate([b2[...], b1[...], b0[...], b3[...], b4[...]]).astype(F32)
    pre_bc = taps_b[3:4, :] * bc
    for k in range(3):
        pre_bc += taps_b[k : k + 1, :] * pltpu.roll(bc, 3 - k, 0) * info[:, k : k + 1]
    sig_bc = jax.nn.sigmoid(pre_bc)
    conv_bc = pre_bc * sig_bc
    own_sig = sig_bc[2 * T : 3 * T]
    silu_bc[...] = own_sig * (1.0 + pre_bc[2 * T : 3 * T] * (1.0 - own_sig))
    bprev[...] = conv_bc[: 2 * T, :STATE].astype(BF)
    cnext[...] = conv_bc[3 * T :, STATE:].astype(BF)
    bown[...] = conv_bc[2 * T : 3 * T, :STATE]
    cown[...] = conv_bc[2 * T : 3 * T, STATE:]
    s_ref[...] = dot(cown[...], bown[...], 1, 1, EXACT)
    d_s[...] = jnp.zeros_like(d_s)
    d_b[...] = jnp.zeros_like(d_b)
    d_c[...] = jnp.zeros_like(d_c)
    acc[...] = jnp.zeros_like(acc)

    def pair(i, carry):
        at = pl.ds(pl.multiple_of(i * 128, 128), 128)
        ca = pltpu.roll(cols_a[...], (128 - 2 * i) % 128, 1)
        cb = pltpu.roll(cols_b[...], (128 - 2 * i) % 128, 1)

        def wide(c, q):
            return jnp.where(low, c[:, 32 * q : 32 * q + 1], c[:, 32 * q + 1 : 32 * q + 2])

        def tall(c, q):
            return c[:, 32 * q : 32 * q + 1], c[:, 32 * q + 1 : 32 * q + 2]

        taps = tapx_ref[:, at]
        xe = jnp.concatenate([x2[:, at], x1[:, at], x0[:, at]]).astype(F32)
        pre = taps[3:4, :] * xe
        for k in range(3):
            pre += taps[k : k + 1, :] * pltpu.roll(xe, 3 - k, 0) * masks[k]
        sig = jax.nn.sigmoid(pre)
        xc = pre * sig
        xown = xc[2 * T :]
        sown = sig[2 * T :]
        dsilu = sown * (1.0 + pre[2 * T :] * (1.0 - sown))
        dt_w = wide(ca, 0)
        toward_w = wide(ca, 3)
        xw = jnp.concatenate([xc[:T] * wide(cb, 0), xc[T : 2 * T] * wide(cb, 1)]).astype(BF)
        start = dot(xw, bprev[...], 0, 0)
        gw = jnp.concatenate(
            [g1[:, at].astype(F32) * wide(cb, 2), g2[:, at].astype(F32) * wide(cb, 3)]
        ).astype(BF)
        end_grad = dot(gw, cnext[...], 0, 0)
        start_b = start.astype(BF)
        end_b = end_grad.astype(BF)
        gy = g0[:, at].astype(F32)
        gg = jnp.concatenate([jnp.where(low, gy, 0.0), jnp.where(low, 0.0, gy)]).astype(BF)
        xt = xown * dt_w
        xt_b = xt.astype(BF)
        xx = jnp.concatenate([jnp.where(low, xt, 0.0), jnp.where(low, 0.0, xt)]).astype(BF)
        d_m = dot(gg, xt_b, 1, 1)
        cum_a, cum_b = tall(ca, 1)
        bias = bias_ref[...]
        decay_t = jnp.concatenate(
            [
                jnp.exp(cum_a - cum_rows[pl.ds(2 * i, 1), :] + bias),
                jnp.exp(cum_b - cum_rows[pl.ds(2 * i + 1, 1), :] + bias),
            ]
        )
        s_all = s_ref[...]
        s_two = jnp.concatenate([s_all, s_all])
        ls = decay_t * s_two
        ldm = decay_t * d_m
        d_s[...] += ldm[:T] + ldm[T:]
        d_x = dot(ls.astype(BF), gg, 0, 0)
        car = jnp.concatenate(tall(ca, 2))
        tow = jnp.concatenate(tall(ca, 3))
        c_u = car * dot(gg, start_b, 1, 0)
        d_c[...] += c_u[:T] + c_u[T:]
        c_own = cown[...]
        c_two = jnp.concatenate([c_own, c_own])
        r = jnp.sum(ldm * s_two + c_u * c_two, axis=1, keepdims=True)
        t_v = tow * dot(xx, end_b, 1, 0)
        d_b[...] += t_v[:T] + t_v[T:]
        d_xe = dot(bown[...].astype(BF), end_b, 1, 1) * toward_w
        d_xt = d_x + d_xe
        prod = xown * d_xt
        q_a = jnp.sum(jnp.where(low, prod, 0.0), axis=1, keepdims=True)
        q_b = jnp.sum(jnp.where(low, 0.0, prod), axis=1, keepdims=True)
        ends = jnp.sum(xt * d_xe, axis=0, keepdims=True)
        inner = end_grad * start
        low_row = low[:1]
        through_a, through_b = (v[T - 1 :, :] for v in tall(ca, 2))
        last_a = jnp.sum(jnp.where(low_row, ends, 0.0), axis=1, keepdims=True) + through_a * jnp.sum(
            jnp.sum(inner[:HEAD], axis=0, keepdims=True), axis=1, keepdims=True
        )
        last_b = jnp.sum(jnp.where(low_row, 0.0, ends), axis=1, keepdims=True) + through_b * jnp.sum(
            jnp.sum(inner[HEAD:], axis=0, keepdims=True), axis=1, keepdims=True
        )
        dt_a, dt_b = tall(ca, 0)
        final = row[:, :1] == T - 1
        cum_ga = r[:T] - dt_a * q_a + jnp.where(final, last_a, 0.0)
        cum_gb = r[T:] - dt_b * q_b + jnp.where(final, last_b, 0.0)
        placed = jnp.where(
            lane == 0,
            q_a,
            jnp.where(
                lane == 1, q_b, jnp.where(lane == 32, cum_ga, jnp.where(lane == 33, cum_gb, 0.0))
            ),
        )
        acc[...] += pltpu.roll(placed, 2 * i, 1)
        d_pre = (dt_w * d_xt + skip_ref[:, at] * gy) * dsilu
        own = taps[3:4, :] * d_pre
        rim = jnp.zeros((8, 128), F32)
        for k in range(3):
            d = 3 - k
            z = pltpu.roll(taps[k : k + 1, :] * masks[k, 2 * T :] * d_pre, T - d, 0)
            own += jnp.where(row < T - d, z, 0.0)
            rim += jnp.where(row[T - 8 :] < T - d, 0.0, z[T - 8 :])
        dx_ref[:, at] = own.astype(BF)
        tail_ref[:, at] = own[T - 8 :]
        rim_ref[:, at] = rim
        return carry

    lax.fori_loop(0, pairs, pair, 0)

    ds = d_s[...]
    full_c = d_c[...] + dot(ds, bown[...], 1, 0, EXACT)
    full_b = d_b[...] + dot(ds, cown[...], 0, 0, EXACT)
    d_pre = jnp.concatenate([full_b, full_c], axis=1) * silu_bc[...]
    own = taps_b[3:4, :] * d_pre
    rim = jnp.zeros((8, 2 * STATE), F32)
    row2 = lax.broadcasted_iota(jnp.int32, (T, 2 * STATE), 0)
    for k in range(3):
        d = 3 - k
        z = pltpu.roll(taps_b[k : k + 1, :] * info[2 * T : 3 * T, k : k + 1] * d_pre, T - d, 0)
        own += jnp.where(row2 < T - d, z, 0.0)
        rim += jnp.where(row2[T - 8 :] < T - d, 0.0, z[T - 8 :])
    dbc_ref[...] = own
    rimbc_ref[...] = rim
    total = acc[...]
    d_log = pltpu.roll(dot(tri, total, 0, 0, EXACT), 96, 1)
    raw = raw_ref[2 * T : 3 * T, :]
    ddt_ref[...] = ((total - decay * d_log) * jax.nn.sigmoid(raw))[:, :32]


def ssm(xs, gs, bcs, raw, info, segrow, decay, skip, tapx, tapb):
    T, W = xs[0].shape
    vm = pltpu.VMEM
    return pl.pallas_call(
        ssm_kernel,
        out_shape=(
            jax.ShapeDtypeStruct((T, W), BF),
            jax.ShapeDtypeStruct((8, W), F32),
            jax.ShapeDtypeStruct((8, W), F32),
            jax.ShapeDtypeStruct((T, 2 * STATE), F32),
            jax.ShapeDtypeStruct((8, 2 * STATE), F32),
            jax.ShapeDtypeStruct((T, 32), F32),
        ),
        scratch_shapes=[
            vm((3, 3 * T, 128), F32), vm((T, T), F32), vm((T, T), F32), vm((T, 128), F32),
            vm((T, 128), F32), vm((128, T), F32), vm((2 * T, STATE), BF), vm((2 * T, STATE), BF),
            vm((T, STATE), F32), vm((T, STATE), F32), vm((T, 2 * STATE), F32),
            vm((T, T), F32), vm((T, STATE), F32), vm((T, STATE), F32), vm((T, 128), F32),
        ],
        compiler_params=pltpu.CompilerParams(vmem_limit_bytes=40 << 20),
        cost_estimate=pl.CostEstimate(
            flops=2 * 9 * T * 256 * W, bytes_accessed=8 * T * W * 2, transcendentals=6 * T * W
        ),
    )(*xs, *gs, *bcs, raw, info, segrow, decay, skip, tapx, tapb)


MESH = pl.DeviceIdType.MESH
NC = 256
HI = 16
CH = 256
LAG = 3
YLAG = 3
PUB = 4


def pieces(v):
    hi = v.astype(BF)
    rest = v - hi.astype(F32)
    mid = rest.astype(BF)
    lo = (rest - mid.astype(F32)).astype(BF)
    return hi, mid, lo


def fused_kernel(
    hidden, w, x, g, raw_in, decay_in, skip_in, tapx_in, tapb_in, span_in,
    gx_out, gu_out, ddt_out, gw_out,
    raw_ref, decay_ref, skip_ref, tapx_ref, tapb_ref, span_ref, ddt_ref,
    xv, gv, hv, wh, xhalo, xf, dsf, aw, bw, dtw, bx, tx, ag, thrc, start, endg, sn, sp,
    masks, same_ref, alive_ref, last_ref, small, ds_acc, part, partr, tails, silu_bc,
    sm_ref, lastb, alivec, db_acc, dc_acc, dps, dpsr, rims, rimx_s, rimx_r, gxtail, r_acc, q_acc, l_acc,
    hall, dall, gxs, gus, gws,
    s_loc, s_ws, s_wr, s_ys, s_yr, s_hs, s_hr, s_halo, s_fs, s_fr, s_bs, s_br,
    s_ps, s_pr, s_tr, s_ds, s_dr, s_rr, s_rim, s_zs, s_zr, s_xs, s_xr, s_cs, s_cr, s_small, s_out,
):
    T, W = gxs.shape
    gi, c, f, h = (lax.axis_index(a) for a in ("groups", "ctx", "fsdp", "head"))
    n_ctx = lax.axis_size("ctx")
    DH = hv.shape[1]
    chunks = W // NC
    wrows = wh.shape[0] // 2 // chunks
    heads = raw_ref.shape[0]
    wb = hall.shape[2]
    first, last_c = c == 0, c == n_ctx - 1
    needing = h != f
    me = c * 2 + f

    def remote(src, dst, ss, rs, device):
        return pltpu.make_async_remote_copy(
            src_ref=src, dst_ref=dst, send_sem=ss, recv_sem=rs, device_id=device, device_id_type=MESH
        )

    smalls = [
        pltpu.make_async_copy(src, dst, s_small.at[i])
        for i, (src, dst) in enumerate(
            (
                (span_in, span_ref), (raw_in, raw_ref), (decay_in, decay_ref), (skip_in, skip_ref),
                (tapx_in, tapx_ref), (tapb_in, tapb_ref),
            )
        )
    ]
    for copy in smalls:
        copy.start()
    barrier = pltpu.get_barrier_semaphore()
    for o in range(1, 4 * n_ctx):
        oc, of, oh = o // 4, (o // 2) % 2, o % 2
        pl.semaphore_signal(
            barrier, 1, device_id=(gi, lax.rem(c + oc, n_ctx), lax.rem(f + of, 2), lax.rem(h + oh, 2)),
            device_id_type=MESH,
        )
    pl.semaphore_signal(barrier, 1, device_id=(1 - gi, c, f, h), device_id_type=MESH)
    pl.semaphore_wait(barrier, 4 * n_ctx)

    def w_rows(k):
        return pl.ds(pl.multiple_of(k * wrows, wrows), wrows)

    def w_rows(k):
        return pl.ds(pl.multiple_of(k * wrows, wrows), wrows)

    def w_send(k):
        at = w_rows(gi * chunks + k)
        return remote(w.at[at], wh.at[at], s_ws.at[k], s_wr.at[k], (gi, c, 1 - f, h))

    def w_forward(k):
        at = w_rows(gi * chunks + k)
        return remote(wh.at[at], wh.at[at], s_ys.at[k], s_yr.at[k], (1 - gi, c, f, h))

    def w_all(copy, act):
        lax.fori_loop(0, chunks, lambda k, z: (getattr(copy(k), act)(), z)[1], 0)

    def h_send(d, ff):
        cc = lax.rem(c + d, n_ctx)
        at = pl.ds(pl.multiple_of((cc * 2 + ff) * wb, wb), wb)
        return remote(
            hidden.at[:, at], hall.at[me], s_hs.at[d + n_ctx * (1 if ff is not f else 0)], s_hr.at[me], (gi, cc, ff, h)
        )

    halo_copy = remote(
        x.at[T - HI :], xhalo, s_halo.at[0], s_halo.at[1], (gi, lax.rem(c + 1, n_ctx), f, h)
    )

    @pl.when(jnp.logical_not(last_c))
    def _():
        halo_copy.start()

    x_load = pltpu.make_async_copy(x, xv, s_loc.at[0])
    g_load = pltpu.make_async_copy(g, gv, s_loc.at[1])
    h_load = pltpu.make_async_copy(hidden, hv, s_loc.at[2])
    w_load = pltpu.make_async_copy(w, wh, s_loc.at[3])
    own_at = pl.ds(pl.multiple_of(me * wb, wb), wb)
    own_load = pltpu.make_async_copy(hidden.at[:, own_at], hall.at[me], s_loc.at[4])
    x_load.start()
    g_load.start()

    @pl.when(jnp.logical_not(needing))
    def _():
        w_all(w_send, "start")
        w_load.start()

    for d in range(1, n_ctx):
        h_send(d, f).start()
    h_load.start()
    own_load.start()

    @pl.when(first)
    def _():
        xhalo[...] = jnp.zeros_like(xhalo)
        tails[...] = jnp.zeros_like(tails)
        start[...] = jnp.zeros_like(start)

    @pl.when(last_c)
    def _():
        endg[...] = jnp.zeros_like(endg)
        rims[...] = jnp.zeros_like(rims)
        rimx_r[...] = jnp.zeros_like(rimx_r)

    for copy in smalls:
        copy.wait()
    ends = [span_ref[0, 0]]
    for i in range(1, span_ref.shape[1]):
        ends.append(ends[-1] + span_ref[0, i])

    def segment(pos):
        counted = sum((e <= pos).astype(jnp.int32) for e in ends)
        return jnp.where(pos >= 0, counted, -1)

    pos0 = c * T
    row = lax.broadcasted_iota(jnp.int32, (T, 128), 0)
    lane = lax.broadcasted_iota(jnp.int32, (T, 128), 1)
    seg = segment(pos0 + row)
    for k in range(3):
        m = (segment(pos0 + row - 3 + k) == seg).astype(F32)
        masks[k] = jnp.concatenate([m, m], axis=1)
    same = (seg == segment(pos0 + lane)) & (row >= lane)
    same_ref[...] = same.astype(F32)
    seg_before = segment(jnp.full((T, 128), pos0 - 1, jnp.int32))
    seg_last = segment(jnp.full((T, 128), pos0 + T - 1, jnp.int32))
    alive_ref[...] = (seg == seg_before).astype(F32)
    last_ref[...] = (seg == seg_last).astype(F32)
    through = (seg_last == seg_before).astype(F32)[:heads]

    decay = decay_ref[...]
    raw = raw_ref[...].T
    dt = jnp.maximum(raw, 0.0) + jnp.log1p(jnp.exp(-jnp.abs(raw)))
    tri = (row >= lane).astype(F32)
    cum = dot(tri, -dt * decay, 1, 0, EXACT)
    ea = jnp.exp(cum)
    eb = jnp.exp(-cum)
    small[0] = dt
    small[1] = ea
    small[2] = eb
    small[3] = raw
    eye = (
        lax.broadcasted_iota(jnp.int32, (heads, heads), 0)
        == lax.broadcasted_iota(jnp.int32, (heads, heads), 1)
    ).astype(F32)
    ones = jnp.ones((heads, 128), BF)
    thr = through * sum(dot(p, ones, 1, 0) for p in pieces(eye * ea[T - 1 :, :]))
    ds_acc[...] = jnp.zeros_like(ds_acc)
    r_acc[...] = jnp.zeros_like(r_acc)
    q_acc[...] = jnp.zeros_like(q_acc)
    l_acc[...] = jnp.zeros_like(l_acc)
    db_acc[...] = jnp.zeros_like(db_acc)
    dc_acc[...] = jnp.zeros_like(dc_acc)

    per = NC // HEAD

    def spread(k):
        hr = lax.broadcasted_iota(jnp.int32, (heads, NC), 0)
        cl = lax.broadcasted_iota(jnp.int32, (heads, NC), 1)
        return (hr == k * per + cl // HEAD).astype(F32).astype(BF)

    def widen(v, sel):
        return sum(dot(p, sel, 1, 0) for p in pieces(v))

    def narrow(v, sel):
        hi, mid, _ = pieces(v)
        return dot(hi, sel, 1, 1) + dot(mid, sel, 1, 1)

    def chunk(k):
        return pl.ds(pl.multiple_of(k * NC, NC), NC)

    x_load.wait()
    g_load.wait()

    @pl.when(jnp.logical_not(first))
    def _():
        halo_copy.wait_recv()

    part[...] = jnp.zeros_like(part)
    h_load.wait()

    @pl.when(jnp.logical_not(needing))
    def _():
        w_load.wait()

    def product(i):
        part[...] += dot(hv[:, w_rows(i)], wh[w_rows(i)], 1, 0)

    def second(k, z):
        @pl.when(needing)
        def _():
            w_forward(k).wait_recv()

        product((1 - gi) * chunks + k)
        return z

    def prepare(k, z):
        @pl.when(needing)
        def _():
            w_send(k).wait_recv()
            w_forward(k).start()

        product(gi * chunks + k)

        @pl.when(k >= YLAG)
        def _():
            second(k - YLAG, 0)

        at = chunk(k)
        taps = tapx_ref[:, at]
        xe = jnp.concatenate([xhalo[:, at], xv[:, at]]).astype(F32)
        pre = taps[3:4, :] * xe[HI:]
        for d in range(1, 4):
            pre += taps[3 - d : 4 - d, :] * pltpu.roll(xe, d, 0)[HI:] * masks[3 - d]
        sig = jax.nn.sigmoid(pre)
        xc = pre * sig
        xf[:, at] = xc
        dsf[:, at] = sig * (1.0 + pre * (1.0 - sig))
        sel = spread(k)
        dt_w, a_w, b_w = widen(small[0], sel), widen(small[1], sel), widen(small[2], sel)
        dtw[:, at] = dt_w
        aw[:, at] = a_w
        bw[:, at] = b_w
        scaled = xc * dt_w * b_w
        b_x = scaled.astype(BF)
        bx[:, at] = b_x
        tx[:, at] = (scaled * a_w[T - 1 :, :]).astype(BF)
        a_g = (a_w * gv[:, at].astype(F32)).astype(BF)
        ag[:, at] = a_g
        ds_acc[...] += dot(a_g, b_x, 1, 1)
        thrc[at, :] = sum(dot(sel, p, 0, 0) for p in pieces(thr))
        return z

    lax.fori_loop(0, chunks, prepare, 0)

    @pl.when(jnp.logical_not(needing))
    def _():
        w_all(w_send, "wait_send")

    for d in (*range(1, n_ctx), 0):
        h_send(d, 1 - f).start()

    lax.fori_loop(chunks - YLAG, chunks, second, 0)

    p_swap = remote(part, partr, s_ps.at[0], s_pr, (gi, c, f, 1 - h))
    p_swap.start()
    p_tails = [
        remote(
            part.at[T - 8 :], tails.at[h], s_ps.at[1 + o], s_tr.at[h],
            (gi, lax.rem(c + 1, n_ctx), f, lax.rem(h + o, 2)),
        )
        for o in range(2)
    ]

    @pl.when(jnp.logical_not(last_c))
    def _():
        for p in p_tails:
            p.start()

    p_swap.wait_recv()

    @pl.when(jnp.logical_not(first))
    def _():
        for o in range(2):
            remote(part.at[T - 8 :], tails.at[o], s_ps.at[1], s_tr.at[o], (gi, c, f, 1 - h)).wait_recv()

    taps_b = tapb_ref[...]
    bc = (part[...] + partr[...]).astype(BF).astype(F32)
    tail = (tails[0] + tails[1]).astype(BF).astype(F32)
    be = jnp.concatenate([tail, bc])
    pre_bc = taps_b[3:4, :] * bc
    for d in range(1, 4):
        pre_bc += taps_b[3 - d : 4 - d, :] * pltpu.roll(be, d, 0)[8:] * masks[3 - d]
    sig_bc = jax.nn.sigmoid(pre_bc)
    conv_bc = pre_bc * sig_bc
    silu_bc[...] = sig_bc * (1.0 + pre_bc * (1.0 - sig_bc))
    b_own, c_own = conv_bc[:, :STATE], conv_bc[:, STATE:]
    lastb[...] = (last_ref[...] * b_own).astype(BF)
    alivec[...] = (alive_ref[...] * c_own).astype(BF)
    def piece(k):
        return pl.ds(pl.multiple_of(k * CH, CH), CH)

    def f_copy(k):
        return remote(sn.at[piece(k)], start.at[piece(k)], s_fs.at[k], s_fr.at[k], (gi, lax.rem(c + 1, n_ctx), f, h))

    def b_copy(k):
        return remote(
            sp.at[piece(k)], endg.at[piece(k)], s_bs.at[k], s_br.at[k], (gi, lax.rem(c + n_ctx - 1, n_ctx), f, h)
        )

    def forward(k):
        @pl.when(jnp.logical_not(first))
        def _():
            f_copy(k).wait_recv()

        at = piece(k)
        e = dot(tx[:, at], lastb[...], 0, 0)
        sn[at, :] = (e + thrc[at, :] * start[at, :].astype(F32)).astype(BF)

        @pl.when(jnp.logical_not(last_c))
        def _():
            f_copy(k).start()

    def backward(k):
        @pl.when(jnp.logical_not(last_c))
        def _():
            b_copy(k).wait_recv()

        at = piece(k)
        e = dot(ag[:, at], alivec[...], 0, 0)
        sp[at, :] = (e + thrc[at, :] * endg[at, :].astype(F32)).astype(BF)

        @pl.when(jnp.logical_not(first))
        def _():
            b_copy(k).start()

    row_n = lax.broadcasted_iota(jnp.int32, (T, NC), 0)
    row_8 = lax.broadcasted_iota(jnp.int32, (8, NC), 0)

    def transposed_conv(d_pre, taps):
        own = taps[3:4, :] * d_pre
        rim = jnp.zeros((8, NC), F32)
        for d in range(1, 4):
            z = pltpu.roll(taps[3 - d : 4 - d, :] * masks[3 - d] * d_pre, T - d, 0)
            own += jnp.where(row_n < T - d, z, 0.0)
            rim += jnp.where(row_8 < 8 - d, 0.0, z[T - 8 :])
        return own, rim

    def collect(k):
        at = chunk(k)
        db_acc[...] += dot(tx[:, at], endg[at, :], 1, 0)
        dc_acc[...] += dot(ag[:, at], start[at, :], 1, 0)

    def finish(k):
        at = chunk(k)
        taps = tapx_ref[:, at]
        sel = spread(k)
        sm = sm_ref[...]
        a_w, b_w = aw[:, at], bw[:, at]
        gf = gv[:, at].astype(F32)
        b_x, a_g = bx[:, at], ag[:, at]
        st, en = start[at, :], endg[at, :]
        y = dot(sm, b_x, 1, 0) + dot(alivec[...], st, 1, 1)
        r_acc[...] += narrow(a_w * gf * y, sel)
        d_xt = b_w * (dot(sm, a_g, 0, 0) + a_w[T - 1 :, :] * dot(lastb[...], en, 1, 1))
        q_acc[...] += narrow(xf[:, at] * d_xt, sel)
        prod = en.astype(F32) * sn[at, :].astype(F32)
        hi, mid, _ = pieces(prod)
        ones8 = jnp.ones((8, 128), BF)
        l_acc[...] += narrow(dot(ones8, hi, 1, 1) + dot(ones8, mid, 1, 1), sel)
        skip_w = widen(jnp.broadcast_to(skip_ref[...], (8, heads)), sel)[:1]
        d_pre = (dtw[:, at] * d_xt + skip_w * gf) * dsf[:, at]
        own, rim = transposed_conv(d_pre, taps)
        gxs[:, at] = own.astype(BF)
        gxtail[:, at] = own[T - HI :]
        rimx_s[:, at] = rim

    inner = jnp.logical_and(c > 0, c < n_ctx - 1)
    pieces_n = W // CH
    group = NC // CH
    offset = jnp.where(inner, LAG, pieces_n)
    early = c < n_ctx // 2

    def lead(k, z):
        @pl.when(early)
        def _():
            forward(k)

        @pl.when(jnp.logical_not(early))
        def _():
            backward(k)

        return z

    def scores():
        same_f = same_ref[...] > 0.5
        sm_ref[...] = jnp.where(same_f, dot(c_own, b_own, 1, 1, EXACT), 0.0).astype(BF)
        d_sm = jnp.where(same_f, ds_acc[...], 0.0)
        dps[:, :STATE] = dot(d_sm, c_own, 0, 0, EXACT)
        dps[:, STATE:] = dot(d_sm, b_own, 1, 0, EXACT)

    def step(k, z):
        @pl.when(k + offset < pieces_n)
        def _():
            lead(k + offset, 0)

        @pl.when(early)
        def _():
            backward(k)

        @pl.when(jnp.logical_not(early))
        def _():
            forward(k)

        @pl.when(lax.rem(k, group) == group - 1)
        def _():
            collect(k // group)

            @pl.when(k >= group)
            def _():
                finish(k // group - 1)

        return z

    lax.fori_loop(0, jnp.where(inner, 0, offset), lead, 0)
    scores()
    lax.fori_loop(0, jnp.where(inner, offset, 0), lead, 0)
    lax.fori_loop(0, pieces_n, step, 0)

    rimx = remote(rimx_s, rimx_r, s_rim.at[0], s_rim.at[1], (gi, lax.rem(c + n_ctx - 1, n_ctx), f, h))

    alive, last = alive_ref[...], last_ref[...]
    d_bcc = jnp.concatenate([last * db_acc[...], alive * dc_acc[...]], axis=1)
    dps[...] = (dps[...] + d_bcc) * silu_bc[...]
    d_swap = remote(dps, dpsr, s_ds.at[0], s_dr, (gi, c, f, 1 - h))
    d_swap.start()
    d_rims = [
        remote(
            dps.at[:8], rims.at[h], s_ds.at[1 + o], s_rr.at[h],
            (gi, lax.rem(c + n_ctx - 1, n_ctx), f, lax.rem(h + o, 2)),
        )
        for o in range(2)
    ]

    @pl.when(jnp.logical_not(first))
    def _():
        for p in d_rims:
            p.start()

    finish(chunks - 1)

    d_swap.wait_recv()

    @pl.when(jnp.logical_not(last_c))
    def _():
        for o in range(2):
            remote(dps.at[:8], rims.at[o], s_ds.at[1], s_rr.at[o], (gi, c, f, 1 - h)).wait_recv()

    own, _ = transposed_conv(dps[...] + dpsr[...], taps_b)
    rim_in = rims[0] + rims[1]
    row8 = lax.broadcasted_iota(jnp.int32, (8, 2 * STATE), 0)
    npos = pos0 + T + row8
    nseg = segment(npos)
    rim = jnp.zeros((8, 2 * STATE), F32)
    for d in range(1, 4):
        mask = (segment(npos - d) == nseg).astype(F32)
        z = pltpu.roll(taps_b[3 - d : 4 - d, :] * mask * rim_in, 8 - d, 0)
        rim += jnp.where(row8 < 8 - d, 0.0, z)
    d_bc = jnp.concatenate([own[: T - 8], own[T - 8 :] + rim]).astype(BF)
    dall[me] = d_bc

    half = pl.ds(pl.multiple_of(h * (T // 2), T // 2), T // 2)
    other = pl.ds(pl.multiple_of((1 - h) * (T // 2), T // 2), T // 2)

    def z_copy(d):
        return remote(
            dall.at[me, half], dall.at[me, half], s_zs.at[d], s_zr.at[me], (gi, lax.rem(c + d, n_ctx), f, h)
        )

    def x_copy(cc):
        b = cc * 2 + f
        return remote(dall.at[b, half], dall.at[b, half], s_xs.at[cc], s_xr.at[cc], (gi, c, 1 - f, h))

    def c_copy(b):
        return remote(dall.at[b, half], dall.at[b, half], s_cs.at[b], s_cr.at[b], (gi, c, f, 1 - h))

    def from_z(cc):
        b = cc * 2 + f
        return remote(dall.at[b, half], dall.at[b, half], s_zs.at[0], s_zr.at[b], (gi, c, f, 1 - h))

    def from_x(cc):
        b = cc * 2 + 1 - f
        return remote(dall.at[b, half], dall.at[b, half], s_xs.at[0], s_xr.at[cc], (gi, c, f, 1 - h))

    def from_c(b):
        return remote(dall.at[b, other], dall.at[b, other], s_cs.at[0], s_cr.at[b], (gi, c, f, 1 - h))

    left = c < n_ctx // 2
    nearest = [c + 1 - 2 * lax.rem(c, 2), jnp.where(left, 2, 1), jnp.where(left, 3, 0)]
    x_copy(c).start()
    for cc in nearest[::-1]:
        z_copy(lax.rem(cc - c + n_ctx, n_ctx)).start()

    @pl.when(jnp.logical_not(first))
    def _():
        rimx.start()

    def grad_u(k, z):
        at = w_rows(k)
        gus[:, at] = dot(dall[me], wh[at], 1, 1).astype(BF)
        return z

    parts = 2 * chunks
    marks = [parts // 2, parts * 11 // 16, parts * 7 // 8, parts]
    lax.fori_loop(0, marks[0], grad_u, 0)
    from_x(c).wait_recv()
    c_copy(c * 2 + 1 - f).start()
    for i, cc in enumerate(nearest):
        from_z(cc).wait_recv()
        x_copy(cc).start()
        c_copy(cc * 2 + f).start()
        lax.fori_loop(marks[i], marks[i + 1], grad_u, 0)
    u_out = pltpu.make_async_copy(gus, gu_out, s_out.at[0])
    u_out.start()

    total_q = q_acc[...]
    dts = small[0]
    at_end = row[:, :heads] == T - 1
    d_cum = r_acc[...] - dts * total_q + jnp.where(at_end, l_acc[:1, :], 0.0)
    d_log = dot(tri, d_cum, 0, 0, EXACT)
    ddt_ref[...] = ((total_q - decay_ref[...] * d_log) * jax.nn.sigmoid(small[3])).T
    t_out = pltpu.make_async_copy(ddt_ref, ddt_out, s_out.at[3])
    t_out.start()

    for cc in nearest:
        from_x(cc).wait_recv()
        c_copy(cc * 2 + 1 - f).start()

    @pl.when(jnp.logical_not(last_c))
    def _():
        rimx.wait_recv()

    fixed = gxtail[HI - 8 :, :] + rimx_r[...]
    gxs[T - HI :, :] = jnp.concatenate([gxtail[: HI - 8, :], fixed]).astype(BF)
    x_out = pltpu.make_async_copy(gxs, gx_out, s_out.at[1])
    x_out.start()

    def h_wait(b):
        remote(hall.at[b], hall.at[b], s_hs.at[0], s_hr.at[b], (gi, c, f, 1 - h)).wait_recv()

    own_load.wait()
    for d in range(1, n_ctx):
        b = lax.rem(c + d, n_ctx) * 2 + f
        from_c(b).wait_recv()
        h_wait(b)
    for d in range(n_ctx):
        b = lax.rem(c + d, n_ctx) * 2 + 1 - f
        from_c(b).wait_recv()
        h_wait(b)
    gws[...] = dot(
        hall[...].reshape(2 * n_ctx * T, wb), dall[...].reshape(2 * n_ctx * T, 2 * STATE), 0, 0
    )
    w_out = pltpu.make_async_copy(gws, gw_out, s_out.at[2])
    w_out.start()

    @pl.when(needing)
    def _():
        w_all(w_forward, "wait_send")

    @pl.when(jnp.logical_not(last_c))
    def _():
        halo_copy.wait_send()
        for p in p_tails:
            p.wait_send()
        lax.fori_loop(0, W // CH, lambda k, z: (f_copy(k).wait_send(), z)[1], 0)

    @pl.when(jnp.logical_not(first))
    def _():
        for p in d_rims:
            p.wait_send()
        rimx.wait_send()
        lax.fori_loop(0, W // CH, lambda k, z: (b_copy(k).wait_send(), z)[1], 0)

    p_swap.wait_send()
    d_swap.wait_send()
    for d in range(n_ctx):
        h_send(d, 1 - f).wait_send()
        x_copy(lax.rem(c + d, n_ctx)).wait_send()
        c_copy(lax.rem(c + d, n_ctx) * 2 + 1 - f).wait_send()
        if d:
            h_send(d, f).wait_send()
            z_copy(d).wait_send()
            c_copy(lax.rem(c + d, n_ctx) * 2 + f).wait_send()
    u_out.wait()
    x_out.wait()
    w_out.wait()
    t_out.wait()


def fused(hidden, w, x, g, raw, decay, skip, tapx, tapb, spans):
    T, W = x.shape
    DH = hidden.shape[1]
    n_ctx = lax.axis_size("ctx")
    blocks = 2 * n_ctx
    wb = DH // blocks
    heads = raw.shape[0]
    K = W // CH
    U = W // NC
    vm, dma = pltpu.VMEM, pltpu.SemaphoreType.DMA
    spec = pl.BlockSpec
    hbm = spec(memory_space=pltpu.HBM)
    out = spec(memory_space=pl.ANY)
    S2 = 2 * STATE
    return pl.pallas_call(
        fused_kernel,
        out_shape=(
            jax.ShapeDtypeStruct((T, W), BF),
            jax.ShapeDtypeStruct((T, DH), BF),
            jax.ShapeDtypeStruct((heads, T), F32),
            jax.ShapeDtypeStruct((wb, S2), F32),
        ),
        in_specs=[hbm] * 10,
        out_specs=(out,) * 4,
        scratch_shapes=[
            vm((heads, T), F32), vm((1, heads), F32), vm((1, heads), F32), vm((4, W), F32), vm((4, S2), F32),
            pltpu.SMEM(spans.shape, jnp.int32), vm((heads, T), F32),
            vm((T, W), BF), vm((T, W), BF), vm((T, DH), BF), vm((DH, S2), BF), vm((HI, W), BF),
            vm((T, W), F32), vm((T, W), F32), vm((T, W), F32), vm((T, W), F32), vm((T, W), F32),
            vm((T, W), BF), vm((T, W), BF), vm((T, W), BF), vm((W, STATE), F32),
            vm((W, STATE), BF), vm((W, STATE), BF), vm((W, STATE), BF), vm((W, STATE), BF),
            vm((3, T, S2), F32), vm((T, STATE), F32), vm((T, STATE), F32), vm((T, STATE), F32),
            vm((4, T, heads), F32), vm((T, T), F32), vm((T, S2), F32), vm((T, S2), F32), vm((2, 8, S2), F32),
            vm((T, S2), F32), vm((T, T), BF), vm((T, STATE), BF), vm((T, STATE), BF),
            vm((T, STATE), F32), vm((T, STATE), F32), vm((T, S2), F32), vm((T, S2), F32), vm((2, 8, S2), F32),
            vm((8, W), F32), vm((8, W), F32), vm((HI, W), F32),
            vm((T, heads), F32), vm((T, heads), F32), vm((8, heads), F32),
            vm((blocks, T, wb), BF), vm((blocks, T, S2), BF),
            vm((T, W), BF), vm((T, DH), BF), vm((wb, S2), F32),
            dma((5,)), dma((U,)), dma((U,)), dma((U,)), dma((U,)), dma((blocks,)), dma((blocks,)), dma((2,)),
            dma((K,)), dma((K,)), dma((K,)), dma((K,)),
            dma((3,)), dma, dma((2,)), dma((3,)), dma, dma((2,)), dma((2,)),
            dma((n_ctx,)), dma((blocks,)), dma((n_ctx,)), dma((n_ctx,)), dma((blocks,)), dma((blocks,)), dma((6,)), dma((4,)),
        ],
        compiler_params=pltpu.CompilerParams(
            collective_id=0, has_side_effects=True, vmem_limit_bytes=60 << 20
        ),
        cost_estimate=pl.CostEstimate(
            flops=2 * T * 256 * (W * 9 + DH * 4), bytes_accessed=8 << 20, transcendentals=4 * T * W
        ),
    )(hidden, w, x, g, raw, decay, skip, tapx, tapb, spans)


def publish_kernel(*refs):
    n = (len(refs) - 2) // 3
    ins, outs, held, in_sem, out_sem = refs[:n], refs[n : 2 * n], refs[2 * n : 3 * n], refs[-2], refs[-1]
    loads, stores = [], []
    for i in range(n):
        rows = ins[i].shape[0] // PUB
        for j in range(PUB):
            at = pl.ds(j * rows, rows)
            loads.append(pltpu.make_async_copy(ins[i].at[at], held[i].at[at], in_sem.at[i, j]))
            stores.append(pltpu.make_async_copy(held[i].at[at], outs[i].at[at], out_sem.at[i, j]))
    for copy in loads:
        copy.start()
    for load, store in zip(loads, stores):
        load.wait()
        store.start()
    for copy in stores:
        copy.wait()


def publish(arrays):
    n = len(arrays)
    hbm = pl.BlockSpec(memory_space=pl.ANY)
    return pl.pallas_call(
        publish_kernel,
        out_shape=tuple(jax.ShapeDtypeStruct(a.shape, a.dtype) for a in arrays),
        in_specs=[hbm] * n,
        out_specs=(hbm,) * n,
        scratch_shapes=[pltpu.VMEM(a.shape, a.dtype) for a in arrays]
        + [pltpu.SemaphoreType.DMA((n, PUB)), pltpu.SemaphoreType.DMA((n, PUB))],
        compiler_params=pltpu.CompilerParams(vmem_limit_bytes=60 << 20),
    )(*arrays)


def on_device(
    hidden_in, w_bc, x_in, dt_raw, decay_rate, conv_x, conv_bc, skip_gain, span_len, grad_y
):
    T = x_in.shape[1]
    hidden = hidden_in[0]
    half_width = hidden.shape[1]
    n_ctx, n_fsdp, n_head = (lax.axis_size(a) for a in ("ctx", "fsdp", "head"))
    assert T * 2 == MOST and dt_raw.shape[2] == 32
    x0, g0, raw0 = x_in[0], grad_y[0], dt_raw[0]
    if (lax.axis_size("groups"), n_ctx, n_fsdp, n_head) == (2, 4, 2, 2):
        outs = fused(
            hidden, w_bc, x0, g0, raw0.T, decay_rate[None, :], skip_gain[None, :], conv_x, conv_bc, span_len
        )
        outs = publish(outs)
        return (outs[0][None], outs[1][None], outs[2].T[None], outs[3][None])
    if n_fsdp == n_head:
        route = [(f * n_head + h, h * n_head + f) for f in range(n_fsdp) for h in range(n_head)]
        w_half = lax.ppermute(w_bc, ("fsdp", "head"), route)
    else:
        w_full = lax.all_gather(w_bc, "fsdp", axis=0, tiled=True)
        w_half = lax.dynamic_slice_in_dim(
            w_full, lax.axis_index("head") * half_width, half_width, 0
        )
    raws = [shifted(raw0, "ctx", d) for d in (2, 1)] + [raw0] + [shifted(raw0, "ctx", -d) for d in (1, 2)]
    x1, g1 = shifted(x0, "ctx", 1), shifted(g0, "ctx", -1)
    x2, g2 = shifted(x0, "ctx", 2), shifted(g0, "ctx", -2)

    swap = [(i, (i + 1) % n_head) for i in range(n_head)]
    partial_bc = jnp.dot(hidden, w_half, preferred_element_type=F32)
    bc_pre = (partial_bc + lax.ppermute(partial_bc, "head", swap)).astype(BF)
    bcs = [shifted(bc_pre, "ctx", d) for d in (2, 1)] + [bc_pre] + [shifted(bc_pre, "ctx", -d) for d in (1, 2)]

    n_blocks = n_ctx * n_fsdp
    blocks = hidden.reshape(T, n_blocks, half_width // n_blocks).transpose(1, 0, 2)
    hidden_all = lax.all_to_all(blocks, ("ctx", "fsdp"), 0, 0, tiled=True)

    position = (lax.axis_index("ctx") - 2) * T + jnp.arange(-3, 5 * T, dtype=jnp.int32)
    spans = span_len.shape[1]
    earlier = jnp.arange(spans)[:, None] <= jnp.arange(spans)[None, :]
    span_ends = jnp.sum(jnp.where(earlier, span_len[0][:, None], 0), axis=0)
    counted = jnp.sum((span_ends[None, :] <= position[:, None]).astype(jnp.int32), axis=1)
    segment = jnp.where(position >= 0, counted, -1).astype(F32)
    own_seg = segment[3:]
    by_block = own_seg.reshape(5, T)
    before = jnp.broadcast_to(segment[2 : 2 + 5 * T : T][:, None], (5, T)).reshape(-1)
    last = jnp.broadcast_to(by_block[:, T - 1 :], (5, T)).reshape(-1)
    info = jnp.stack(
        [(segment[k : k + 5 * T] == own_seg).astype(F32) for k in range(3)]
        + [(own_seg == before).astype(F32), (own_seg == last).astype(F32), own_seg],
        axis=1,
    )
    segrow = by_block[2:3]
    raw = jnp.tile(jnp.concatenate(raws), (1, 4))
    decay = jnp.tile(decay_rate, 4)[None, :]
    skip = jnp.repeat(skip_gain, HEAD)[None, :]

    dx, tail, rim, dbc, rimbc, ddt = ssm(
        (x2, x1, x0), (g0, g1, g2), bcs, raw, info, segrow, decay, skip, conv_x, conv_bc
    )
    back = shifted(rim, "ctx", -1)
    grad_x = lax.dynamic_update_slice(dx, (tail + back).astype(BF), (T - 8, 0))

    other = lax.ppermute(dbc, "head", swap)
    rim_same = shifted(rimbc, "ctx", -1)
    cross = [
        (c * n_head + h, (c - 1) * n_head + (h + 1) % n_head)
        for c in range(1, n_ctx)
        for h in range(n_head)
    ]
    rim_cross = lax.ppermute(rimbc, ("ctx", "head"), cross)
    d_bc = ((dbc + other) + jnp.pad(rim_same + rim_cross, ((T - 8, 0), (0, 0)))).astype(BF)
    grad_u = lax.dot_general(
        d_bc, w_half, (((1,), (1,)), ((), ())), preferred_element_type=F32
    ).astype(BF)
    d_all = lax.all_gather(d_bc, ("ctx", "fsdp"), axis=0)
    grad_w = lax.dot_general(
        hidden_all.reshape(n_blocks * T, -1),
        d_all.reshape(n_blocks * T, -1),
        (((0,), (0,)), ((), ())),
        preferred_element_type=F32,
    )
    return (grad_x[None], grad_u[None], ddt[None], grad_w[None])


def solution(mesh):
    return jax.shard_map(
        on_device,
        mesh=mesh,
        in_specs=(
            P(("groups", "fsdp"), "ctx", "head"),
            P("fsdp", None),
            P(("groups", "fsdp"), "ctx", "head"),
            P(("groups", "fsdp"), "ctx", "head"),
            P("head"),
            P(None, "head"),
            P(),
            P("head"),
            P(("groups", "fsdp"), None),
            P(("groups", "fsdp"), "ctx", "head"),
        ),
        out_specs=(
            P(("groups", "fsdp"), "ctx", "head"),
            P(("groups", "fsdp"), "ctx", "head"),
            P(("groups", "fsdp"), "ctx", "head"),
            P(("groups", "head"), ("ctx", "fsdp"), None),
        ),
        check_vma=False,
    )
```

```python
import jax
import jax.numpy as jnp
from jax import lax
from jax.experimental import pallas as pl
from jax.experimental.pallas import tpu as pltpu
from jax.sharding import PartitionSpec as P

STATE = 128
HEAD = 64
MOST = 256
BF = jnp.bfloat16
F32 = jnp.float32
EXACT = lax.Precision.HIGHEST


def shifted(block, axis, distance):
    devices = range(lax.axis_size(axis))
    route = [(i - distance, i) for i in devices if i - distance in devices]
    return lax.ppermute(block, axis, route)


def dot(a, b, ca, cb, precision=None):
    return lax.dot_general(
        a, b, (((ca,), (cb,)), ((), ())), precision=precision, preferred_element_type=F32
    )


def ssm_kernel(
    x2, x1, x0, g0, g1, g2, b2, b1, b0, b3, b4, raw_ref, info_ref, segrow_ref,
    decay_ref, skip_ref, tapx_ref, tapb_ref,
    dx_ref, tail_ref, rim_ref, dbc_ref, rimbc_ref, ddt_ref,
    masks, bias_ref, s_ref, cols_a, cols_b, cum_rows, bprev, cnext, bown, cown,
    silu_bc, d_s, d_b, d_c, acc,
):
    T = x0.shape[0]
    pairs = x0.shape[1] // 128
    lane = lax.broadcasted_iota(jnp.int32, (T, 128), 1)
    row = lax.broadcasted_iota(jnp.int32, (T, 128), 0)
    low = lane < HEAD
    group = lane // 32
    info = info_ref[...]
    for k in range(3):
        masks[k] = jnp.broadcast_to(info[: 3 * T, k : k + 1], (3 * T, 128))

    def col(block, k):
        return info[block * T : (block + 1) * T, k : k + 1]

    tri = (row >= lane).astype(F32)
    decay = decay_ref[...]
    dts, cums, carried, toward = [], [], [], []
    for j in range(5):
        raw = raw_ref[j * T : (j + 1) * T, :]
        dt = jnp.maximum(raw, 0.0) + jnp.log1p(jnp.exp(-jnp.abs(raw)))
        cum = dot(tri, -dt * decay, 1, 0, EXACT)
        dts.append(dt)
        cums.append(cum)
        carried.append(jnp.exp(cum) * col(j, 3))
        toward.append(jnp.exp(cum[T - 1 :, :] - cum) * col(j, 4))
    a1 = dts[1] * toward[1]
    a2 = dts[0] * toward[0] * carried[1][T - 1 :, :]
    c1 = carried[3]
    c2 = carried[4] * carried[3][T - 1 :, :]

    def packed(p, q, r, s):
        return jnp.where(group == 0, p, jnp.where(group == 1, q, jnp.where(group == 2, r, s)))

    cols_a[...] = packed(dts[2], cums[2], carried[2], toward[2])
    cols_b[...] = packed(a2, a1, c1, c2)
    cum_rows[...] = cums[2].T
    same = col(2, 5) == segrow_ref[...]
    bias_ref[...] = jnp.where(same & (row >= lane), 0.0, -1e30)

    taps_b = tapb_ref[...]
    bc = jnp.concatenate([b2[...], b1[...], b0[...], b3[...], b4[...]]).astype(F32)
    pre_bc = taps_b[3:4, :] * bc
    for k in range(3):
        pre_bc += taps_b[k : k + 1, :] * pltpu.roll(bc, 3 - k, 0) * info[:, k : k + 1]
    sig_bc = jax.nn.sigmoid(pre_bc)
    conv_bc = pre_bc * sig_bc
    own_sig = sig_bc[2 * T : 3 * T]
    silu_bc[...] = own_sig * (1.0 + pre_bc[2 * T : 3 * T] * (1.0 - own_sig))
    bprev[...] = conv_bc[: 2 * T, :STATE].astype(BF)
    cnext[...] = conv_bc[3 * T :, STATE:].astype(BF)
    bown[...] = conv_bc[2 * T : 3 * T, :STATE]
    cown[...] = conv_bc[2 * T : 3 * T, STATE:]
    s_ref[...] = dot(cown[...], bown[...], 1, 1, EXACT)
    d_s[...] = jnp.zeros_like(d_s)
    d_b[...] = jnp.zeros_like(d_b)
    d_c[...] = jnp.zeros_like(d_c)
    acc[...] = jnp.zeros_like(acc)

    def pair(i, carry):
        at = pl.ds(pl.multiple_of(i * 128, 128), 128)
        ca = pltpu.roll(cols_a[...], (128 - 2 * i) % 128, 1)
        cb = pltpu.roll(cols_b[...], (128 - 2 * i) % 128, 1)

        def wide(c, q):
            return jnp.where(low, c[:, 32 * q : 32 * q + 1], c[:, 32 * q + 1 : 32 * q + 2])

        def tall(c, q):
            return c[:, 32 * q : 32 * q + 1], c[:, 32 * q + 1 : 32 * q + 2]

        taps = tapx_ref[:, at]
        xe = jnp.concatenate([x2[:, at], x1[:, at], x0[:, at]]).astype(F32)
        pre = taps[3:4, :] * xe
        for k in range(3):
            pre += taps[k : k + 1, :] * pltpu.roll(xe, 3 - k, 0) * masks[k]
        sig = jax.nn.sigmoid(pre)
        xc = pre * sig
        xown = xc[2 * T :]
        sown = sig[2 * T :]
        dsilu = sown * (1.0 + pre[2 * T :] * (1.0 - sown))
        dt_w = wide(ca, 0)
        toward_w = wide(ca, 3)
        xw = jnp.concatenate([xc[:T] * wide(cb, 0), xc[T : 2 * T] * wide(cb, 1)]).astype(BF)
        start = dot(xw, bprev[...], 0, 0)
        gw = jnp.concatenate(
            [g1[:, at].astype(F32) * wide(cb, 2), g2[:, at].astype(F32) * wide(cb, 3)]
        ).astype(BF)
        end_grad = dot(gw, cnext[...], 0, 0)
        start_b = start.astype(BF)
        end_b = end_grad.astype(BF)
        gy = g0[:, at].astype(F32)
        gg = jnp.concatenate([jnp.where(low, gy, 0.0), jnp.where(low, 0.0, gy)]).astype(BF)
        xt = xown * dt_w
        xt_b = xt.astype(BF)
        xx = jnp.concatenate([jnp.where(low, xt, 0.0), jnp.where(low, 0.0, xt)]).astype(BF)
        d_m = dot(gg, xt_b, 1, 1)
        cum_a, cum_b = tall(ca, 1)
        bias = bias_ref[...]
        decay_t = jnp.concatenate(
            [
                jnp.exp(cum_a - cum_rows[pl.ds(2 * i, 1), :] + bias),
                jnp.exp(cum_b - cum_rows[pl.ds(2 * i + 1, 1), :] + bias),
            ]
        )
        s_all = s_ref[...]
        s_two = jnp.concatenate([s_all, s_all])
        ls = decay_t * s_two
        ldm = decay_t * d_m
        d_s[...] += ldm[:T] + ldm[T:]
        d_x = dot(ls.astype(BF), gg, 0, 0)
        car = jnp.concatenate(tall(ca, 2))
        tow = jnp.concatenate(tall(ca, 3))
        c_u = car * dot(gg, start_b, 1, 0)
        d_c[...] += c_u[:T] + c_u[T:]
        c_own = cown[...]
        c_two = jnp.concatenate([c_own, c_own])
        r = jnp.sum(ldm * s_two + c_u * c_two, axis=1, keepdims=True)
        t_v = tow * dot(xx, end_b, 1, 0)
        d_b[...] += t_v[:T] + t_v[T:]
        d_xe = dot(bown[...].astype(BF), end_b, 1, 1) * toward_w
        d_xt = d_x + d_xe
        prod = xown * d_xt
        q_a = jnp.sum(jnp.where(low, prod, 0.0), axis=1, keepdims=True)
        q_b = jnp.sum(jnp.where(low, 0.0, prod), axis=1, keepdims=True)
        ends = jnp.sum(xt * d_xe, axis=0, keepdims=True)
        inner = end_grad * start
        low_row = low[:1]
        through_a, through_b = (v[T - 1 :, :] for v in tall(ca, 2))
        last_a = jnp.sum(jnp.where(low_row, ends, 0.0), axis=1, keepdims=True) + through_a * jnp.sum(
            jnp.sum(inner[:HEAD], axis=0, keepdims=True), axis=1, keepdims=True
        )
        last_b = jnp.sum(jnp.where(low_row, 0.0, ends), axis=1, keepdims=True) + through_b * jnp.sum(
            jnp.sum(inner[HEAD:], axis=0, keepdims=True), axis=1, keepdims=True
        )
        dt_a, dt_b = tall(ca, 0)
        final = row[:, :1] == T - 1
        cum_ga = r[:T] - dt_a * q_a + jnp.where(final, last_a, 0.0)
        cum_gb = r[T:] - dt_b * q_b + jnp.where(final, last_b, 0.0)
        placed = jnp.where(
            lane == 0,
            q_a,
            jnp.where(
                lane == 1, q_b, jnp.where(lane == 32, cum_ga, jnp.where(lane == 33, cum_gb, 0.0))
            ),
        )
        acc[...] += pltpu.roll(placed, 2 * i, 1)
        d_pre = (dt_w * d_xt + skip_ref[:, at] * gy) * dsilu
        own = taps[3:4, :] * d_pre
        rim = jnp.zeros((8, 128), F32)
        for k in range(3):
            d = 3 - k
            z = pltpu.roll(taps[k : k + 1, :] * masks[k, 2 * T :] * d_pre, T - d, 0)
            own += jnp.where(row < T - d, z, 0.0)
            rim += jnp.where(row[T - 8 :] < T - d, 0.0, z[T - 8 :])
        dx_ref[:, at] = own.astype(BF)
        tail_ref[:, at] = own[T - 8 :]
        rim_ref[:, at] = rim
        return carry

    lax.fori_loop(0, pairs, pair, 0)

    ds = d_s[...]
    full_c = d_c[...] + dot(ds, bown[...], 1, 0, EXACT)
    full_b = d_b[...] + dot(ds, cown[...], 0, 0, EXACT)
    d_pre = jnp.concatenate([full_b, full_c], axis=1) * silu_bc[...]
    own = taps_b[3:4, :] * d_pre
    rim = jnp.zeros((8, 2 * STATE), F32)
    row2 = lax.broadcasted_iota(jnp.int32, (T, 2 * STATE), 0)
    for k in range(3):
        d = 3 - k
        z = pltpu.roll(taps_b[k : k + 1, :] * info[2 * T : 3 * T, k : k + 1] * d_pre, T - d, 0)
        own += jnp.where(row2 < T - d, z, 0.0)
        rim += jnp.where(row2[T - 8 :] < T - d, 0.0, z[T - 8 :])
    dbc_ref[...] = own
    rimbc_ref[...] = rim
    total = acc[...]
    d_log = pltpu.roll(dot(tri, total, 0, 0, EXACT), 96, 1)
    raw = raw_ref[2 * T : 3 * T, :]
    ddt_ref[...] = ((total - decay * d_log) * jax.nn.sigmoid(raw))[:, :32]


def ssm(xs, gs, bcs, raw, info, segrow, decay, skip, tapx, tapb):
    T, W = xs[0].shape
    vm = pltpu.VMEM
    return pl.pallas_call(
        ssm_kernel,
        out_shape=(
            jax.ShapeDtypeStruct((T, W), BF),
            jax.ShapeDtypeStruct((8, W), F32),
            jax.ShapeDtypeStruct((8, W), F32),
            jax.ShapeDtypeStruct((T, 2 * STATE), F32),
            jax.ShapeDtypeStruct((8, 2 * STATE), F32),
            jax.ShapeDtypeStruct((T, 32), F32),
        ),
        scratch_shapes=[
            vm((3, 3 * T, 128), F32), vm((T, T), F32), vm((T, T), F32), vm((T, 128), F32),
            vm((T, 128), F32), vm((128, T), F32), vm((2 * T, STATE), BF), vm((2 * T, STATE), BF),
            vm((T, STATE), F32), vm((T, STATE), F32), vm((T, 2 * STATE), F32),
            vm((T, T), F32), vm((T, STATE), F32), vm((T, STATE), F32), vm((T, 128), F32),
        ],
        compiler_params=pltpu.CompilerParams(vmem_limit_bytes=40 << 20),
        cost_estimate=pl.CostEstimate(
            flops=2 * 9 * T * 256 * W, bytes_accessed=8 * T * W * 2, transcendentals=6 * T * W
        ),
    )(*xs, *gs, *bcs, raw, info, segrow, decay, skip, tapx, tapb)


MESH = pl.DeviceIdType.MESH
NC = 256
HI = 16
CH = 256
LAG = 3
YLAG = 4
PUB = 2


def pieces(v):
    hi = v.astype(BF)
    rest = v - hi.astype(F32)
    mid = rest.astype(BF)
    lo = (rest - mid.astype(F32)).astype(BF)
    return hi, mid, lo


def fused_kernel(
    hidden, w, x, g, raw_in, decay_in, skip_in, tapx_in, tapb_in, span_in,
    gx_out, gu_out, ddt_out, gw_out,
    raw_ref, decay_ref, skip_ref, tapx_ref, tapb_ref, span_ref, ddt_ref,
    xv, gv, hv, wh, xhalo, xf, dsf, aw, bw, dtw, bx, tx, ag, thrc, start, endg, sn, sp,
    masks, same_ref, alive_ref, last_ref, small, ds_acc, part, partr, tails, silu_bc,
    sm_ref, lastb, alivec, db_acc, dc_acc, dps, dpsr, rims, rimx_s, rimx_r, gxtail, r_acc, q_acc, l_acc,
    hall, dall, gxs, gus, gws,
    s_loc, s_ws, s_wr, s_ys, s_yr, s_hs, s_hr, s_halo, s_fs, s_fr, s_bs, s_br,
    s_ps, s_pr, s_tr, s_ds, s_dr, s_rr, s_rim, s_zs, s_zr, s_xs, s_xr, s_cs, s_cr, s_small, s_out,
):
    T, W = gxs.shape
    gi, c, f, h = (lax.axis_index(a) for a in ("groups", "ctx", "fsdp", "head"))
    n_ctx = lax.axis_size("ctx")
    DH = hv.shape[1]
    chunks = W // NC
    wrows = wh.shape[0] // 2 // chunks
    heads = raw_ref.shape[0]
    wb = hall.shape[2]
    first, last_c = c == 0, c == n_ctx - 1
    needing = h != f
    me = c * 2 + f

    def remote(src, dst, ss, rs, device):
        return pltpu.make_async_remote_copy(
            src_ref=src, dst_ref=dst, send_sem=ss, recv_sem=rs, device_id=device, device_id_type=MESH
        )

    smalls = [
        pltpu.make_async_copy(src, dst, s_small.at[i])
        for i, (src, dst) in enumerate(
            (
                (span_in, span_ref), (raw_in, raw_ref), (decay_in, decay_ref), (skip_in, skip_ref),
                (tapx_in, tapx_ref), (tapb_in, tapb_ref),
            )
        )
    ]
    for copy in smalls:
        copy.start()
    barrier = pltpu.get_barrier_semaphore()
    for o in range(1, 4 * n_ctx):
        oc, of, oh = o // 4, (o // 2) % 2, o % 2
        pl.semaphore_signal(
            barrier, 1, device_id=(gi, lax.rem(c + oc, n_ctx), lax.rem(f + of, 2), lax.rem(h + oh, 2)),
            device_id_type=MESH,
        )
    pl.semaphore_signal(barrier, 1, device_id=(1 - gi, c, f, h), device_id_type=MESH)
    pl.semaphore_wait(barrier, 4 * n_ctx)

    def w_rows(k):
        return pl.ds(pl.multiple_of(k * wrows, wrows), wrows)

    def w_rows(k):
        return pl.ds(pl.multiple_of(k * wrows, wrows), wrows)

    def w_send(k):
        at = w_rows(gi * chunks + k)
        return remote(w.at[at], wh.at[at], s_ws.at[k], s_wr.at[k], (gi, c, 1 - f, h))

    def w_forward(k):
        at = w_rows(gi * chunks + k)
        return remote(wh.at[at], wh.at[at], s_ys.at[k], s_yr.at[k], (1 - gi, c, f, h))

    def w_all(copy, act):
        lax.fori_loop(0, chunks, lambda k, z: (getattr(copy(k), act)(), z)[1], 0)

    def h_send(d, ff):
        cc = lax.rem(c + d, n_ctx)
        at = pl.ds(pl.multiple_of((cc * 2 + ff) * wb, wb), wb)
        return remote(
            hidden.at[:, at], hall.at[me], s_hs.at[d + n_ctx * (1 if ff is not f else 0)], s_hr.at[me], (gi, cc, ff, h)
        )

    halo_copy = remote(
        x.at[T - HI :], xhalo, s_halo.at[0], s_halo.at[1], (gi, lax.rem(c + 1, n_ctx), f, h)
    )

    @pl.when(jnp.logical_not(last_c))
    def _():
        halo_copy.start()

    x_load = pltpu.make_async_copy(x, xv, s_loc.at[0])
    g_load = pltpu.make_async_copy(g, gv, s_loc.at[1])
    h_load = pltpu.make_async_copy(hidden, hv, s_loc.at[2])
    w_load = pltpu.make_async_copy(w, wh, s_loc.at[3])
    own_at = pl.ds(pl.multiple_of(me * wb, wb), wb)
    own_load = pltpu.make_async_copy(hidden.at[:, own_at], hall.at[me], s_loc.at[4])
    x_load.start()
    g_load.start()

    @pl.when(jnp.logical_not(needing))
    def _():
        w_all(w_send, "start")
        w_load.start()

    for d in range(1, n_ctx):
        h_send(d, f).start()
    h_load.start()
    own_load.start()

    @pl.when(first)
    def _():
        xhalo[...] = jnp.zeros_like(xhalo)
        tails[...] = jnp.zeros_like(tails)
        start[...] = jnp.zeros_like(start)

    @pl.when(last_c)
    def _():
        endg[...] = jnp.zeros_like(endg)
        rims[...] = jnp.zeros_like(rims)
        rimx_r[...] = jnp.zeros_like(rimx_r)

    for copy in smalls:
        copy.wait()
    ends = [span_ref[0, 0]]
    for i in range(1, span_ref.shape[1]):
        ends.append(ends[-1] + span_ref[0, i])

    def segment(pos):
        counted = sum((e <= pos).astype(jnp.int32) for e in ends)
        return jnp.where(pos >= 0, counted, -1)

    pos0 = c * T
    row = lax.broadcasted_iota(jnp.int32, (T, 128), 0)
    lane = lax.broadcasted_iota(jnp.int32, (T, 128), 1)
    seg = segment(pos0 + row)
    for k in range(3):
        m = (segment(pos0 + row - 3 + k) == seg).astype(F32)
        masks[k] = jnp.concatenate([m, m], axis=1)
    same = (seg == segment(pos0 + lane)) & (row >= lane)
    same_ref[...] = same.astype(F32)
    seg_before = segment(jnp.full((T, 128), pos0 - 1, jnp.int32))
    seg_last = segment(jnp.full((T, 128), pos0 + T - 1, jnp.int32))
    alive_ref[...] = (seg == seg_before).astype(F32)
    last_ref[...] = (seg == seg_last).astype(F32)
    through = (seg_last == seg_before).astype(F32)[:heads]

    decay = decay_ref[...]
    raw = raw_ref[...].T
    dt = jnp.maximum(raw, 0.0) + jnp.log1p(jnp.exp(-jnp.abs(raw)))
    tri = (row >= lane).astype(F32)
    cum = dot(tri, -dt * decay, 1, 0, EXACT)
    ea = jnp.exp(cum)
    eb = jnp.exp(-cum)
    small[0] = dt
    small[1] = ea
    small[2] = eb
    small[3] = raw
    eye = (
        lax.broadcasted_iota(jnp.int32, (heads, heads), 0)
        == lax.broadcasted_iota(jnp.int32, (heads, heads), 1)
    ).astype(F32)
    ones = jnp.ones((heads, 128), BF)
    thr = through * sum(dot(p, ones, 1, 0) for p in pieces(eye * ea[T - 1 :, :]))
    ds_acc[...] = jnp.zeros_like(ds_acc)
    r_acc[...] = jnp.zeros_like(r_acc)
    q_acc[...] = jnp.zeros_like(q_acc)
    l_acc[...] = jnp.zeros_like(l_acc)
    db_acc[...] = jnp.zeros_like(db_acc)
    dc_acc[...] = jnp.zeros_like(dc_acc)

    per = NC // HEAD

    def spread(k):
        hr = lax.broadcasted_iota(jnp.int32, (heads, NC), 0)
        cl = lax.broadcasted_iota(jnp.int32, (heads, NC), 1)
        return (hr == k * per + cl // HEAD).astype(F32).astype(BF)

    def widen(v, sel):
        return sum(dot(p, sel, 1, 0) for p in pieces(v))

    def narrow(v, sel):
        hi, mid, _ = pieces(v)
        return dot(hi, sel, 1, 1) + dot(mid, sel, 1, 1)

    def chunk(k):
        return pl.ds(pl.multiple_of(k * NC, NC), NC)

    x_load.wait()
    g_load.wait()

    @pl.when(jnp.logical_not(first))
    def _():
        halo_copy.wait_recv()

    part[...] = jnp.zeros_like(part)
    h_load.wait()

    @pl.when(jnp.logical_not(needing))
    def _():
        w_load.wait()

    def product(i):
        part[...] += dot(hv[:, w_rows(i)], wh[w_rows(i)], 1, 0)

    def second(k, z):
        @pl.when(needing)
        def _():
            w_forward(k).wait_recv()

        product((1 - gi) * chunks + k)
        return z

    def prepare(k, z):
        @pl.when(needing)
        def _():
            w_send(k).wait_recv()
            w_forward(k).start()

        product(gi * chunks + k)

        @pl.when(k >= YLAG)
        def _():
            second(k - YLAG, 0)

        at = chunk(k)
        taps = tapx_ref[:, at]
        xe = jnp.concatenate([xhalo[:, at], xv[:, at]]).astype(F32)
        pre = taps[3:4, :] * xe[HI:]
        for d in range(1, 4):
            pre += taps[3 - d : 4 - d, :] * pltpu.roll(xe, d, 0)[HI:] * masks[3 - d]
        sig = jax.nn.sigmoid(pre)
        xc = pre * sig
        xf[:, at] = xc
        dsf[:, at] = sig * (1.0 + pre * (1.0 - sig))
        sel = spread(k)
        dt_w, a_w, b_w = widen(small[0], sel), widen(small[1], sel), widen(small[2], sel)
        dtw[:, at] = dt_w
        aw[:, at] = a_w
        bw[:, at] = b_w
        scaled = xc * dt_w * b_w
        b_x = scaled.astype(BF)
        bx[:, at] = b_x
        tx[:, at] = (scaled * a_w[T - 1 :, :]).astype(BF)
        a_g = (a_w * gv[:, at].astype(F32)).astype(BF)
        ag[:, at] = a_g
        ds_acc[...] += dot(a_g, b_x, 1, 1)
        thrc[at, :] = sum(dot(sel, p, 0, 0) for p in pieces(thr))
        return z

    lax.fori_loop(0, chunks, prepare, 0)

    @pl.when(jnp.logical_not(needing))
    def _():
        w_all(w_send, "wait_send")

    for d in (*range(1, n_ctx), 0):
        h_send(d, 1 - f).start()

    lax.fori_loop(chunks - YLAG, chunks, second, 0)

    p_swap = remote(part, partr, s_ps.at[0], s_pr, (gi, c, f, 1 - h))
    p_swap.start()
    p_tails = [
        remote(
            part.at[T - 8 :], tails.at[h], s_ps.at[1 + o], s_tr.at[h],
            (gi, lax.rem(c + 1, n_ctx), f, lax.rem(h + o, 2)),
        )
        for o in range(2)
    ]

    @pl.when(jnp.logical_not(last_c))
    def _():
        for p in p_tails:
            p.start()

    p_swap.wait_recv()

    @pl.when(jnp.logical_not(first))
    def _():
        for o in range(2):
            remote(part.at[T - 8 :], tails.at[o], s_ps.at[1], s_tr.at[o], (gi, c, f, 1 - h)).wait_recv()

    taps_b = tapb_ref[...]
    bc = (part[...] + partr[...]).astype(BF).astype(F32)
    tail = (tails[0] + tails[1]).astype(BF).astype(F32)
    be = jnp.concatenate([tail, bc])
    pre_bc = taps_b[3:4, :] * bc
    for d in range(1, 4):
        pre_bc += taps_b[3 - d : 4 - d, :] * pltpu.roll(be, d, 0)[8:] * masks[3 - d]
    sig_bc = jax.nn.sigmoid(pre_bc)
    conv_bc = pre_bc * sig_bc
    silu_bc[...] = sig_bc * (1.0 + pre_bc * (1.0 - sig_bc))
    b_own, c_own = conv_bc[:, :STATE], conv_bc[:, STATE:]
    lastb[...] = (last_ref[...] * b_own).astype(BF)
    alivec[...] = (alive_ref[...] * c_own).astype(BF)
    def piece(k):
        return pl.ds(pl.multiple_of(k * CH, CH), CH)

    def f_copy(k):
        return remote(sn.at[piece(k)], start.at[piece(k)], s_fs.at[k], s_fr.at[k], (gi, lax.rem(c + 1, n_ctx), f, h))

    def b_copy(k):
        return remote(
            sp.at[piece(k)], endg.at[piece(k)], s_bs.at[k], s_br.at[k], (gi, lax.rem(c + n_ctx - 1, n_ctx), f, h)
        )

    def forward(k):
        @pl.when(jnp.logical_not(first))
        def _():
            f_copy(k).wait_recv()

        at = piece(k)
        e = dot(tx[:, at], lastb[...], 0, 0)
        sn[at, :] = (e + thrc[at, :] * start[at, :].astype(F32)).astype(BF)

        @pl.when(jnp.logical_not(last_c))
        def _():
            f_copy(k).start()

    def backward(k):
        @pl.when(jnp.logical_not(last_c))
        def _():
            b_copy(k).wait_recv()

        at = piece(k)
        e = dot(ag[:, at], alivec[...], 0, 0)
        sp[at, :] = (e + thrc[at, :] * endg[at, :].astype(F32)).astype(BF)

        @pl.when(jnp.logical_not(first))
        def _():
            b_copy(k).start()

    row_n = lax.broadcasted_iota(jnp.int32, (T, NC), 0)
    row_8 = lax.broadcasted_iota(jnp.int32, (8, NC), 0)

    def transposed_conv(d_pre, taps):
        own = taps[3:4, :] * d_pre
        rim = jnp.zeros((8, NC), F32)
        for d in range(1, 4):
            z = pltpu.roll(taps[3 - d : 4 - d, :] * masks[3 - d] * d_pre, T - d, 0)
            own += jnp.where(row_n < T - d, z, 0.0)
            rim += jnp.where(row_8 < 8 - d, 0.0, z[T - 8 :])
        return own, rim

    def collect(k):
        at = chunk(k)
        db_acc[...] += dot(tx[:, at], endg[at, :], 1, 0)
        dc_acc[...] += dot(ag[:, at], start[at, :], 1, 0)

    def finish(k):
        at = chunk(k)
        taps = tapx_ref[:, at]
        sel = spread(k)
        sm = sm_ref[...]
        a_w, b_w = aw[:, at], bw[:, at]
        gf = gv[:, at].astype(F32)
        b_x, a_g = bx[:, at], ag[:, at]
        st, en = start[at, :], endg[at, :]
        y = dot(sm, b_x, 1, 0) + dot(alivec[...], st, 1, 1)
        r_acc[...] += narrow(a_w * gf * y, sel)
        d_xt = b_w * (dot(sm, a_g, 0, 0) + a_w[T - 1 :, :] * dot(lastb[...], en, 1, 1))
        q_acc[...] += narrow(xf[:, at] * d_xt, sel)
        prod = en.astype(F32) * sn[at, :].astype(F32)
        hi, mid, _ = pieces(prod)
        ones8 = jnp.ones((8, 128), BF)
        l_acc[...] += narrow(dot(ones8, hi, 1, 1) + dot(ones8, mid, 1, 1), sel)
        skip_w = widen(jnp.broadcast_to(skip_ref[...], (8, heads)), sel)[:1]
        d_pre = (dtw[:, at] * d_xt + skip_w * gf) * dsf[:, at]
        own, rim = transposed_conv(d_pre, taps)
        gxs[:, at] = own.astype(BF)
        gxtail[:, at] = own[T - HI :]
        rimx_s[:, at] = rim

    inner = jnp.logical_and(c > 0, c < n_ctx - 1)
    pieces_n = W // CH
    group = NC // CH
    offset = jnp.where(inner, LAG, pieces_n)
    early = c < n_ctx // 2

    def lead(k, z):
        @pl.when(early)
        def _():
            forward(k)

        @pl.when(jnp.logical_not(early))
        def _():
            backward(k)

        return z

    def scores():
        same_f = same_ref[...] > 0.5
        sm_ref[...] = jnp.where(same_f, dot(c_own, b_own, 1, 1, EXACT), 0.0).astype(BF)
        d_sm = jnp.where(same_f, ds_acc[...], 0.0)
        dps[:, :STATE] = dot(d_sm, c_own, 0, 0, EXACT)
        dps[:, STATE:] = dot(d_sm, b_own, 1, 0, EXACT)

    def step(k, z):
        @pl.when(k + offset < pieces_n)
        def _():
            lead(k + offset, 0)

        @pl.when(early)
        def _():
            backward(k)

        @pl.when(jnp.logical_not(early))
        def _():
            forward(k)

        @pl.when(lax.rem(k, group) == group - 1)
        def _():
            collect(k // group)

            @pl.when(k >= group)
            def _():
                finish(k // group - 1)

        return z

    lax.fori_loop(0, jnp.where(inner, 0, offset), lead, 0)
    scores()
    lax.fori_loop(0, jnp.where(inner, offset, 0), lead, 0)
    lax.fori_loop(0, pieces_n, step, 0)

    rimx = remote(rimx_s, rimx_r, s_rim.at[0], s_rim.at[1], (gi, lax.rem(c + n_ctx - 1, n_ctx), f, h))

    alive, last = alive_ref[...], last_ref[...]
    d_bcc = jnp.concatenate([last * db_acc[...], alive * dc_acc[...]], axis=1)
    dps[...] = (dps[...] + d_bcc) * silu_bc[...]
    d_swap = remote(dps, dpsr, s_ds.at[0], s_dr, (gi, c, f, 1 - h))
    d_swap.start()
    d_rims = [
        remote(
            dps.at[:8], rims.at[h], s_ds.at[1 + o], s_rr.at[h],
            (gi, lax.rem(c + n_ctx - 1, n_ctx), f, lax.rem(h + o, 2)),
        )
        for o in range(2)
    ]

    @pl.when(jnp.logical_not(first))
    def _():
        for p in d_rims:
            p.start()

    finish(chunks - 1)

    d_swap.wait_recv()

    @pl.when(jnp.logical_not(last_c))
    def _():
        for o in range(2):
            remote(dps.at[:8], rims.at[o], s_ds.at[1], s_rr.at[o], (gi, c, f, 1 - h)).wait_recv()

    own, _ = transposed_conv(dps[...] + dpsr[...], taps_b)
    rim_in = rims[0] + rims[1]
    row8 = lax.broadcasted_iota(jnp.int32, (8, 2 * STATE), 0)
    npos = pos0 + T + row8
    nseg = segment(npos)
    rim = jnp.zeros((8, 2 * STATE), F32)
    for d in range(1, 4):
        mask = (segment(npos - d) == nseg).astype(F32)
        z = pltpu.roll(taps_b[3 - d : 4 - d, :] * mask * rim_in, 8 - d, 0)
        rim += jnp.where(row8 < 8 - d, 0.0, z)
    d_bc = jnp.concatenate([own[: T - 8], own[T - 8 :] + rim]).astype(BF)
    dall[me] = d_bc

    half = pl.ds(pl.multiple_of(h * (T // 2), T // 2), T // 2)
    other = pl.ds(pl.multiple_of((1 - h) * (T // 2), T // 2), T // 2)

    def z_copy(d):
        return remote(
            dall.at[me, half], dall.at[me, half], s_zs.at[d], s_zr.at[me], (gi, lax.rem(c + d, n_ctx), f, h)
        )

    def x_copy(cc):
        b = cc * 2 + f
        return remote(dall.at[b, half], dall.at[b, half], s_xs.at[cc], s_xr.at[cc], (gi, c, 1 - f, h))

    def c_copy(b):
        return remote(dall.at[b, half], dall.at[b, half], s_cs.at[b], s_cr.at[b], (gi, c, f, 1 - h))

    def from_z(cc):
        b = cc * 2 + f
        return remote(dall.at[b, half], dall.at[b, half], s_zs.at[0], s_zr.at[b], (gi, c, f, 1 - h))

    def from_x(cc):
        b = cc * 2 + 1 - f
        return remote(dall.at[b, half], dall.at[b, half], s_xs.at[0], s_xr.at[cc], (gi, c, f, 1 - h))

    def from_c(b):
        return remote(dall.at[b, other], dall.at[b, other], s_cs.at[0], s_cr.at[b], (gi, c, f, 1 - h))

    left = c < n_ctx // 2
    nearest = [c + 1 - 2 * lax.rem(c, 2), jnp.where(left, 2, 1), jnp.where(left, 3, 0)]
    x_copy(c).start()
    for cc in nearest[::-1]:
        z_copy(lax.rem(cc - c + n_ctx, n_ctx)).start()

    @pl.when(jnp.logical_not(first))
    def _():
        rimx.start()

    def grad_u(k, z):
        at = w_rows(k)
        gus[:, at] = dot(dall[me], wh[at], 1, 1).astype(BF)
        return z

    parts = 2 * chunks
    marks = [parts // 2, parts * 11 // 16, parts * 7 // 8, parts]
    lax.fori_loop(0, marks[0], grad_u, 0)
    from_x(c).wait_recv()
    c_copy(c * 2 + 1 - f).start()
    for i, cc in enumerate(nearest):
        from_z(cc).wait_recv()
        x_copy(cc).start()
        c_copy(cc * 2 + f).start()
        lax.fori_loop(marks[i], marks[i + 1], grad_u, 0)
    u_out = pltpu.make_async_copy(gus, gu_out, s_out.at[0])
    u_out.start()

    total_q = q_acc[...]
    dts = small[0]
    at_end = row[:, :heads] == T - 1
    d_cum = r_acc[...] - dts * total_q + jnp.where(at_end, l_acc[:1, :], 0.0)
    d_log = dot(tri, d_cum, 0, 0, EXACT)
    ddt_ref[...] = ((total_q - decay_ref[...] * d_log) * jax.nn.sigmoid(small[3])).T
    t_out = pltpu.make_async_copy(ddt_ref, ddt_out, s_out.at[3])
    t_out.start()

    for cc in nearest:
        from_x(cc).wait_recv()
        c_copy(cc * 2 + 1 - f).start()

    @pl.when(jnp.logical_not(last_c))
    def _():
        rimx.wait_recv()

    fixed = gxtail[HI - 8 :, :] + rimx_r[...]
    gxs[T - HI :, :] = jnp.concatenate([gxtail[: HI - 8, :], fixed]).astype(BF)
    x_out = pltpu.make_async_copy(gxs, gx_out, s_out.at[1])
    x_out.start()

    def h_wait(b):
        remote(hall.at[b], hall.at[b], s_hs.at[0], s_hr.at[b], (gi, c, f, 1 - h)).wait_recv()

    own_load.wait()
    for d in range(1, n_ctx):
        b = lax.rem(c + d, n_ctx) * 2 + f
        from_c(b).wait_recv()
        h_wait(b)
    for d in range(n_ctx):
        b = lax.rem(c + d, n_ctx) * 2 + 1 - f
        from_c(b).wait_recv()
        h_wait(b)
    gws[...] = dot(
        hall[...].reshape(2 * n_ctx * T, wb), dall[...].reshape(2 * n_ctx * T, 2 * STATE), 0, 0
    )
    w_out = pltpu.make_async_copy(gws, gw_out, s_out.at[2])
    w_out.start()

    @pl.when(needing)
    def _():
        w_all(w_forward, "wait_send")

    @pl.when(jnp.logical_not(last_c))
    def _():
        halo_copy.wait_send()
        for p in p_tails:
            p.wait_send()
        lax.fori_loop(0, W // CH, lambda k, z: (f_copy(k).wait_send(), z)[1], 0)

    @pl.when(jnp.logical_not(first))
    def _():
        for p in d_rims:
            p.wait_send()
        rimx.wait_send()
        lax.fori_loop(0, W // CH, lambda k, z: (b_copy(k).wait_send(), z)[1], 0)

    p_swap.wait_send()
    d_swap.wait_send()
    for d in range(n_ctx):
        h_send(d, 1 - f).wait_send()
        x_copy(lax.rem(c + d, n_ctx)).wait_send()
        c_copy(lax.rem(c + d, n_ctx) * 2 + 1 - f).wait_send()
        if d:
            h_send(d, f).wait_send()
            z_copy(d).wait_send()
            c_copy(lax.rem(c + d, n_ctx) * 2 + f).wait_send()
    u_out.wait()
    x_out.wait()
    w_out.wait()
    t_out.wait()


def fused(hidden, w, x, g, raw, decay, skip, tapx, tapb, spans):
    T, W = x.shape
    DH = hidden.shape[1]
    n_ctx = lax.axis_size("ctx")
    blocks = 2 * n_ctx
    wb = DH // blocks
    heads = raw.shape[0]
    K = W // CH
    U = W // NC
    vm, dma = pltpu.VMEM, pltpu.SemaphoreType.DMA
    spec = pl.BlockSpec
    hbm = spec(memory_space=pltpu.HBM)
    out = spec(memory_space=pl.ANY)
    S2 = 2 * STATE
    return pl.pallas_call(
        fused_kernel,
        out_shape=(
            jax.ShapeDtypeStruct((T, W), BF),
            jax.ShapeDtypeStruct((T, DH), BF),
            jax.ShapeDtypeStruct((heads, T), F32),
            jax.ShapeDtypeStruct((wb, S2), F32),
        ),
        in_specs=[hbm] * 10,
        out_specs=(out,) * 4,
        scratch_shapes=[
            vm((heads, T), F32), vm((1, heads), F32), vm((1, heads), F32), vm((4, W), F32), vm((4, S2), F32),
            pltpu.SMEM(spans.shape, jnp.int32), vm((heads, T), F32),
            vm((T, W), BF), vm((T, W), BF), vm((T, DH), BF), vm((DH, S2), BF), vm((HI, W), BF),
            vm((T, W), F32), vm((T, W), F32), vm((T, W), F32), vm((T, W), F32), vm((T, W), F32),
            vm((T, W), BF), vm((T, W), BF), vm((T, W), BF), vm((W, STATE), F32),
            vm((W, STATE), BF), vm((W, STATE), BF), vm((W, STATE), BF), vm((W, STATE), BF),
            vm((3, T, S2), F32), vm((T, STATE), F32), vm((T, STATE), F32), vm((T, STATE), F32),
            vm((4, T, heads), F32), vm((T, T), F32), vm((T, S2), F32), vm((T, S2), F32), vm((2, 8, S2), F32),
            vm((T, S2), F32), vm((T, T), BF), vm((T, STATE), BF), vm((T, STATE), BF),
            vm((T, STATE), F32), vm((T, STATE), F32), vm((T, S2), F32), vm((T, S2), F32), vm((2, 8, S2), F32),
            vm((8, W), F32), vm((8, W), F32), vm((HI, W), F32),
            vm((T, heads), F32), vm((T, heads), F32), vm((8, heads), F32),
            vm((blocks, T, wb), BF), vm((blocks, T, S2), BF),
            vm((T, W), BF), vm((T, DH), BF), vm((wb, S2), F32),
            dma((5,)), dma((U,)), dma((U,)), dma((U,)), dma((U,)), dma((blocks,)), dma((blocks,)), dma((2,)),
            dma((K,)), dma((K,)), dma((K,)), dma((K,)),
            dma((3,)), dma, dma((2,)), dma((3,)), dma, dma((2,)), dma((2,)),
            dma((n_ctx,)), dma((blocks,)), dma((n_ctx,)), dma((n_ctx,)), dma((blocks,)), dma((blocks,)), dma((6,)), dma((4,)),
        ],
        compiler_params=pltpu.CompilerParams(
            collective_id=0, has_side_effects=True, vmem_limit_bytes=60 << 20
        ),
        cost_estimate=pl.CostEstimate(
            flops=2 * T * 256 * (W * 9 + DH * 4), bytes_accessed=8 << 20, transcendentals=4 * T * W
        ),
    )(hidden, w, x, g, raw, decay, skip, tapx, tapb, spans)


def publish_kernel(*refs):
    n = (len(refs) - 2) // 3
    ins, outs, held, in_sem, out_sem = refs[:n], refs[n : 2 * n], refs[2 * n : 3 * n], refs[-2], refs[-1]
    loads, stores = [], []
    for i in range(n):
        rows = ins[i].shape[0] // PUB
        for j in range(PUB):
            at = pl.ds(j * rows, rows)
            loads.append(pltpu.make_async_copy(ins[i].at[at], held[i].at[at], in_sem.at[i, j]))
            stores.append(pltpu.make_async_copy(held[i].at[at], outs[i].at[at], out_sem.at[i, j]))
    for copy in loads:
        copy.start()
    for load, store in zip(loads, stores):
        load.wait()
        store.start()
    for copy in stores:
        copy.wait()


def publish(arrays):
    n = len(arrays)
    hbm = pl.BlockSpec(memory_space=pl.ANY)
    return pl.pallas_call(
        publish_kernel,
        out_shape=tuple(jax.ShapeDtypeStruct(a.shape, a.dtype) for a in arrays),
        in_specs=[hbm] * n,
        out_specs=(hbm,) * n,
        scratch_shapes=[pltpu.VMEM(a.shape, a.dtype) for a in arrays]
        + [pltpu.SemaphoreType.DMA((n, PUB)), pltpu.SemaphoreType.DMA((n, PUB))],
        compiler_params=pltpu.CompilerParams(vmem_limit_bytes=60 << 20),
    )(*arrays)


def on_device(
    hidden_in, w_bc, x_in, dt_raw, decay_rate, conv_x, conv_bc, skip_gain, span_len, grad_y
):
    T = x_in.shape[1]
    hidden = hidden_in[0]
    half_width = hidden.shape[1]
    n_ctx, n_fsdp, n_head = (lax.axis_size(a) for a in ("ctx", "fsdp", "head"))
    assert T * 2 == MOST and dt_raw.shape[2] == 32
    x0, g0, raw0 = x_in[0], grad_y[0], dt_raw[0]
    if (lax.axis_size("groups"), n_ctx, n_fsdp, n_head) == (2, 4, 2, 2):
        outs = fused(
            hidden, w_bc, x0, g0, raw0.T, decay_rate[None, :], skip_gain[None, :], conv_x, conv_bc, span_len
        )
        outs = publish(outs)
        return (outs[0][None], outs[1][None], outs[2].T[None], outs[3][None])
    if n_fsdp == n_head:
        route = [(f * n_head + h, h * n_head + f) for f in range(n_fsdp) for h in range(n_head)]
        w_half = lax.ppermute(w_bc, ("fsdp", "head"), route)
    else:
        w_full = lax.all_gather(w_bc, "fsdp", axis=0, tiled=True)
        w_half = lax.dynamic_slice_in_dim(
            w_full, lax.axis_index("head") * half_width, half_width, 0
        )
    raws = [shifted(raw0, "ctx", d) for d in (2, 1)] + [raw0] + [shifted(raw0, "ctx", -d) for d in (1, 2)]
    x1, g1 = shifted(x0, "ctx", 1), shifted(g0, "ctx", -1)
    x2, g2 = shifted(x0, "ctx", 2), shifted(g0, "ctx", -2)

    swap = [(i, (i + 1) % n_head) for i in range(n_head)]
    partial_bc = jnp.dot(hidden, w_half, preferred_element_type=F32)
    bc_pre = (partial_bc + lax.ppermute(partial_bc, "head", swap)).astype(BF)
    bcs = [shifted(bc_pre, "ctx", d) for d in (2, 1)] + [bc_pre] + [shifted(bc_pre, "ctx", -d) for d in (1, 2)]

    n_blocks = n_ctx * n_fsdp
    blocks = hidden.reshape(T, n_blocks, half_width // n_blocks).transpose(1, 0, 2)
    hidden_all = lax.all_to_all(blocks, ("ctx", "fsdp"), 0, 0, tiled=True)

    position = (lax.axis_index("ctx") - 2) * T + jnp.arange(-3, 5 * T, dtype=jnp.int32)
    spans = span_len.shape[1]
    earlier = jnp.arange(spans)[:, None] <= jnp.arange(spans)[None, :]
    span_ends = jnp.sum(jnp.where(earlier, span_len[0][:, None], 0), axis=0)
    counted = jnp.sum((span_ends[None, :] <= position[:, None]).astype(jnp.int32), axis=1)
    segment = jnp.where(position >= 0, counted, -1).astype(F32)
    own_seg = segment[3:]
    by_block = own_seg.reshape(5, T)
    before = jnp.broadcast_to(segment[2 : 2 + 5 * T : T][:, None], (5, T)).reshape(-1)
    last = jnp.broadcast_to(by_block[:, T - 1 :], (5, T)).reshape(-1)
    info = jnp.stack(
        [(segment[k : k + 5 * T] == own_seg).astype(F32) for k in range(3)]
        + [(own_seg == before).astype(F32), (own_seg == last).astype(F32), own_seg],
        axis=1,
    )
    segrow = by_block[2:3]
    raw = jnp.tile(jnp.concatenate(raws), (1, 4))
    decay = jnp.tile(decay_rate, 4)[None, :]
    skip = jnp.repeat(skip_gain, HEAD)[None, :]

    dx, tail, rim, dbc, rimbc, ddt = ssm(
        (x2, x1, x0), (g0, g1, g2), bcs, raw, info, segrow, decay, skip, conv_x, conv_bc
    )
    back = shifted(rim, "ctx", -1)
    grad_x = lax.dynamic_update_slice(dx, (tail + back).astype(BF), (T - 8, 0))

    other = lax.ppermute(dbc, "head", swap)
    rim_same = shifted(rimbc, "ctx", -1)
    cross = [
        (c * n_head + h, (c - 1) * n_head + (h + 1) % n_head)
        for c in range(1, n_ctx)
        for h in range(n_head)
    ]
    rim_cross = lax.ppermute(rimbc, ("ctx", "head"), cross)
    d_bc = ((dbc + other) + jnp.pad(rim_same + rim_cross, ((T - 8, 0), (0, 0)))).astype(BF)
    grad_u = lax.dot_general(
        d_bc, w_half, (((1,), (1,)), ((), ())), preferred_element_type=F32
    ).astype(BF)
    d_all = lax.all_gather(d_bc, ("ctx", "fsdp"), axis=0)
    grad_w = lax.dot_general(
        hidden_all.reshape(n_blocks * T, -1),
        d_all.reshape(n_blocks * T, -1),
        (((0,), (0,)), ((), ())),
        preferred_element_type=F32,
    )
    return (grad_x[None], grad_u[None], ddt[None], grad_w[None])


def solution(mesh):
    return jax.shard_map(
        on_device,
        mesh=mesh,
        in_specs=(
            P(("groups", "fsdp"), "ctx", "head"),
            P("fsdp", None),
            P(("groups", "fsdp"), "ctx", "head"),
            P(("groups", "fsdp"), "ctx", "head"),
            P("head"),
            P(None, "head"),
            P(),
            P("head"),
            P(("groups", "fsdp"), None),
            P(("groups", "fsdp"), "ctx", "head"),
        ),
        out_specs=(
            P(("groups", "fsdp"), "ctx", "head"),
            P(("groups", "fsdp"), "ctx", "head"),
            P(("groups", "fsdp"), "ctx", "head"),
            P(("groups", "head"), ("ctx", "fsdp"), None),
        ),
        check_vma=False,
    )
```

```python
import jax
import jax.numpy as jnp
from jax import lax
from jax.experimental import pallas as pl
from jax.experimental.pallas import tpu as pltpu
from jax.sharding import PartitionSpec as P

STATE = 128
HEAD = 64
MOST = 256
BF = jnp.bfloat16
F32 = jnp.float32
EXACT = lax.Precision.HIGHEST


def shifted(block, axis, distance):
    devices = range(lax.axis_size(axis))
    route = [(i - distance, i) for i in devices if i - distance in devices]
    return lax.ppermute(block, axis, route)


def dot(a, b, ca, cb, precision=None):
    return lax.dot_general(
        a, b, (((ca,), (cb,)), ((), ())), precision=precision, preferred_element_type=F32
    )


def ssm_kernel(
    x2, x1, x0, g0, g1, g2, b2, b1, b0, b3, b4, raw_ref, info_ref, segrow_ref,
    decay_ref, skip_ref, tapx_ref, tapb_ref,
    dx_ref, tail_ref, rim_ref, dbc_ref, rimbc_ref, ddt_ref,
    masks, bias_ref, s_ref, cols_a, cols_b, cum_rows, bprev, cnext, bown, cown,
    silu_bc, d_s, d_b, d_c, acc,
):
    T = x0.shape[0]
    pairs = x0.shape[1] // 128
    lane = lax.broadcasted_iota(jnp.int32, (T, 128), 1)
    row = lax.broadcasted_iota(jnp.int32, (T, 128), 0)
    low = lane < HEAD
    group = lane // 32
    info = info_ref[...]
    for k in range(3):
        masks[k] = jnp.broadcast_to(info[: 3 * T, k : k + 1], (3 * T, 128))

    def col(block, k):
        return info[block * T : (block + 1) * T, k : k + 1]

    tri = (row >= lane).astype(F32)
    decay = decay_ref[...]
    dts, cums, carried, toward = [], [], [], []
    for j in range(5):
        raw = raw_ref[j * T : (j + 1) * T, :]
        dt = jnp.maximum(raw, 0.0) + jnp.log1p(jnp.exp(-jnp.abs(raw)))
        cum = dot(tri, -dt * decay, 1, 0, EXACT)
        dts.append(dt)
        cums.append(cum)
        carried.append(jnp.exp(cum) * col(j, 3))
        toward.append(jnp.exp(cum[T - 1 :, :] - cum) * col(j, 4))
    a1 = dts[1] * toward[1]
    a2 = dts[0] * toward[0] * carried[1][T - 1 :, :]
    c1 = carried[3]
    c2 = carried[4] * carried[3][T - 1 :, :]

    def packed(p, q, r, s):
        return jnp.where(group == 0, p, jnp.where(group == 1, q, jnp.where(group == 2, r, s)))

    cols_a[...] = packed(dts[2], cums[2], carried[2], toward[2])
    cols_b[...] = packed(a2, a1, c1, c2)
    cum_rows[...] = cums[2].T
    same = col(2, 5) == segrow_ref[...]
    bias_ref[...] = jnp.where(same & (row >= lane), 0.0, -1e30)

    taps_b = tapb_ref[...]
    bc = jnp.concatenate([b2[...], b1[...], b0[...], b3[...], b4[...]]).astype(F32)
    pre_bc = taps_b[3:4, :] * bc
    for k in range(3):
        pre_bc += taps_b[k : k + 1, :] * pltpu.roll(bc, 3 - k, 0) * info[:, k : k + 1]
    sig_bc = jax.nn.sigmoid(pre_bc)
    conv_bc = pre_bc * sig_bc
    own_sig = sig_bc[2 * T : 3 * T]
    silu_bc[...] = own_sig * (1.0 + pre_bc[2 * T : 3 * T] * (1.0 - own_sig))
    bprev[...] = conv_bc[: 2 * T, :STATE].astype(BF)
    cnext[...] = conv_bc[3 * T :, STATE:].astype(BF)
    bown[...] = conv_bc[2 * T : 3 * T, :STATE]
    cown[...] = conv_bc[2 * T : 3 * T, STATE:]
    s_ref[...] = dot(cown[...], bown[...], 1, 1, EXACT)
    d_s[...] = jnp.zeros_like(d_s)
    d_b[...] = jnp.zeros_like(d_b)
    d_c[...] = jnp.zeros_like(d_c)
    acc[...] = jnp.zeros_like(acc)

    def pair(i, carry):
        at = pl.ds(pl.multiple_of(i * 128, 128), 128)
        ca = pltpu.roll(cols_a[...], (128 - 2 * i) % 128, 1)
        cb = pltpu.roll(cols_b[...], (128 - 2 * i) % 128, 1)

        def wide(c, q):
            return jnp.where(low, c[:, 32 * q : 32 * q + 1], c[:, 32 * q + 1 : 32 * q + 2])

        def tall(c, q):
            return c[:, 32 * q : 32 * q + 1], c[:, 32 * q + 1 : 32 * q + 2]

        taps = tapx_ref[:, at]
        xe = jnp.concatenate([x2[:, at], x1[:, at], x0[:, at]]).astype(F32)
        pre = taps[3:4, :] * xe
        for k in range(3):
            pre += taps[k : k + 1, :] * pltpu.roll(xe, 3 - k, 0) * masks[k]
        sig = jax.nn.sigmoid(pre)
        xc = pre * sig
        xown = xc[2 * T :]
        sown = sig[2 * T :]
        dsilu = sown * (1.0 + pre[2 * T :] * (1.0 - sown))
        dt_w = wide(ca, 0)
        toward_w = wide(ca, 3)
        xw = jnp.concatenate([xc[:T] * wide(cb, 0), xc[T : 2 * T] * wide(cb, 1)]).astype(BF)
        start = dot(xw, bprev[...], 0, 0)
        gw = jnp.concatenate(
            [g1[:, at].astype(F32) * wide(cb, 2), g2[:, at].astype(F32) * wide(cb, 3)]
        ).astype(BF)
        end_grad = dot(gw, cnext[...], 0, 0)
        start_b = start.astype(BF)
        end_b = end_grad.astype(BF)
        gy = g0[:, at].astype(F32)
        gg = jnp.concatenate([jnp.where(low, gy, 0.0), jnp.where(low, 0.0, gy)]).astype(BF)
        xt = xown * dt_w
        xt_b = xt.astype(BF)
        xx = jnp.concatenate([jnp.where(low, xt, 0.0), jnp.where(low, 0.0, xt)]).astype(BF)
        d_m = dot(gg, xt_b, 1, 1)
        cum_a, cum_b = tall(ca, 1)
        bias = bias_ref[...]
        decay_t = jnp.concatenate(
            [
                jnp.exp(cum_a - cum_rows[pl.ds(2 * i, 1), :] + bias),
                jnp.exp(cum_b - cum_rows[pl.ds(2 * i + 1, 1), :] + bias),
            ]
        )
        s_all = s_ref[...]
        s_two = jnp.concatenate([s_all, s_all])
        ls = decay_t * s_two
        ldm = decay_t * d_m
        d_s[...] += ldm[:T] + ldm[T:]
        d_x = dot(ls.astype(BF), gg, 0, 0)
        car = jnp.concatenate(tall(ca, 2))
        tow = jnp.concatenate(tall(ca, 3))
        c_u = car * dot(gg, start_b, 1, 0)
        d_c[...] += c_u[:T] + c_u[T:]
        c_own = cown[...]
        c_two = jnp.concatenate([c_own, c_own])
        r = jnp.sum(ldm * s_two + c_u * c_two, axis=1, keepdims=True)
        t_v = tow * dot(xx, end_b, 1, 0)
        d_b[...] += t_v[:T] + t_v[T:]
        d_xe = dot(bown[...].astype(BF), end_b, 1, 1) * toward_w
        d_xt = d_x + d_xe
        prod = xown * d_xt
        q_a = jnp.sum(jnp.where(low, prod, 0.0), axis=1, keepdims=True)
        q_b = jnp.sum(jnp.where(low, 0.0, prod), axis=1, keepdims=True)
        ends = jnp.sum(xt * d_xe, axis=0, keepdims=True)
        inner = end_grad * start
        low_row = low[:1]
        through_a, through_b = (v[T - 1 :, :] for v in tall(ca, 2))
        last_a = jnp.sum(jnp.where(low_row, ends, 0.0), axis=1, keepdims=True) + through_a * jnp.sum(
            jnp.sum(inner[:HEAD], axis=0, keepdims=True), axis=1, keepdims=True
        )
        last_b = jnp.sum(jnp.where(low_row, 0.0, ends), axis=1, keepdims=True) + through_b * jnp.sum(
            jnp.sum(inner[HEAD:], axis=0, keepdims=True), axis=1, keepdims=True
        )
        dt_a, dt_b = tall(ca, 0)
        final = row[:, :1] == T - 1
        cum_ga = r[:T] - dt_a * q_a + jnp.where(final, last_a, 0.0)
        cum_gb = r[T:] - dt_b * q_b + jnp.where(final, last_b, 0.0)
        placed = jnp.where(
            lane == 0,
            q_a,
            jnp.where(
                lane == 1, q_b, jnp.where(lane == 32, cum_ga, jnp.where(lane == 33, cum_gb, 0.0))
            ),
        )
        acc[...] += pltpu.roll(placed, 2 * i, 1)
        d_pre = (dt_w * d_xt + skip_ref[:, at] * gy) * dsilu
        own = taps[3:4, :] * d_pre
        rim = jnp.zeros((8, 128), F32)
        for k in range(3):
            d = 3 - k
            z = pltpu.roll(taps[k : k + 1, :] * masks[k, 2 * T :] * d_pre, T - d, 0)
            own += jnp.where(row < T - d, z, 0.0)
            rim += jnp.where(row[T - 8 :] < T - d, 0.0, z[T - 8 :])
        dx_ref[:, at] = own.astype(BF)
        tail_ref[:, at] = own[T - 8 :]
        rim_ref[:, at] = rim
        return carry

    lax.fori_loop(0, pairs, pair, 0)

    ds = d_s[...]
    full_c = d_c[...] + dot(ds, bown[...], 1, 0, EXACT)
    full_b = d_b[...] + dot(ds, cown[...], 0, 0, EXACT)
    d_pre = jnp.concatenate([full_b, full_c], axis=1) * silu_bc[...]
    own = taps_b[3:4, :] * d_pre
    rim = jnp.zeros((8, 2 * STATE), F32)
    row2 = lax.broadcasted_iota(jnp.int32, (T, 2 * STATE), 0)
    for k in range(3):
        d = 3 - k
        z = pltpu.roll(taps_b[k : k + 1, :] * info[2 * T : 3 * T, k : k + 1] * d_pre, T - d, 0)
        own += jnp.where(row2 < T - d, z, 0.0)
        rim += jnp.where(row2[T - 8 :] < T - d, 0.0, z[T - 8 :])
    dbc_ref[...] = own
    rimbc_ref[...] = rim
    total = acc[...]
    d_log = pltpu.roll(dot(tri, total, 0, 0, EXACT), 96, 1)
    raw = raw_ref[2 * T : 3 * T, :]
    ddt_ref[...] = ((total - decay * d_log) * jax.nn.sigmoid(raw))[:, :32]


def ssm(xs, gs, bcs, raw, info, segrow, decay, skip, tapx, tapb):
    T, W = xs[0].shape
    vm = pltpu.VMEM
    return pl.pallas_call(
        ssm_kernel,
        out_shape=(
            jax.ShapeDtypeStruct((T, W), BF),
            jax.ShapeDtypeStruct((8, W), F32),
            jax.ShapeDtypeStruct((8, W), F32),
            jax.ShapeDtypeStruct((T, 2 * STATE), F32),
            jax.ShapeDtypeStruct((8, 2 * STATE), F32),
            jax.ShapeDtypeStruct((T, 32), F32),
        ),
        scratch_shapes=[
            vm((3, 3 * T, 128), F32), vm((T, T), F32), vm((T, T), F32), vm((T, 128), F32),
            vm((T, 128), F32), vm((128, T), F32), vm((2 * T, STATE), BF), vm((2 * T, STATE), BF),
            vm((T, STATE), F32), vm((T, STATE), F32), vm((T, 2 * STATE), F32),
            vm((T, T), F32), vm((T, STATE), F32), vm((T, STATE), F32), vm((T, 128), F32),
        ],
        compiler_params=pltpu.CompilerParams(vmem_limit_bytes=40 << 20),
        cost_estimate=pl.CostEstimate(
            flops=2 * 9 * T * 256 * W, bytes_accessed=8 * T * W * 2, transcendentals=6 * T * W
        ),
    )(*xs, *gs, *bcs, raw, info, segrow, decay, skip, tapx, tapb)


MESH = pl.DeviceIdType.MESH
NC = 256
HI = 16
CH = 256
LAG = 3
YLAG = 4
PUB = 2


def pieces(v):
    hi = v.astype(BF)
    rest = v - hi.astype(F32)
    mid = rest.astype(BF)
    lo = (rest - mid.astype(F32)).astype(BF)
    return hi, mid, lo


def fused_kernel(
    hidden, w, x, g, raw_in, decay_in, skip_in, tapx_in, tapb_in, span_in,
    gx_out, gu_out, ddt_out, gw_out,
    raw_ref, decay_ref, skip_ref, tapx_ref, tapb_ref, span_ref, ddt_ref,
    xv, gv, hv, wh, xhalo, xf, dsf, aw, bw, dtw, bx, tx, ag, thrc, start, endg, sn, sp,
    masks, same_ref, alive_ref, last_ref, small, ds_acc, part, partr, tails, silu_bc,
    sm_ref, lastb, alivec, db_acc, dc_acc, dps, dpsr, rims, rimx_s, rimx_r, gxtail, r_acc, q_acc, l_acc,
    hall, dall, gxs, gus, gws,
    s_loc, s_ws, s_wr, s_ys, s_yr, s_hs, s_hr, s_halo, s_fs, s_fr, s_bs, s_br,
    s_ps, s_pr, s_tr, s_ds, s_dr, s_rr, s_rim, s_zs, s_zr, s_xs, s_xr, s_cs, s_cr, s_small, s_out,
):
    T, W = gxs.shape
    gi, c, f, h = (lax.axis_index(a) for a in ("groups", "ctx", "fsdp", "head"))
    n_ctx = lax.axis_size("ctx")
    DH = hv.shape[1]
    chunks = W // NC
    wrows = wh.shape[0] // 2 // chunks
    heads = raw_ref.shape[0]
    wb = hall.shape[2]
    first, last_c = c == 0, c == n_ctx - 1
    needing = h != f
    me = c * 2 + f

    def remote(src, dst, ss, rs, device):
        return pltpu.make_async_remote_copy(
            src_ref=src, dst_ref=dst, send_sem=ss, recv_sem=rs, device_id=device, device_id_type=MESH
        )

    smalls = [
        pltpu.make_async_copy(src, dst, s_small.at[i])
        for i, (src, dst) in enumerate(
            (
                (span_in, span_ref), (raw_in, raw_ref), (decay_in, decay_ref), (skip_in, skip_ref),
                (tapx_in, tapx_ref), (tapb_in, tapb_ref),
            )
        )
    ]
    for copy in smalls:
        copy.start()
    barrier = pltpu.get_barrier_semaphore()
    for o in range(1, 4 * n_ctx):
        oc, of, oh = o // 4, (o // 2) % 2, o % 2
        pl.semaphore_signal(
            barrier, 1, device_id=(gi, lax.rem(c + oc, n_ctx), lax.rem(f + of, 2), lax.rem(h + oh, 2)),
            device_id_type=MESH,
        )
    pl.semaphore_signal(barrier, 1, device_id=(1 - gi, c, f, h), device_id_type=MESH)
    pl.semaphore_wait(barrier, 4 * n_ctx)

    def w_rows(k):
        return pl.ds(pl.multiple_of(k * wrows, wrows), wrows)

    def w_rows(k):
        return pl.ds(pl.multiple_of(k * wrows, wrows), wrows)

    def w_send(k):
        at = w_rows(gi * chunks + k)
        return remote(w.at[at], wh.at[at], s_ws.at[k], s_wr.at[k], (gi, c, 1 - f, h))

    def w_forward(k):
        at = w_rows(gi * chunks + k)
        return remote(wh.at[at], wh.at[at], s_ys.at[k], s_yr.at[k], (1 - gi, c, f, h))

    def w_all(copy, act):
        lax.fori_loop(0, chunks, lambda k, z: (getattr(copy(k), act)(), z)[1], 0)

    def h_send(d, ff):
        cc = lax.rem(c + d, n_ctx)
        at = pl.ds(pl.multiple_of((cc * 2 + ff) * wb, wb), wb)
        return remote(
            hidden.at[:, at], hall.at[me], s_hs.at[d + n_ctx * (1 if ff is not f else 0)], s_hr.at[me], (gi, cc, ff, h)
        )

    halo_copy = remote(
        x.at[T - HI :], xhalo, s_halo.at[0], s_halo.at[1], (gi, lax.rem(c + 1, n_ctx), f, h)
    )

    @pl.when(jnp.logical_not(last_c))
    def _():
        halo_copy.start()

    x_load = pltpu.make_async_copy(x, xv, s_loc.at[0])
    g_load = pltpu.make_async_copy(g, gv, s_loc.at[1])
    h_load = pltpu.make_async_copy(hidden, hv, s_loc.at[2])
    w_load = pltpu.make_async_copy(w, wh, s_loc.at[3])
    own_at = pl.ds(pl.multiple_of(me * wb, wb), wb)
    own_load = pltpu.make_async_copy(hidden.at[:, own_at], hall.at[me], s_loc.at[4])
    x_load.start()
    g_load.start()

    @pl.when(jnp.logical_not(needing))
    def _():
        w_all(w_send, "start")
        w_load.start()

    for d in sorted(range(1, n_ctx), key=lambda d: abs(d - n_ctx // 2)):
        h_send(d, f).start()
    h_load.start()
    own_load.start()

    @pl.when(first)
    def _():
        xhalo[...] = jnp.zeros_like(xhalo)
        tails[...] = jnp.zeros_like(tails)
        start[...] = jnp.zeros_like(start)

    @pl.when(last_c)
    def _():
        endg[...] = jnp.zeros_like(endg)
        rims[...] = jnp.zeros_like(rims)
        rimx_r[...] = jnp.zeros_like(rimx_r)

    for copy in smalls:
        copy.wait()
    ends = [span_ref[0, 0]]
    for i in range(1, span_ref.shape[1]):
        ends.append(ends[-1] + span_ref[0, i])

    def segment(pos):
        counted = sum((e <= pos).astype(jnp.int32) for e in ends)
        return jnp.where(pos >= 0, counted, -1)

    pos0 = c * T
    row = lax.broadcasted_iota(jnp.int32, (T, 128), 0)
    lane = lax.broadcasted_iota(jnp.int32, (T, 128), 1)
    seg = segment(pos0 + row)
    for k in range(3):
        m = (segment(pos0 + row - 3 + k) == seg).astype(F32)
        masks[k] = jnp.concatenate([m, m], axis=1)
    same = (seg == segment(pos0 + lane)) & (row >= lane)
    same_ref[...] = same.astype(F32)
    seg_before = segment(jnp.full((T, 128), pos0 - 1, jnp.int32))
    seg_last = segment(jnp.full((T, 128), pos0 + T - 1, jnp.int32))
    alive_ref[...] = (seg == seg_before).astype(F32)
    last_ref[...] = (seg == seg_last).astype(F32)
    through = (seg_last == seg_before).astype(F32)[:heads]

    decay = decay_ref[...]
    raw = raw_ref[...].T
    dt = jnp.maximum(raw, 0.0) + jnp.log1p(jnp.exp(-jnp.abs(raw)))
    tri = (row >= lane).astype(F32)
    cum = dot(tri, -dt * decay, 1, 0, EXACT)
    ea = jnp.exp(cum)
    eb = jnp.exp(-cum)
    small[0] = dt
    small[1] = ea
    small[2] = eb
    small[3] = raw
    eye = (
        lax.broadcasted_iota(jnp.int32, (heads, heads), 0)
        == lax.broadcasted_iota(jnp.int32, (heads, heads), 1)
    ).astype(F32)
    ones = jnp.ones((heads, 128), BF)
    thr = through * sum(dot(p, ones, 1, 0) for p in pieces(eye * ea[T - 1 :, :]))
    ds_acc[...] = jnp.zeros_like(ds_acc)
    r_acc[...] = jnp.zeros_like(r_acc)
    q_acc[...] = jnp.zeros_like(q_acc)
    l_acc[...] = jnp.zeros_like(l_acc)
    db_acc[...] = jnp.zeros_like(db_acc)
    dc_acc[...] = jnp.zeros_like(dc_acc)

    per = NC // HEAD

    def spread(k):
        hr = lax.broadcasted_iota(jnp.int32, (heads, NC), 0)
        cl = lax.broadcasted_iota(jnp.int32, (heads, NC), 1)
        return (hr == k * per + cl // HEAD).astype(F32).astype(BF)

    def widen(v, sel):
        return sum(dot(p, sel, 1, 0) for p in pieces(v))

    def narrow(v, sel):
        hi, mid, _ = pieces(v)
        return dot(hi, sel, 1, 1) + dot(mid, sel, 1, 1)

    def chunk(k):
        return pl.ds(pl.multiple_of(k * NC, NC), NC)

    x_load.wait()
    g_load.wait()

    @pl.when(jnp.logical_not(first))
    def _():
        halo_copy.wait_recv()

    part[...] = jnp.zeros_like(part)
    h_load.wait()

    @pl.when(jnp.logical_not(needing))
    def _():
        w_load.wait()

    def product(i):
        part[...] += dot(hv[:, w_rows(i)], wh[w_rows(i)], 1, 0)

    def second(k, z):
        @pl.when(needing)
        def _():
            w_forward(k).wait_recv()

        product((1 - gi) * chunks + k)
        return z

    def prepare(k, z):
        @pl.when(needing)
        def _():
            w_send(k).wait_recv()
            w_forward(k).start()

        product(gi * chunks + k)

        @pl.when(k >= YLAG)
        def _():
            second(k - YLAG, 0)

        at = chunk(k)
        taps = tapx_ref[:, at]
        xe = jnp.concatenate([xhalo[:, at], xv[:, at]]).astype(F32)
        pre = taps[3:4, :] * xe[HI:]
        for d in range(1, 4):
            pre += taps[3 - d : 4 - d, :] * pltpu.roll(xe, d, 0)[HI:] * masks[3 - d]
        sig = jax.nn.sigmoid(pre)
        xc = pre * sig
        xf[:, at] = xc
        dsf[:, at] = sig * (1.0 + pre * (1.0 - sig))
        sel = spread(k)
        dt_w, a_w, b_w = widen(small[0], sel), widen(small[1], sel), widen(small[2], sel)
        dtw[:, at] = dt_w
        aw[:, at] = a_w
        bw[:, at] = b_w
        scaled = xc * dt_w * b_w
        b_x = scaled.astype(BF)
        bx[:, at] = b_x
        tx[:, at] = (scaled * a_w[T - 1 :, :]).astype(BF)
        a_g = (a_w * gv[:, at].astype(F32)).astype(BF)
        ag[:, at] = a_g
        ds_acc[...] += dot(a_g, b_x, 1, 1)
        thrc[at, :] = sum(dot(sel, p, 0, 0) for p in pieces(thr))
        return z

    lax.fori_loop(0, chunks, prepare, 0)

    @pl.when(jnp.logical_not(needing))
    def _():
        w_all(w_send, "wait_send")

    for d in (*range(1, n_ctx), 0):
        h_send(d, 1 - f).start()

    lax.fori_loop(chunks - YLAG, chunks, second, 0)

    p_swap = remote(part, partr, s_ps.at[0], s_pr, (gi, c, f, 1 - h))
    p_swap.start()
    p_tails = [
        remote(
            part.at[T - 8 :], tails.at[h], s_ps.at[1 + o], s_tr.at[h],
            (gi, lax.rem(c + 1, n_ctx), f, lax.rem(h + o, 2)),
        )
        for o in range(2)
    ]

    @pl.when(jnp.logical_not(last_c))
    def _():
        for p in p_tails:
            p.start()

    p_swap.wait_recv()

    @pl.when(jnp.logical_not(first))
    def _():
        for o in range(2):
            remote(part.at[T - 8 :], tails.at[o], s_ps.at[1], s_tr.at[o], (gi, c, f, 1 - h)).wait_recv()

    taps_b = tapb_ref[...]
    bc = (part[...] + partr[...]).astype(BF).astype(F32)
    tail = (tails[0] + tails[1]).astype(BF).astype(F32)
    be = jnp.concatenate([tail, bc])
    pre_bc = taps_b[3:4, :] * bc
    for d in range(1, 4):
        pre_bc += taps_b[3 - d : 4 - d, :] * pltpu.roll(be, d, 0)[8:] * masks[3 - d]
    sig_bc = jax.nn.sigmoid(pre_bc)
    conv_bc = pre_bc * sig_bc
    silu_bc[...] = sig_bc * (1.0 + pre_bc * (1.0 - sig_bc))
    b_own, c_own = conv_bc[:, :STATE], conv_bc[:, STATE:]
    lastb[...] = (last_ref[...] * b_own).astype(BF)
    alivec[...] = (alive_ref[...] * c_own).astype(BF)
    def piece(k):
        return pl.ds(pl.multiple_of(k * CH, CH), CH)

    def f_copy(k):
        return remote(sn.at[piece(k)], start.at[piece(k)], s_fs.at[k], s_fr.at[k], (gi, lax.rem(c + 1, n_ctx), f, h))

    def b_copy(k):
        return remote(
            sp.at[piece(k)], endg.at[piece(k)], s_bs.at[k], s_br.at[k], (gi, lax.rem(c + n_ctx - 1, n_ctx), f, h)
        )

    def forward(k):
        @pl.when(jnp.logical_not(first))
        def _():
            f_copy(k).wait_recv()

        at = piece(k)
        e = dot(tx[:, at], lastb[...], 0, 0)
        sn[at, :] = (e + thrc[at, :] * start[at, :].astype(F32)).astype(BF)

        @pl.when(jnp.logical_not(last_c))
        def _():
            f_copy(k).start()

    def backward(k):
        @pl.when(jnp.logical_not(last_c))
        def _():
            b_copy(k).wait_recv()

        at = piece(k)
        e = dot(ag[:, at], alivec[...], 0, 0)
        sp[at, :] = (e + thrc[at, :] * endg[at, :].astype(F32)).astype(BF)

        @pl.when(jnp.logical_not(first))
        def _():
            b_copy(k).start()

    row_n = lax.broadcasted_iota(jnp.int32, (T, NC), 0)
    row_8 = lax.broadcasted_iota(jnp.int32, (8, NC), 0)

    def transposed_conv(d_pre, taps):
        own = taps[3:4, :] * d_pre
        rim = jnp.zeros((8, NC), F32)
        for d in range(1, 4):
            z = pltpu.roll(taps[3 - d : 4 - d, :] * masks[3 - d] * d_pre, T - d, 0)
            own += jnp.where(row_n < T - d, z, 0.0)
            rim += jnp.where(row_8 < 8 - d, 0.0, z[T - 8 :])
        return own, rim

    def collect(k):
        at = chunk(k)
        db_acc[...] += dot(tx[:, at], endg[at, :], 1, 0)
        dc_acc[...] += dot(ag[:, at], start[at, :], 1, 0)

    def finish(k):
        at = chunk(k)
        taps = tapx_ref[:, at]
        sel = spread(k)
        sm = sm_ref[...]
        a_w, b_w = aw[:, at], bw[:, at]
        gf = gv[:, at].astype(F32)
        b_x, a_g = bx[:, at], ag[:, at]
        st, en = start[at, :], endg[at, :]
        y = dot(sm, b_x, 1, 0) + dot(alivec[...], st, 1, 1)
        r_acc[...] += narrow(a_w * gf * y, sel)
        d_xt = b_w * (dot(sm, a_g, 0, 0) + a_w[T - 1 :, :] * dot(lastb[...], en, 1, 1))
        q_acc[...] += narrow(xf[:, at] * d_xt, sel)
        prod = en.astype(F32) * sn[at, :].astype(F32)
        hi, mid, _ = pieces(prod)
        ones8 = jnp.ones((8, 128), BF)
        l_acc[...] += narrow(dot(ones8, hi, 1, 1) + dot(ones8, mid, 1, 1), sel)
        skip_w = widen(jnp.broadcast_to(skip_ref[...], (8, heads)), sel)[:1]
        d_pre = (dtw[:, at] * d_xt + skip_w * gf) * dsf[:, at]
        own, rim = transposed_conv(d_pre, taps)
        gxs[:, at] = own.astype(BF)
        gxtail[:, at] = own[T - HI :]
        rimx_s[:, at] = rim

    inner = jnp.logical_and(c > 0, c < n_ctx - 1)
    pieces_n = W // CH
    group = NC // CH
    offset = jnp.where(inner, LAG, pieces_n)
    early = c < n_ctx // 2

    def lead(k, z):
        @pl.when(early)
        def _():
            forward(k)

        @pl.when(jnp.logical_not(early))
        def _():
            backward(k)

        return z

    def scores():
        same_f = same_ref[...] > 0.5
        sm_ref[...] = jnp.where(same_f, dot(c_own, b_own, 1, 1, EXACT), 0.0).astype(BF)
        d_sm = jnp.where(same_f, ds_acc[...], 0.0)
        dps[:, :STATE] = dot(d_sm, c_own, 0, 0, EXACT)
        dps[:, STATE:] = dot(d_sm, b_own, 1, 0, EXACT)

    def step(k, z):
        @pl.when(k + offset < pieces_n)
        def _():
            lead(k + offset, 0)

        @pl.when(early)
        def _():
            backward(k)

        @pl.when(jnp.logical_not(early))
        def _():
            forward(k)

        @pl.when(lax.rem(k, group) == group - 1)
        def _():
            collect(k // group)

            @pl.when(k >= group)
            def _():
                finish(k // group - 1)

        return z

    lax.fori_loop(0, jnp.where(inner, 0, offset), lead, 0)
    scores()
    lax.fori_loop(0, jnp.where(inner, offset, 0), lead, 0)
    lax.fori_loop(0, pieces_n, step, 0)

    rimx = remote(rimx_s, rimx_r, s_rim.at[0], s_rim.at[1], (gi, lax.rem(c + n_ctx - 1, n_ctx), f, h))

    alive, last = alive_ref[...], last_ref[...]
    d_bcc = jnp.concatenate([last * db_acc[...], alive * dc_acc[...]], axis=1)
    dps[...] = (dps[...] + d_bcc) * silu_bc[...]
    d_swap = remote(dps, dpsr, s_ds.at[0], s_dr, (gi, c, f, 1 - h))
    d_swap.start()
    d_rims = [
        remote(
            dps.at[:8], rims.at[h], s_ds.at[1 + o], s_rr.at[h],
            (gi, lax.rem(c + n_ctx - 1, n_ctx), f, lax.rem(h + o, 2)),
        )
        for o in range(2)
    ]

    @pl.when(jnp.logical_not(first))
    def _():
        for p in d_rims:
            p.start()

    finish(chunks - 1)

    d_swap.wait_recv()

    @pl.when(jnp.logical_not(last_c))
    def _():
        for o in range(2):
            remote(dps.at[:8], rims.at[o], s_ds.at[1], s_rr.at[o], (gi, c, f, 1 - h)).wait_recv()

    own, _ = transposed_conv(dps[...] + dpsr[...], taps_b)
    rim_in = rims[0] + rims[1]
    row8 = lax.broadcasted_iota(jnp.int32, (8, 2 * STATE), 0)
    npos = pos0 + T + row8
    nseg = segment(npos)
    rim = jnp.zeros((8, 2 * STATE), F32)
    for d in range(1, 4):
        mask = (segment(npos - d) == nseg).astype(F32)
        z = pltpu.roll(taps_b[3 - d : 4 - d, :] * mask * rim_in, 8 - d, 0)
        rim += jnp.where(row8 < 8 - d, 0.0, z)
    d_bc = jnp.concatenate([own[: T - 8], own[T - 8 :] + rim]).astype(BF)
    dall[me] = d_bc

    half = pl.ds(pl.multiple_of(h * (T // 2), T // 2), T // 2)
    other = pl.ds(pl.multiple_of((1 - h) * (T // 2), T // 2), T // 2)

    def z_copy(d):
        return remote(
            dall.at[me, half], dall.at[me, half], s_zs.at[d], s_zr.at[me], (gi, lax.rem(c + d, n_ctx), f, h)
        )

    def x_copy(cc):
        b = cc * 2 + f
        return remote(dall.at[b, half], dall.at[b, half], s_xs.at[cc], s_xr.at[cc], (gi, c, 1 - f, h))

    def c_copy(b):
        return remote(dall.at[b, half], dall.at[b, half], s_cs.at[b], s_cr.at[b], (gi, c, f, 1 - h))

    def from_z(cc):
        b = cc * 2 + f
        return remote(dall.at[b, half], dall.at[b, half], s_zs.at[0], s_zr.at[b], (gi, c, f, 1 - h))

    def from_x(cc):
        b = cc * 2 + 1 - f
        return remote(dall.at[b, half], dall.at[b, half], s_xs.at[0], s_xr.at[cc], (gi, c, f, 1 - h))

    def from_c(b):
        return remote(dall.at[b, other], dall.at[b, other], s_cs.at[0], s_cr.at[b], (gi, c, f, 1 - h))

    left = c < n_ctx // 2
    nearest = [c + 1 - 2 * lax.rem(c, 2), jnp.where(left, 2, 1), jnp.where(left, 3, 0)]
    x_copy(c).start()
    for cc in nearest[::-1]:
        z_copy(lax.rem(cc - c + n_ctx, n_ctx)).start()

    @pl.when(jnp.logical_not(first))
    def _():
        rimx.start()

    def grad_u(k, z):
        at = w_rows(k)
        gus[:, at] = dot(dall[me], wh[at], 1, 1).astype(BF)
        return z

    parts = 2 * chunks
    marks = [parts // 2, parts * 11 // 16, parts * 7 // 8, parts]
    lax.fori_loop(0, marks[0], grad_u, 0)
    from_x(c).wait_recv()
    c_copy(c * 2 + 1 - f).start()
    for i, cc in enumerate(nearest):
        from_z(cc).wait_recv()
        x_copy(cc).start()
        c_copy(cc * 2 + f).start()
        lax.fori_loop(marks[i], marks[i + 1], grad_u, 0)
    u_out = pltpu.make_async_copy(gus, gu_out, s_out.at[0])
    u_out.start()

    total_q = q_acc[...]
    dts = small[0]
    at_end = row[:, :heads] == T - 1
    d_cum = r_acc[...] - dts * total_q + jnp.where(at_end, l_acc[:1, :], 0.0)
    d_log = dot(tri, d_cum, 0, 0, EXACT)
    ddt_ref[...] = ((total_q - decay_ref[...] * d_log) * jax.nn.sigmoid(small[3])).T
    t_out = pltpu.make_async_copy(ddt_ref, ddt_out, s_out.at[3])
    t_out.start()

    for cc in nearest:
        from_x(cc).wait_recv()
        c_copy(cc * 2 + 1 - f).start()

    @pl.when(jnp.logical_not(last_c))
    def _():
        rimx.wait_recv()

    fixed = gxtail[HI - 8 :, :] + rimx_r[...]
    gxs[T - HI :, :] = jnp.concatenate([gxtail[: HI - 8, :], fixed]).astype(BF)
    x_out = pltpu.make_async_copy(gxs, gx_out, s_out.at[1])
    x_out.start()

    def h_wait(b):
        remote(hall.at[b], hall.at[b], s_hs.at[0], s_hr.at[b], (gi, c, f, 1 - h)).wait_recv()

    own_load.wait()
    for d in range(1, n_ctx):
        b = lax.rem(c + d, n_ctx) * 2 + f
        from_c(b).wait_recv()
        h_wait(b)
    for d in range(n_ctx):
        b = lax.rem(c + d, n_ctx) * 2 + 1 - f
        from_c(b).wait_recv()
        h_wait(b)
    gws[...] = dot(
        hall[...].reshape(2 * n_ctx * T, wb), dall[...].reshape(2 * n_ctx * T, 2 * STATE), 0, 0
    )
    w_out = pltpu.make_async_copy(gws, gw_out, s_out.at[2])
    w_out.start()

    @pl.when(needing)
    def _():
        w_all(w_forward, "wait_send")

    @pl.when(jnp.logical_not(last_c))
    def _():
        halo_copy.wait_send()
        for p in p_tails:
            p.wait_send()
        lax.fori_loop(0, W // CH, lambda k, z: (f_copy(k).wait_send(), z)[1], 0)

    @pl.when(jnp.logical_not(first))
    def _():
        for p in d_rims:
            p.wait_send()
        rimx.wait_send()
        lax.fori_loop(0, W // CH, lambda k, z: (b_copy(k).wait_send(), z)[1], 0)

    p_swap.wait_send()
    d_swap.wait_send()
    for d in range(n_ctx):
        h_send(d, 1 - f).wait_send()
        x_copy(lax.rem(c + d, n_ctx)).wait_send()
        c_copy(lax.rem(c + d, n_ctx) * 2 + 1 - f).wait_send()
        if d:
            h_send(d, f).wait_send()
            z_copy(d).wait_send()
            c_copy(lax.rem(c + d, n_ctx) * 2 + f).wait_send()
    u_out.wait()
    x_out.wait()
    w_out.wait()
    t_out.wait()


def fused(hidden, w, x, g, raw, decay, skip, tapx, tapb, spans):
    T, W = x.shape
    DH = hidden.shape[1]
    n_ctx = lax.axis_size("ctx")
    blocks = 2 * n_ctx
    wb = DH // blocks
    heads = raw.shape[0]
    K = W // CH
    U = W // NC
    vm, dma = pltpu.VMEM, pltpu.SemaphoreType.DMA
    spec = pl.BlockSpec
    hbm = spec(memory_space=pltpu.HBM)
    out = spec(memory_space=pl.ANY)
    S2 = 2 * STATE
    return pl.pallas_call(
        fused_kernel,
        out_shape=(
            jax.ShapeDtypeStruct((T, W), BF),
            jax.ShapeDtypeStruct((T, DH), BF),
            jax.ShapeDtypeStruct((heads, T), F32),
            jax.ShapeDtypeStruct((wb, S2), F32),
        ),
        in_specs=[hbm] * 10,
        out_specs=(out,) * 4,
        scratch_shapes=[
            vm((heads, T), F32), vm((1, heads), F32), vm((1, heads), F32), vm((4, W), F32), vm((4, S2), F32),
            pltpu.SMEM(spans.shape, jnp.int32), vm((heads, T), F32),
            vm((T, W), BF), vm((T, W), BF), vm((T, DH), BF), vm((DH, S2), BF), vm((HI, W), BF),
            vm((T, W), F32), vm((T, W), F32), vm((T, W), F32), vm((T, W), F32), vm((T, W), F32),
            vm((T, W), BF), vm((T, W), BF), vm((T, W), BF), vm((W, STATE), F32),
            vm((W, STATE), BF), vm((W, STATE), BF), vm((W, STATE), BF), vm((W, STATE), BF),
            vm((3, T, S2), F32), vm((T, STATE), F32), vm((T, STATE), F32), vm((T, STATE), F32),
            vm((4, T, heads), F32), vm((T, T), F32), vm((T, S2), F32), vm((T, S2), F32), vm((2, 8, S2), F32),
            vm((T, S2), F32), vm((T, T), BF), vm((T, STATE), BF), vm((T, STATE), BF),
            vm((T, STATE), F32), vm((T, STATE), F32), vm((T, S2), F32), vm((T, S2), F32), vm((2, 8, S2), F32),
            vm((8, W), F32), vm((8, W), F32), vm((HI, W), F32),
            vm((T, heads), F32), vm((T, heads), F32), vm((8, heads), F32),
            vm((blocks, T, wb), BF), vm((blocks, T, S2), BF),
            vm((T, W), BF), vm((T, DH), BF), vm((wb, S2), F32),
            dma((5,)), dma((U,)), dma((U,)), dma((U,)), dma((U,)), dma((blocks,)), dma((blocks,)), dma((2,)),
            dma((K,)), dma((K,)), dma((K,)), dma((K,)),
            dma((3,)), dma, dma((2,)), dma((3,)), dma, dma((2,)), dma((2,)),
            dma((n_ctx,)), dma((blocks,)), dma((n_ctx,)), dma((n_ctx,)), dma((blocks,)), dma((blocks,)), dma((6,)), dma((4,)),
        ],
        compiler_params=pltpu.CompilerParams(
            collective_id=0, has_side_effects=True, vmem_limit_bytes=60 << 20
        ),
        cost_estimate=pl.CostEstimate(
            flops=2 * T * 256 * (W * 9 + DH * 4), bytes_accessed=8 << 20, transcendentals=4 * T * W
        ),
    )(hidden, w, x, g, raw, decay, skip, tapx, tapb, spans)


def publish_kernel(*refs):
    n = (len(refs) - 2) // 3
    ins, outs, held, in_sem, out_sem = refs[:n], refs[n : 2 * n], refs[2 * n : 3 * n], refs[-2], refs[-1]
    loads, stores = [], []
    for i in range(n):
        rows = ins[i].shape[0] // PUB
        for j in range(PUB):
            at = pl.ds(j * rows, rows)
            loads.append(pltpu.make_async_copy(ins[i].at[at], held[i].at[at], in_sem.at[i, j]))
            stores.append(pltpu.make_async_copy(held[i].at[at], outs[i].at[at], out_sem.at[i, j]))
    for copy in loads:
        copy.start()
    for load, store in zip(loads, stores):
        load.wait()
        store.start()
    for copy in stores:
        copy.wait()


def publish(arrays):
    n = len(arrays)
    hbm = pl.BlockSpec(memory_space=pl.ANY)
    return pl.pallas_call(
        publish_kernel,
        out_shape=tuple(jax.ShapeDtypeStruct(a.shape, a.dtype) for a in arrays),
        in_specs=[hbm] * n,
        out_specs=(hbm,) * n,
        scratch_shapes=[pltpu.VMEM(a.shape, a.dtype) for a in arrays]
        + [pltpu.SemaphoreType.DMA((n, PUB)), pltpu.SemaphoreType.DMA((n, PUB))],
        compiler_params=pltpu.CompilerParams(vmem_limit_bytes=60 << 20),
    )(*arrays)


def on_device(
    hidden_in, w_bc, x_in, dt_raw, decay_rate, conv_x, conv_bc, skip_gain, span_len, grad_y
):
    T = x_in.shape[1]
    hidden = hidden_in[0]
    half_width = hidden.shape[1]
    n_ctx, n_fsdp, n_head = (lax.axis_size(a) for a in ("ctx", "fsdp", "head"))
    assert T * 2 == MOST and dt_raw.shape[2] == 32
    x0, g0, raw0 = x_in[0], grad_y[0], dt_raw[0]
    if (lax.axis_size("groups"), n_ctx, n_fsdp, n_head) == (2, 4, 2, 2):
        outs = fused(
            hidden, w_bc, x0, g0, raw0.T, decay_rate[None, :], skip_gain[None, :], conv_x, conv_bc, span_len
        )
        outs = publish(outs)
        return (outs[0][None], outs[1][None], outs[2].T[None], outs[3][None])
    if n_fsdp == n_head:
        route = [(f * n_head + h, h * n_head + f) for f in range(n_fsdp) for h in range(n_head)]
        w_half = lax.ppermute(w_bc, ("fsdp", "head"), route)
    else:
        w_full = lax.all_gather(w_bc, "fsdp", axis=0, tiled=True)
        w_half = lax.dynamic_slice_in_dim(
            w_full, lax.axis_index("head") * half_width, half_width, 0
        )
    raws = [shifted(raw0, "ctx", d) for d in (2, 1)] + [raw0] + [shifted(raw0, "ctx", -d) for d in (1, 2)]
    x1, g1 = shifted(x0, "ctx", 1), shifted(g0, "ctx", -1)
    x2, g2 = shifted(x0, "ctx", 2), shifted(g0, "ctx", -2)

    swap = [(i, (i + 1) % n_head) for i in range(n_head)]
    partial_bc = jnp.dot(hidden, w_half, preferred_element_type=F32)
    bc_pre = (partial_bc + lax.ppermute(partial_bc, "head", swap)).astype(BF)
    bcs = [shifted(bc_pre, "ctx", d) for d in (2, 1)] + [bc_pre] + [shifted(bc_pre, "ctx", -d) for d in (1, 2)]

    n_blocks = n_ctx * n_fsdp
    blocks = hidden.reshape(T, n_blocks, half_width // n_blocks).transpose(1, 0, 2)
    hidden_all = lax.all_to_all(blocks, ("ctx", "fsdp"), 0, 0, tiled=True)

    position = (lax.axis_index("ctx") - 2) * T + jnp.arange(-3, 5 * T, dtype=jnp.int32)
    spans = span_len.shape[1]
    earlier = jnp.arange(spans)[:, None] <= jnp.arange(spans)[None, :]
    span_ends = jnp.sum(jnp.where(earlier, span_len[0][:, None], 0), axis=0)
    counted = jnp.sum((span_ends[None, :] <= position[:, None]).astype(jnp.int32), axis=1)
    segment = jnp.where(position >= 0, counted, -1).astype(F32)
    own_seg = segment[3:]
    by_block = own_seg.reshape(5, T)
    before = jnp.broadcast_to(segment[2 : 2 + 5 * T : T][:, None], (5, T)).reshape(-1)
    last = jnp.broadcast_to(by_block[:, T - 1 :], (5, T)).reshape(-1)
    info = jnp.stack(
        [(segment[k : k + 5 * T] == own_seg).astype(F32) for k in range(3)]
        + [(own_seg == before).astype(F32), (own_seg == last).astype(F32), own_seg],
        axis=1,
    )
    segrow = by_block[2:3]
    raw = jnp.tile(jnp.concatenate(raws), (1, 4))
    decay = jnp.tile(decay_rate, 4)[None, :]
    skip = jnp.repeat(skip_gain, HEAD)[None, :]

    dx, tail, rim, dbc, rimbc, ddt = ssm(
        (x2, x1, x0), (g0, g1, g2), bcs, raw, info, segrow, decay, skip, conv_x, conv_bc
    )
    back = shifted(rim, "ctx", -1)
    grad_x = lax.dynamic_update_slice(dx, (tail + back).astype(BF), (T - 8, 0))

    other = lax.ppermute(dbc, "head", swap)
    rim_same = shifted(rimbc, "ctx", -1)
    cross = [
        (c * n_head + h, (c - 1) * n_head + (h + 1) % n_head)
        for c in range(1, n_ctx)
        for h in range(n_head)
    ]
    rim_cross = lax.ppermute(rimbc, ("ctx", "head"), cross)
    d_bc = ((dbc + other) + jnp.pad(rim_same + rim_cross, ((T - 8, 0), (0, 0)))).astype(BF)
    grad_u = lax.dot_general(
        d_bc, w_half, (((1,), (1,)), ((), ())), preferred_element_type=F32
    ).astype(BF)
    d_all = lax.all_gather(d_bc, ("ctx", "fsdp"), axis=0)
    grad_w = lax.dot_general(
        hidden_all.reshape(n_blocks * T, -1),
        d_all.reshape(n_blocks * T, -1),
        (((0,), (0,)), ((), ())),
        preferred_element_type=F32,
    )
    return (grad_x[None], grad_u[None], ddt[None], grad_w[None])


def solution(mesh):
    return jax.shard_map(
        on_device,
        mesh=mesh,
        in_specs=(
            P(("groups", "fsdp"), "ctx", "head"),
            P("fsdp", None),
            P(("groups", "fsdp"), "ctx", "head"),
            P(("groups", "fsdp"), "ctx", "head"),
            P("head"),
            P(None, "head"),
            P(),
            P("head"),
            P(("groups", "fsdp"), None),
            P(("groups", "fsdp"), "ctx", "head"),
        ),
        out_specs=(
            P(("groups", "fsdp"), "ctx", "head"),
            P(("groups", "fsdp"), "ctx", "head"),
            P(("groups", "fsdp"), "ctx", "head"),
            P(("groups", "head"), ("ctx", "fsdp"), None),
        ),
        check_vma=False,
    )
```
